32 devices in a mesh: dp: 16 (over z, x, core), tp: 2 (over y).
Axes of the slice: x: 2, y: 2, z: 4, core: 2. Of those that a mesh axis runs over, the one named last changes fastest.
Arguments:
- hidden_in: bfloat16 [2, 16, 1024, 768], P(None, 'dp', 'tp'), may hold values from -6 to 6
- segment_ids: int32 [2, 16, 1024], P(None, 'dp'), may hold values from 0 to 15, never falling along the last dimension, each value on 1 to 128 neighbouring positions
- bucket_of: int32 [2047], replicated, may hold values from 0 to 31
- attn_gain: bfloat16 [768], P('dp'), may hold values from 0.5 to 1.5
- w_query: bfloat16 [768, 768], P('dp', 'tp'), may hold values from -0.02734375 to 0.02734375
- w_key: bfloat16 [768, 768], P('dp', 'tp'), may hold values from -0.21875 to 0.21875
- w_value: bfloat16 [768, 768], P('dp', 'tp'), may hold values from -0.21875 to 0.21875
- w_attn_out: bfloat16 [768, 768], P('tp', 'dp'), may hold values from -0.875 to 0.875
- bias_table: float32 [32, 12], P(None, 'tp'), may hold values from -4 to 4
- ffn_gain: bfloat16 [768], P('dp'), may hold values from 0.5 to 1.5
- w_gate: bfloat16 [768, 2048], P('dp', 'tp'), may hold values from -0.21875 to 0.21875
- w_up: bfloat16 [768, 2048], P('dp', 'tp'), may hold values from -0.21875 to 0.21875
- w_down: bfloat16 [2048, 768], P('tp', 'dp'), may hold values from -0.125 to 0.125
- cotangent: bfloat16 [2, 16, 1024, 768], P(None, 'dp', 'tp'), may hold values from -6 to 6
Outputs:
- block_out: float32 [2, 16, 1024, 768], P(None, 'dp', 'tp')
- grad_in: float32 [2, 16, 1024, 768], P(None, 'dp', 'tp')
- grad_attn_gain: float32 [768], P('dp')
- grad_query: float32 [768, 768], P('dp', 'tp')
- grad_key: float32 [768, 768], P('dp', 'tp')
- grad_value: float32 [768, 768], P('dp', 'tp')
- grad_attn_out: float32 [768, 768], P('tp', 'dp')
- grad_bias: float32 [32, 12], P(None, 'tp')
- grad_ffn_gain: float32 [768], P('dp')
- grad_gate: float32 [768, 2048], P('dp', 'tp')
- grad_up: float32 [768, 2048], P('dp', 'tp')
- grad_down: float32 [2048, 768], P('tp', 'dp')
The draws below stay inside these ranges and needn't reach their ends.
Inputs may be any that keep to these rules, and one draw needn't show every extreme that they name: `segment_ids`: within each row of 1024 positions the numbers never fall; each of the 16 documents spans 1 to 128 positions and one spans exactly 128.
All inputs are finite; a program needn't handle non-finite values.
Results may differ from the reference program's by a relative error of at most 0.019.
Values may be sent and summed in bfloat16 or wider, within the bound.
No kernel may reach another device: no remote copies, remote signals or barrier semaphores. Data moves between devices by JAX's collectives and lax.ppermute only.
A program may use at most 832 MiB of HBM per device.

```python
import math
import jax
import jax.numpy as jnp
import numpy as np
from jax import lax

D = 768
HEADS = 12
HD = 64
FF = 2048
NB = 32
SEQ = 1024
DOCS = 16
MOST = 128
MICRO = 2
ROWS = 16


def with_ends(entries, key, smallest, high):
    longest = entries.shape.index(max(entries.shape))
    spots = []
    for shift in (0, 1):
        where = [jax.random.randint(jax.random.fold_in(key, axis), (), 0, length) for axis, length in enumerate(entries.shape)]
        where[longest] = (where[longest] + shift) % entries.shape[longest]
        spots.append(tuple(where))
    return entries.at[spots[0]].set(smallest).at[spots[1]].set(high)


def with_spikes(drawn, key, source, target, shards_of, factor):
    def block_of(axis_at):
        return (jnp.arange(drawn.shape[axis_at]) // (drawn.shape[axis_at] // shards_of)).reshape((-1,) + (1,) * (drawn.ndim - 1 - axis_at))

    near = jax.random.permutation(key, shards_of)[block_of(target)]
    far = (block_of(target) + shards_of // 2) % shards_of
    return jnp.where((block_of(source) == near) | (block_of(source) == far), factor * drawn, drawn)


def block_levels(own_key, shape, shards, least, largest):
    factor_of, own = 1.0, jax.random.fold_in(own_key, 6)
    for dim, parts in shards:
        heights = jnp.exp(jax.random.uniform(jax.random.fold_in(own, dim), (parts,), jnp.float32, least / len(shards), largest / len(shards)))
        factor_of = factor_of * jnp.repeat(heights, shape[dim] // parts).reshape([-1 if axis == dim else 1 for axis in range(len(shape))])
    return factor_of


def profile(count, total, limit, skew):
    weights = [(1 << 20) // math.isqrt(grade ** skew) + 1 for grade in range(2, count + 1)]
    surplus, counts = total - limit - (count - 1), [1] * (count - 1)
    while surplus > 0:
        movable = [i for i in range(count - 1) if counts[i] < limit]
        mass, budget = sum([weights[i] for i in movable]), surplus
        for i in movable:
            more = min(limit - counts[i], max(1, budget * weights[i] // mass), surplus)
            counts[i] = counts[i] + more
            surplus = surplus - more
    return np.array([limit] + counts)


def ragged_sizes(key, count, total, reach, slope):
    if count == 2:
        one = jax.random.randint(key, (), max(1, total - reach), min(reach, total - 1) + 1)
        return jnp.stack([one, total - one])
    sizes = jnp.asarray(profile(count, total, reach, slope), jnp.int32)
    couples = (count - 1) // 2
    source_of, sink = sizes[1:1 + 2 * couples:2], sizes[2:2 + 2 * couples:2]
    room = jnp.minimum(source_of - 1, reach - sink)
    passed = jax.random.randint(jax.random.fold_in(key, 1), (couples,), 0, 1 << 20) % (room + 1)
    sizes = sizes.at[1:1 + 2 * couples:2].set(source_of - passed).at[2:2 + 2 * couples:2].set(sink + passed)
    return sizes[jax.random.permutation(jax.random.fold_in(key, 2), count)]


def bell_draw(stream_key, dims, scale, most, cuts=(), kind=jnp.bfloat16):
    level = block_levels(stream_key, dims, cuts, -0.22, 0.18) if cuts else 1.0
    drawn = jax.random.normal(stream_key, dims, jnp.float32) * scale * level
    return jnp.minimum(jnp.maximum(drawn, -most), most).astype(kind)


def gaussian_with(own_key, dims, scale, bound, pieces, heavy, kind=jnp.bfloat16):
    array = scale * jax.random.normal(own_key, dims, jnp.float32)
    if pieces:
        array = array * block_levels(own_key, dims, pieces, -0.22, 0.18)
    return jnp.clip(with_spikes(array, jax.random.fold_in(own_key, 3), *heavy), -bound, bound).astype(kind)


def setup_inputs(seed: int = 0) -> dict:
    seeds = jax.random.split(jax.random.key(seed), 15)
    return {
        "hidden_in": gaussian_with(seeds[0], (MICRO, ROWS, SEQ, D), 1.0, 6.0, ((1, 16), (2, 2)), (1, 3, 16, 2.0)),
        "segment_ids": jax.vmap(lambda own: jnp.searchsorted(jnp.cumsum(ragged_sizes(own, DOCS, SEQ, MOST, 1)), jnp.arange(SEQ), side="right"))(jax.random.split(seeds[1], MICRO * ROWS)).reshape((MICRO, ROWS, SEQ)).astype(jnp.int32),
        "bucket_of": with_ends(jax.random.randint(seeds[2], (2 * SEQ - 1,), 0, NB), jax.random.fold_in(seeds[2], 1), 0, NB - 1).astype(jnp.int32),
        "attn_gain": jnp.clip(1.0 + 0.1 * jax.random.normal(seeds[3], (D,), jnp.float32), 0.5, 1.5).astype(jnp.bfloat16),
        "w_query": bell_draw(seeds[4], (D, HEADS * HD), (D * HD) ** -0.5, 0.02734375, ((0, 16), (1, 2))),
        "w_key": bell_draw(seeds[5], (D, HEADS * HD), D ** -0.5, 0.21875, ((0, 16), (1, 2))),
        "w_value": bell_draw(seeds[6], (D, HEADS * HD), D ** -0.5, 0.21875, ((0, 16), (1, 2))),
        "w_attn_out": bell_draw(seeds[7], (HEADS * HD, D), (HEADS * HD // 16) ** -0.5, 0.875, ((0, 2), (1, 16))),
        "bias_table": bell_draw(seeds[8], (NB, HEADS), 1.0, 4.0, ((1, 2),), jnp.float32),
        "ffn_gain": jnp.clip(1.0 + 0.1 * jax.random.normal(seeds[9], (D,), jnp.float32), 0.5, 1.5).astype(jnp.bfloat16),
        "w_gate": bell_draw(seeds[10], (D, FF), D ** -0.5, 0.21875, ((0, 16), (1, 2))),
        "w_up": bell_draw(seeds[11], (D, FF), D ** -0.5, 0.21875, ((0, 16), (1, 2))),
        "w_down": bell_draw(seeds[12], (FF, D), FF ** -0.5, 0.125, ((0, 2), (1, 16))),
        "cotangent": gaussian_with(seeds[13], (MICRO, ROWS, SEQ, D), 1.0, 6.0, ((1, 16), (2, 2)), (1, 3, 16, 2.0)),
    }


EPSILON = 1e-06
HIGHEST_PREC = lax.Precision.HIGHEST

@jax.custom_vjp
def low(v):
    return lax.optimization_barrier(v.astype(jnp.bfloat16)).astype(jnp.float32)

@jax.custom_vjp
def low_back(v):
    return v

def low_keep(v):
    return (low(v), None)

def low_pass(kept, grad):
    return (grad,)

def back_keep(v):
    return (v, None)

def back_low(kept, grad):
    return (low(grad),)
low.defvjp(low_keep, low_pass)
low_back.defvjp(back_keep, back_low)

def rms_norm(values, gain_vec):
    inv_rms = lax.rsqrt(lax.optimization_barrier(jnp.mean(values * values, axis=-1, keepdims=True)) + EPSILON)
    return values * inv_rms * gain_vec

def product(left, right):
    return jnp.dot(left, right, precision=HIGHEST_PREC, preferred_element_type=jnp.float32)

def position_bias(bias_table, bucket_of):
    positions = jnp.arange(SEQ, dtype=jnp.int32)
    offsets = positions[None, :] - positions[:, None] + (SEQ - 1)
    buckets = jnp.take(bucket_of, offsets)
    return jnp.transpose(jnp.take(bias_table, buckets, axis=0), (2, 0, 1))

def layer_row(params, row_input, seg_row, bucket_of):
    attn_gain, w_query, w_key, w_value, w_attn_out, bias_table, ffn_gain, w_gate, w_up, w_down = params
    head_shape = (SEQ, HEADS, HD)
    normed1 = low(rms_norm(row_input, attn_gain))
    queries = low_back(low(product(normed1, w_query))).reshape(head_shape)
    key_rows = low_back(low(product(normed1, w_key))).reshape(head_shape)
    value_rows = low_back(low(product(normed1, w_value))).reshape(head_shape)
    logits = jnp.einsum('ihe,jhe->hij', queries, key_rows, precision=HIGHEST_PREC)
    logits = logits + position_bias(bias_table, bucket_of)
    same_doc = seg_row[:, None] == seg_row[None, :]
    logits = low_back(jnp.where(same_doc[None], logits, -1000000000.0))
    weights = low(jax.nn.softmax(logits, axis=-1))
    heads_out = jnp.einsum('hij,jhe->ihe', weights, value_rows, precision=HIGHEST_PREC)
    heads_out = low_back(low(heads_out)).reshape(SEQ, HEADS * HD)
    middle = row_input + low_back(product(heads_out, w_attn_out))
    normed2 = low(rms_norm(middle, ffn_gain))
    gate_pre = low_back(product(normed2, w_gate))
    up_pre = low_back(product(normed2, w_up))
    hidden = low(jax.nn.gelu(gate_pre, approximate=True) * up_pre)
    return middle + low_back(product(hidden, w_down))

def reference(hidden_in, segment_ids, bucket_of, attn_gain, w_query, w_key, w_value, w_attn_out, bias_table, ffn_gain, w_gate, w_up, w_down, cotangent):
    params = tuple((item.astype(jnp.float32) for item in (attn_gain, w_query, w_key, w_value, w_attn_out, bias_table, ffn_gain, w_gate, w_up, w_down)))
    row_data = hidden_in.astype(jnp.float32).reshape(MICRO * ROWS, SEQ, D)
    segments = segment_ids.reshape(MICRO * ROWS, SEQ)
    row_step = jax.checkpoint(layer_row)

    def forward(params, row_data):
        return lax.map(lambda row_pair: row_step(params, row_pair[0], row_pair[1], bucket_of), (row_data, segments))
    block_out, pull_back = jax.vjp(forward, params, row_data)
    grads, grad_rows = pull_back(cotangent.astype(jnp.float32).reshape(MICRO * ROWS, SEQ, D))
    full_shape = (MICRO, ROWS, SEQ, D)
    return (block_out.reshape(full_shape), grad_rows.reshape(full_shape), grads[0], grads[1], grads[2], grads[3], grads[4], grads[5], grads[6], grads[7], grads[8], grads[9])
```

```python
import functools

import jax
import jax.numpy as jnp
from jax import lax
from jax.experimental import pallas as pl
from jax.experimental.pallas import tpu as pltpu
from jax.sharding import PartitionSpec as P

EPSILON = 1e-06
MASKED = -1000000000.0
HIGHEST_PREC = lax.Precision.HIGHEST
BLOCK = 128
LANES = 128
BF = jnp.bfloat16
F32 = jnp.float32


def log2_of(count):
    return count.bit_length() - 1


def swap(value, axis, bit):
    count = lax.axis_size(axis)
    return lax.ppermute(value, axis, [(i, i ^ (1 << bit)) for i in range(count)])


def own_bit(axis, bit):
    return (lax.axis_index(axis) >> bit) & 1


def stage_order(across_first):
    bits = log2_of(lax.axis_size("dp"))
    high = [("dp", b) for b in range(bits - 1, 1, -1)]
    low = [("dp", 1)] if bits > 1 else []
    middle = [("tp", 0)] + low if across_first else low + [("tp", 0)]
    return high + middle + ([("dp", 0)] if bits > 0 else [])


def gather_rows(piece, order):
    buf, have = piece, []
    for axis, bit in order:
        other = swap(buf, axis, bit)
        first = own_bit(axis, bit) == 0
        low, high = jnp.where(first, buf, other), jnp.where(first, other, buf)
        if axis == "tp":
            buf = jnp.concatenate([low, high], axis=-1)
        else:
            where = sum(1 for b in have if b > bit)
            have.append(bit)
            buf = jnp.stack([low, high], axis=where)
    return buf.reshape(-1, buf.shape[-1])


def scatter_rows(grad, order):
    dp_count = lax.axis_size("dp")
    bits = log2_of(dp_count)
    cur = grad.reshape((2,) * bits + (grad.shape[0] // dp_count, grad.shape[1]))
    have = list(range(bits - 1, -1, -1))
    for axis, bit in reversed(order):
        mine = own_bit(axis, bit)
        if axis == "tp":
            half = cur.shape[-1] // 2
            send = lax.dynamic_slice_in_dim(cur, (1 - mine) * half, half, cur.ndim - 1)
            keep = lax.dynamic_slice_in_dim(cur, mine * half, half, cur.ndim - 1)
        else:
            where = have.index(bit)
            have.pop(where)
            send = lax.dynamic_index_in_dim(cur, 1 - mine, where, keepdims=False)
            keep = lax.dynamic_index_in_dim(cur, mine, where, keepdims=False)
        cur = keep.astype(F32) + swap(send.astype(BF), axis, bit).astype(F32)
    return cur


def pair_columns(pair, local_pairs):
    half, local = divmod(pair, local_pairs)
    width = local_pairs * LANES
    base = half * 3 * width + local * LANES
    return base, base + width, base + 2 * width


def key_blocks(block, last):
    return jnp.maximum(block - 1, 0), block, jnp.minimum(block + 1, last)


def block_mask(segq_ref, segk_ref, block):
    seg_q = segq_ref[0, pl.ds(pl.multiple_of(block * BLOCK, BLOCK), BLOCK), :]
    parts = []
    for step in range(3):
        seg_k = segk_ref[0, pl.ds(block + step, 1), :]
        parts.append(jnp.where(seg_q == seg_k, 0.0, MASKED))
    return jnp.concatenate(parts, axis=1)


def rows_of(ref, block, column):
    return ref[0, pl.ds(pl.multiple_of(block * BLOCK, BLOCK), BLOCK), column : column + LANES]


def window_of(ref, blocks, column):
    return jnp.concatenate([rows_of(ref, b, column) for b in blocks], axis=0)


def split_heads(value):
    first = lax.broadcasted_iota(jnp.int32, value.shape, 1) < LANES // 2
    zero = jnp.zeros_like(value)
    return jnp.where(first, value, zero), jnp.where(first, zero, value)


def dot_nt(left, right):
    return lax.dot_general(left, right, (((1,), (1,)), ((), ())), preferred_element_type=F32)


def dot_nn(left, right):
    return lax.dot_general(left, right, (((1,), (0,)), ((), ())), preferred_element_type=F32)


def dot_tn(left, right):
    return lax.dot_general(left, right, (((0,), (0,)), ((), ())), preferred_element_type=F32)


def softmax_of(logits):
    top = jnp.max(logits, axis=1, keepdims=True)
    powers = jnp.exp(logits - top)
    return powers * (1.0 / jnp.sum(powers, axis=1, keepdims=True))


def attend_kernel(pairs, last, shift_ref, qkv_ref, segq_ref, segk_ref, bias_ref, out_ref):
    block = pl.program_id(1) + shift_ref[0]
    blocks = key_blocks(block, last)
    mask = block_mask(segq_ref, segk_ref, block)
    for pair in range(pairs):
        col_q, col_k, col_v = pair_columns(pair, pairs // 2)
        query = rows_of(qkv_ref, block, col_q)
        keys = split_heads(window_of(qkv_ref, blocks, col_k))
        values = split_heads(window_of(qkv_ref, blocks, col_v))
        mixed = None
        for side in range(2):
            logits = dot_nt(query, keys[side]) + (bias_ref[2 * pair + side] + mask)
            weights = softmax_of(logits).astype(BF)
            part = dot_nn(weights, values[side])
            mixed = part if mixed is None else mixed + part
        out_ref[0, :, pair * LANES : (pair + 1) * LANES] = mixed.astype(BF)


def attend_forward(shift, qkv, seg_q, seg_k, bias, own_blocks):
    rows, length, width = qkv.shape
    heads = bias.shape[0]
    pairs = heads // 2
    last = length // BLOCK - 1
    steps = rows * own_blocks
    cost = pl.CostEstimate(
        flops=steps * heads * 4 * BLOCK * 3 * BLOCK * LANES,
        transcendentals=steps * heads * 3 * BLOCK * BLOCK,
        bytes_accessed=qkv.size * 2 + bias.size * 4 + rows * own_blocks * BLOCK * pairs * LANES * 2,
    )
    return pl.pallas_call(
        functools.partial(attend_kernel, pairs, last),
        out_shape=jax.ShapeDtypeStruct((rows, own_blocks * BLOCK, pairs * LANES), BF),
        grid_spec=pltpu.PrefetchScalarGridSpec(
            num_scalar_prefetch=1,
            grid=(rows, own_blocks),
            in_specs=[
                pl.BlockSpec((1, length, width), lambda r, i, s: (r, 0, 0)),
                pl.BlockSpec((1, length, LANES), lambda r, i, s: (r, 0, 0)),
                pl.BlockSpec((1,) + seg_k.shape[1:], lambda r, i, s: (r, 0, 0)),
                pl.BlockSpec(bias.shape, lambda r, i, s: (0, 0, 0)),
            ],
            out_specs=pl.BlockSpec((1, BLOCK, pairs * LANES), lambda r, i, s: (r, i, 0)),
        ),
        compiler_params=pltpu.CompilerParams(
            dimension_semantics=("arbitrary", "arbitrary"), vmem_limit_bytes=40 << 20
        ),
        cost_estimate=cost,
        name="attend_forward",
    )(shift, qkv, seg_q, seg_k, bias)


def fold_diagonals(block_sum):
    width = 4 * BLOCK
    cur = jnp.concatenate([jnp.zeros((BLOCK, BLOCK), F32), block_sum], axis=1)
    count = BLOCK // 2
    while count >= 8:
        cur = cur[:count] + pltpu.roll(cur[count:], width - count, 1)
        count //= 2
    return cur


def attend_back_kernel(
    pairs,
    last,
    own_blocks,
    shift_ref,
    qkv_ref,
    grad_ref,
    segq_ref,
    segk_ref,
    bias_ref,
    out_ref,
    diag_ref,
    acc_ref,
    sum_ref,
):
    row, block = pl.program_id(0), pl.program_id(1)
    blocks = key_blocks(block, last)
    mask = block_mask(segq_ref, segk_ref, block)
    owned = jnp.logical_and(block >= shift_ref[0], block < shift_ref[0] + own_blocks)
    keep = jnp.where(owned, 1.0, 0.0)

    @pl.when(block == 0)
    def _():
        acc_ref[...] = jnp.zeros_like(acc_ref)

    @pl.when(jnp.logical_and(block == 0, row == 0))
    def _():
        sum_ref[...] = jnp.zeros_like(sum_ref)

    def add_window(column, value):
        for step in range(3):
            place = pl.ds(pl.multiple_of(blocks[step] * BLOCK, BLOCK), BLOCK)
            acc_ref[place, column : column + LANES] += value[step * BLOCK : (step + 1) * BLOCK]

    for pair in range(pairs):
        col_q, col_k, col_v = pair_columns(pair, pairs // 2)
        query = rows_of(qkv_ref, block, col_q)
        grad = rows_of(grad_ref, block, pair * LANES)
        keys = split_heads(window_of(qkv_ref, blocks, col_k))
        values = split_heads(window_of(qkv_ref, blocks, col_v))
        queries, grads = split_heads(query), split_heads(grad)
        grad_q = grad_k = grad_v = None
        for side in range(2):
            head = 2 * pair + side
            logits = dot_nt(query, keys[side]) + (bias_ref[head] + mask)
            probs = softmax_of(logits)
            grad_w = dot_nt(grad, values[side])
            inner = jnp.sum(probs * grad_w, axis=1, keepdims=True)
            grad_l = (probs * (grad_w - inner)).astype(BF)
            sum_ref[head] += grad_l.astype(F32) * keep
            part_q = dot_nn(grad_l, keys[side])
            part_k = dot_tn(grad_l, queries[side])
            part_v = dot_tn(probs.astype(BF), grads[side])
            grad_q = part_q if grad_q is None else grad_q + part_q
            grad_k = part_k if grad_k is None else grad_k + part_k
            grad_v = part_v if grad_v is None else grad_v + part_v
        place = pl.ds(pl.multiple_of(block * BLOCK, BLOCK), BLOCK)
        acc_ref[place, col_q : col_q + LANES] = grad_q
        add_window(col_k, grad_k)
        add_window(col_v, grad_v)

    @pl.when(block == last)
    def _():
        start = pl.multiple_of(shift_ref[0] * BLOCK, BLOCK)
        out_ref[0] = acc_ref[pl.ds(start, own_blocks * BLOCK), :].astype(BF)

    @pl.when(jnp.logical_and(block == last, row == pl.num_programs(0) - 1))
    def _():
        for head in range(2 * pairs):
            diag_ref[head] = fold_diagonals(sum_ref[head])


def attend_backward(shift, qkv, grad_heads, seg_q, seg_k, bias, own_blocks):
    rows, length, width = qkv.shape
    heads = bias.shape[0]
    pairs = heads // 2
    last = length // BLOCK - 1
    steps = rows * (last + 1)
    cost = pl.CostEstimate(
        flops=steps * heads * 10 * BLOCK * 3 * BLOCK * LANES,
        transcendentals=steps * heads * 3 * BLOCK * BLOCK,
        bytes_accessed=qkv.size * 4 + grad_heads.size * 2 + bias.size * 4,
    )
    return pl.pallas_call(
        functools.partial(attend_back_kernel, pairs, last, own_blocks),
        out_shape=(
            jax.ShapeDtypeStruct((rows, own_blocks * BLOCK, width), BF),
            jax.ShapeDtypeStruct((heads, 8, 4 * BLOCK), F32),
        ),
        grid_spec=pltpu.PrefetchScalarGridSpec(
            num_scalar_prefetch=1,
            grid=(rows, last + 1),
            in_specs=[
                pl.BlockSpec((1, length, width), lambda r, i, s: (r, 0, 0)),
                pl.BlockSpec((1,) + grad_heads.shape[1:], lambda r, i, s: (r, 0, 0)),
                pl.BlockSpec((1, length, LANES), lambda r, i, s: (r, 0, 0)),
                pl.BlockSpec((1,) + seg_k.shape[1:], lambda r, i, s: (r, 0, 0)),
                pl.BlockSpec(bias.shape, lambda r, i, s: (0, 0, 0)),
            ],
            out_specs=[
                pl.BlockSpec((1, own_blocks * BLOCK, width), lambda r, i, s: (r, 0, 0)),
                pl.BlockSpec((heads, 8, 4 * BLOCK), lambda r, i, s: (0, 0, 0)),
            ],
            scratch_shapes=[
                pltpu.VMEM((length, width), F32),
                pltpu.VMEM(bias.shape, F32),
            ],
        ),
        compiler_params=pltpu.CompilerParams(
            dimension_semantics=("arbitrary", "arbitrary"), vmem_limit_bytes=48 << 20
        ),
        cost_estimate=cost,
        name="attend_backward",
    )(shift, qkv, grad_heads, seg_q, seg_k, bias)


def bias_kernel(per_offset_ref, out_ref):
    wide = jnp.broadcast_to(per_offset_ref[0], (BLOCK, 4 * BLOCK))
    turned = pltpu.roll(wide, 0, 1, stride=1, stride_axis=0)
    out_ref[0] = turned[:, BLOCK:]


def window_bias(per_offset):
    heads = per_offset.shape[0]
    return pl.pallas_call(
        bias_kernel,
        out_shape=jax.ShapeDtypeStruct((heads, BLOCK, 3 * BLOCK), F32),
        grid=(heads,),
        in_specs=[pl.BlockSpec((1, 1, 4 * BLOCK), lambda h: (h, 0, 0))],
        out_specs=pl.BlockSpec((1, BLOCK, 3 * BLOCK), lambda h: (h, 0, 0)),
        name="window_bias",
    )(per_offset[:, None, :])


def gelu_parts(gate):
    c, a = 0.7978845608028654, 0.044715
    square = gate * gate
    tanh = jnp.tanh(c * gate * (1.0 + a * square))
    t = 0.5 * (1.0 + tanh)
    slope = t + 0.5 * gate * (1.0 - tanh * tanh) * c * (1.0 + 3.0 * a * square)
    return gate * t, slope


def body(
    hidden_in,
    segment_ids,
    bucket_of,
    attn_gain,
    w_query,
    w_key,
    w_value,
    w_attn_out,
    bias_table,
    ffn_gain,
    w_gate,
    w_up,
    w_down,
    cotangent,
):
    micro, local_rows, half, width = hidden_in.shape
    rows = micro * local_rows
    seq = segment_ids.shape[2]
    shard = attn_gain.shape[0]
    dp_count = lax.axis_size("dp")
    tp_index = lax.axis_index("tp")
    left_side = tp_index == 0
    local_heads = bias_table.shape[1]
    buckets = bias_table.shape[0]
    head_cols = w_query.shape[1]
    hidden_cols = w_gate.shape[1]
    own_blocks = half // BLOCK
    length = half + BLOCK
    start = tp_index * BLOCK

    def with_halo(own):
        send = jnp.where(left_side, own[:, half - BLOCK :], own[:, :BLOCK])
        other = swap(send, "tp", 0)
        return jnp.where(
            left_side,
            jnp.concatenate([own, other], axis=1),
            jnp.concatenate([other, own], axis=1),
        )

    gains = jnp.pad(jnp.stack([attn_gain, ffn_gain], axis=1), ((0, 0), (0, LANES - 2)))
    first_shard = jnp.concatenate([w_query, w_key, w_value, gains], axis=1)
    second_shard = jnp.concatenate([w_attn_out.T, w_gate, w_up, w_down.T], axis=1)
    cut = first_shard.shape[1] // (2 * LANES) * LANES
    part_a = gather_rows(first_shard[:, :cut], stage_order(False))
    part_b = gather_rows(first_shard[:, cut:], stage_order(True))
    rest = first_shard.shape[1] - cut
    w_qkv = jnp.concatenate(
        [
            part_a[:, :cut],
            part_b[:, : rest - LANES],
            part_a[:, cut:],
            part_b[:, rest : 2 * rest - LANES],
        ],
        axis=1,
    )
    gain1 = part_b[:, rest - LANES].astype(F32)
    gain2 = part_b[:, rest - LANES + 1].astype(F32)
    second = lax.all_gather(second_shard, ("tp", "dp"), axis=0, tiled=True)
    second = second.reshape(2, width, second_shard.shape[1])
    marks = [head_cols, head_cols + hidden_cols, head_cols + 2 * hidden_cols]
    w_out_t = [second[t, :, : marks[0]] for t in range(2)]
    w_gates = [second[t, :, marks[0] : marks[1]] for t in range(2)]
    w_ups = [second[t, :, marks[1] : marks[2]] for t in range(2)]
    w_down_t = [second[t, :, marks[2] :] for t in range(2)]

    x_own = hidden_in.reshape(rows, half, width)
    x_ext = with_halo(x_own)
    seg = segment_ids.reshape(rows, seq)
    seg_ext = lax.dynamic_slice_in_dim(seg, tp_index * (half - BLOCK), length, 1)
    seg_q = jnp.broadcast_to(seg_ext[:, :, None], (rows, length, LANES))
    seg_k = jnp.pad(seg_ext, ((0, 0), (BLOCK, BLOCK)), constant_values=-1)
    seg_k = seg_k.reshape(rows, length // BLOCK + 2, BLOCK)
    other_table = swap(bias_table, "tp", 0)
    table = jnp.where(
        left_side,
        jnp.concatenate([bias_table, other_table], axis=1),
        jnp.concatenate([other_table, bias_table], axis=1),
    )
    near = bucket_of[seq - 1 - 2 * BLOCK : seq - 1 + 2 * BLOCK]
    onehot = (near[None, :] == jnp.arange(buckets, dtype=jnp.int32)[:, None]).astype(F32)
    per_offset = lax.dot_general(
        table, onehot, (((0,), (0,)), ((), ())), precision=HIGHEST_PREC, preferred_element_type=F32
    )
    bias = window_bias(per_offset)
    shift = tp_index.astype(jnp.int32)[None]

    x_f = x_own.astype(F32).reshape(rows * half, width)
    r1 = lax.rsqrt(jnp.mean(x_f * x_f, axis=-1, keepdims=True) + EPSILON)
    xe_f = x_ext.astype(F32)
    r1_ext = lax.rsqrt(jnp.mean(xe_f * xe_f, axis=-1, keepdims=True) + EPSILON)
    n1_ext = (xe_f * r1_ext * gain1).astype(BF)
    qkv = dot_nn(n1_ext.reshape(rows * length, width), w_qkv).astype(BF)
    qkv = qkv.reshape(rows, length, w_qkv.shape[1])
    heads_out = attend_forward(shift, qkv, seg_q, seg_k, bias, own_blocks)
    heads_flat = heads_out.reshape(rows * half, 2 * head_cols)
    w_out_full = jnp.concatenate(w_out_t, axis=1)
    middle = x_f + dot_nt(heads_flat, w_out_full)

    r2 = lax.rsqrt(jnp.mean(middle * middle, axis=-1, keepdims=True) + EPSILON)
    n2 = (middle * r2 * gain2).astype(BF)
    grad_out = cotangent.reshape(rows * half, width)
    block_out, grad_n2 = middle, None
    grads_gate, grads_up, grads_down = [], [], []
    for t in range(2):
        gate, up = dot_nn(n2, w_gates[t]), dot_nn(n2, w_ups[t])
        act, slope = gelu_parts(gate)
        hidden = (act * up).astype(BF)
        block_out = block_out + dot_nt(hidden, w_down_t[t])
        grads_down.append(dot_tn(grad_out, hidden).astype(BF))
        grad_hidden = dot_nn(grad_out, w_down_t[t])
        grad_gate = (grad_hidden * up * slope).astype(BF)
        grad_up = (grad_hidden * act).astype(BF)
        grads_gate.append(dot_tn(n2, grad_gate).astype(BF))
        grads_up.append(dot_tn(n2, grad_up).astype(BF))
        part = dot_nt(grad_gate, w_gates[t]) + dot_nt(grad_up, w_ups[t])
        grad_n2 = part if grad_n2 is None else grad_n2 + part
    grad_gain2 = jnp.sum(grad_n2 * middle * r2, axis=0)
    scaled = grad_n2 * gain2
    grad_middle = (
        grad_out.astype(F32)
        + r2 * scaled
        - middle * (r2 * r2 * r2) * jnp.mean(scaled * middle, axis=-1, keepdims=True)
    )
    grad_attn = grad_middle.astype(BF)
    grad_attn_ext = with_halo(grad_attn.reshape(rows, half, width))
    grad_heads = dot_nn(grad_attn_ext.reshape(rows * length, width), w_out_full).astype(BF)
    grad_heads = grad_heads.reshape(rows, length, 2 * head_cols)
    grad_out_w = dot_tn(grad_attn, heads_flat).astype(BF)
    first_grads = jnp.concatenate(
        [
            jnp.concatenate(
                [
                    grad_out_w[:, t * head_cols : (t + 1) * head_cols],
                    grads_gate[t],
                    grads_up[t],
                    grads_down[t],
                ],
                axis=1,
            )
            for t in range(2)
        ],
        axis=0,
    )
    first_sums = lax.psum_scatter(first_grads, ("tp", "dp"), scatter_dimension=0, tiled=True)
    first_sums = first_sums.astype(F32)

    grad_qkv, diagonals = attend_backward(
        shift, qkv, grad_heads, seg_q, seg_k, bias, own_blocks
    )
    grad_qkv = grad_qkv.reshape(rows * half, w_qkv.shape[1])
    n1 = lax.dynamic_slice_in_dim(n1_ext, start, half, 1).reshape(rows * half, width)
    grad_qkv_w = dot_tn(n1, grad_qkv).astype(BF)
    grad_n1 = dot_nt(grad_qkv, w_qkv)
    grad_gain1 = jnp.sum(grad_n1 * x_f * r1, axis=0)
    scaled = grad_n1 * gain1
    grad_in = (
        grad_middle
        + r1 * scaled
        - x_f * (r1 * r1 * r1) * jnp.mean(scaled * x_f, axis=-1, keepdims=True)
    )
    cols = 3 * head_cols
    cut = cols // (2 * LANES) * LANES
    sums_a = scatter_rows(
        jnp.concatenate([grad_qkv_w[:, :cut], grad_qkv_w[:, cols : cols + cut]], axis=1),
        stage_order(False),
    )
    sums_b = scatter_rows(
        jnp.concatenate([grad_qkv_w[:, cut:cols], grad_qkv_w[:, cols + cut :]], axis=1),
        stage_order(True),
    )
    qkv_sums = jnp.concatenate([sums_a, sums_b], axis=1)

    offset_sums = diagonals[:, 0]
    for step in range(1, 8):
        offset_sums = offset_sums + jnp.roll(diagonals[:, step], -step, axis=1)
    table_sum = lax.dot_general(
        onehot,
        offset_sums,
        (((1,), (1,)), ((), ())),
        precision=HIGHEST_PREC,
        preferred_element_type=F32,
    )
    small = jnp.concatenate([grad_gain1, grad_gain2, table_sum.reshape(-1)])
    small = lax.psum(small, ("dp", "tp"))
    dp_start = lax.axis_index("dp") * shard
    sum_gain1 = lax.dynamic_slice_in_dim(small[:width], dp_start, shard)
    sum_gain2 = lax.dynamic_slice_in_dim(small[width : 2 * width], dp_start, shard)
    sum_table = small[2 * width :].reshape(buckets, 2 * local_heads)
    sum_table = lax.dynamic_slice_in_dim(sum_table, tp_index * local_heads, local_heads, 1)

    shape = (micro, local_rows, half, width)
    return (
        block_out.reshape(shape),
        grad_in.reshape(shape),
        sum_gain1,
        qkv_sums[:, :head_cols],
        qkv_sums[:, head_cols : 2 * head_cols],
        qkv_sums[:, 2 * head_cols :],
        first_sums[:, : marks[0]].T,
        sum_table,
        sum_gain2,
        first_sums[:, marks[0] : marks[1]],
        first_sums[:, marks[1] : marks[2]],
        first_sums[:, marks[2] :].T,
    )


def solution(mesh):
    in_specs = (
        P(None, "dp", "tp", None),
        P(None, "dp", None),
        P(),
        P("dp"),
        P("dp", "tp"),
        P("dp", "tp"),
        P("dp", "tp"),
        P("tp", "dp"),
        P(None, "tp"),
        P("dp"),
        P("dp", "tp"),
        P("dp", "tp"),
        P("tp", "dp"),
        P(None, "dp", "tp", None),
    )
    out_specs = (
        P(None, "dp", "tp", None),
        P(None, "dp", "tp", None),
        P("dp"),
        P("dp", "tp"),
        P("dp", "tp"),
        P("dp", "tp"),
        P("tp", "dp"),
        P(None, "tp"),
        P("dp"),
        P("dp", "tp"),
        P("dp", "tp"),
        P("tp", "dp"),
    )
    return jax.shard_map(body, mesh=mesh, in_specs=in_specs, out_specs=out_specs, check_vma=False)
```

```python
import functools

import jax
import jax.numpy as jnp
from jax import lax
from jax.experimental import pallas as pl
from jax.experimental.pallas import tpu as pltpu
from jax.sharding import PartitionSpec as P

EPSILON = 1e-06
MASKED = -1000000000.0
HIGHEST_PREC = lax.Precision.HIGHEST
BLOCK = 128
LANES = 128
FEED_CHUNK = 1024
BF = jnp.bfloat16
F32 = jnp.float32


def log2_of(count):
    return count.bit_length() - 1


def swap(value, axis, bit):
    count = lax.axis_size(axis)
    return lax.ppermute(value, axis, [(i, i ^ (1 << bit)) for i in range(count)])


def own_bit(axis, bit):
    return (lax.axis_index(axis) >> bit) & 1


def dp_stages():
    return [("dp", b) for b in range(log2_of(lax.axis_size("dp")) - 1, -1, -1)]


def stage_groups():
    stages = dp_stages()
    near = stages[-2:-1]
    return stages[:-2], (near + [("tp", 0)], [("tp", 0)] + near), stages[-1]


def merge(buf, have, stage):
    axis, bit = stage
    other = swap(buf, axis, bit)
    first = own_bit(axis, bit) == 0
    low, high = jnp.where(first, buf, other), jnp.where(first, other, buf)
    if axis == "tp":
        return jnp.concatenate([low, high], axis=-1), have
    where = sum(1 for s in have if s[1] > bit)
    return jnp.stack([low, high], axis=where), have + [stage]


def tie(values, others):
    both = lax.optimization_barrier((tuple(values), tuple(others)))
    return both[0], both[1]


def gather_halves(piece, cut, before_last):
    far, orders, _ = stage_groups()
    have = []
    for stage in far:
        piece, have = merge(piece, have, stage)
    halves = [(piece[..., :cut], have), (piece[..., cut:], have)]
    for step in range(len(orders[0])):
        if step == len(orders[0]) - 1:
            values, before_last = tie([h[0] for h in halves], before_last)
            halves = [(v, h[1]) for v, h in zip(values, halves)]
        halves = [merge(*half, order[step]) for half, order in zip(halves, orders)]
    shape = (-1, piece.shape[-2])
    return [h[0].reshape(shape + h[0].shape[-1:]) for h in halves], before_last


class Term:
    def __init__(self, array, stages, first=0, count=None):
        self.array, self.stages, self.first = array, list(stages), first
        self.count = array.shape[-1] if count is None else count

    def part(self, done, stage, index):
        starts, sizes, kept = [], [], []
        for dim, own in enumerate(self.stages):
            if own == stage:
                starts.append(index)
            elif own in done:
                starts.append(own_bit(*own))
            else:
                starts.append(0)
                kept.append(2)
            sizes.append(1 if own == stage or own in done else 2)
        rest = self.array.shape[len(self.stages) : -1]
        starts += [0] * len(rest) + [self.first]
        sizes += list(rest) + [self.count]
        part = lax.dynamic_slice(self.array, starts, sizes)
        return part.reshape(tuple(kept) + rest + (self.count,))


class Scatter:
    def __init__(self, terms):
        self.terms, self.done = terms, []
        self.stages = list(terms[0].stages)

    def split(self, stage):
        self.stages.remove(stage)
        send = sum(t.part(self.done, stage, 1 - own_bit(*stage)).astype(F32) for t in self.terms)
        self.done = self.done + [stage]
        return send.astype(BF)

    def add(self, array, first=0, count=None):
        self.terms.append(Term(array, self.stages, first, count))

    def total(self):
        return sum(t.part(self.done, None, 0).astype(F32) for t in self.terms)


def start_near(scatters, orders, step, later=()):
    sends = [s.split(order[step]) for s, order in zip(scatters, orders)]
    if later:
        sends, later = tie(sends, later)
    return [swap(send, *order[step]) for send, order in zip(sends, orders)], later


def end_near(scatters, others, later=()):
    if later:
        others, later = tie(others, later)
    for scatter, other in zip(scatters, others):
        scatter.add(other)
    return later


def far_stage(scatters, stage, later=()):
    send = jnp.concatenate([s.split(stage) for s in scatters], axis=-1)
    if later:
        (send,), later = tie([send], later)
    other = swap(send, *stage)
    wide = other.shape[-1] // len(scatters)
    for index, scatter in enumerate(scatters):
        scatter.add(other, index * wide, wide)
    return later


def sum_everywhere(value):
    for axis, bit in [("tp", 0)] + dp_stages():
        value = value + swap(value, axis, bit)
    return value


def inverse_rms(values):
    return lax.rsqrt(jnp.mean(values * values, axis=-1, keepdims=True) + EPSILON)


def key_blocks(block, last):
    return jnp.maximum(block - 1, 0), block, jnp.minimum(block + 1, last)


def block_mask(seg_rows_ref, seg_lanes_ref, block):
    seg_k = seg_rows_ref[0, pl.ds(pl.multiple_of(block * BLOCK, BLOCK), 3 * BLOCK), :]
    seg_q = seg_lanes_ref[0, pl.ds(block + 1, 1), :]
    mask = jnp.where(seg_k == seg_q, 0.0, MASKED)
    return jnp.concatenate([mask, mask], axis=1)


def place_of(block):
    return pl.ds(pl.multiple_of(block * BLOCK, BLOCK), BLOCK)


def lanes_of(column):
    return pl.ds(pl.multiple_of(column, LANES), LANES)


def window_of(ref, blocks, column):
    return jnp.concatenate([ref[0, place_of(b), lanes_of(column)] for b in blocks], axis=0)


def stack_heads(value):
    first = lax.broadcasted_iota(jnp.int32, value.shape, 1) < LANES // 2
    zero = jnp.zeros_like(value)
    return jnp.concatenate([jnp.where(first, value, zero), jnp.where(first, zero, value)], axis=0)


def unstack_heads(value):
    first = lax.broadcasted_iota(jnp.int32, (LANES, BLOCK), 0) < LANES // 2
    return jnp.where(first, value[:, :BLOCK], value[:, BLOCK:]).T


def dot_nt(left, right):
    return lax.dot_general(left, right, (((1,), (1,)), ((), ())), preferred_element_type=F32)


def dot_nn(left, right):
    return lax.dot_general(left, right, (((1,), (0,)), ((), ())), preferred_element_type=F32)


def dot_tn(left, right):
    return lax.dot_general(left, right, (((0,), (0,)), ((), ())), preferred_element_type=F32)


def pair_columns(pair, half_pairs):
    half, local = divmod(pair, half_pairs)
    width = half_pairs * LANES
    base = half * 3 * width + local * LANES
    return base, base + width, base + 2 * width


def softmax_of(logits):
    top = jnp.max(logits, axis=0, keepdims=True)
    powers = jnp.exp(logits - top)
    return powers * (1.0 / jnp.sum(powers, axis=0, keepdims=True))


def column_pieces(part_a, part_b):
    wide_a, wide_b = part_a.shape[1] // 2, part_b.shape[1] // 2
    at, pieces = 0, []
    for half in range(2):
        for ref, wide, used in ((part_a, wide_a, wide_a), (part_b, wide_b, wide_b - LANES)):
            pieces.append((ref, half * wide, at, used))
            at += used
    return pieces


def attend_kernel(
    pairs,
    last,
    shift_ref,
    x_ref,
    halo_ref,
    gain_ref,
    a_own_ref,
    a_other_ref,
    b_own_ref,
    b_other_ref,
    segr_ref,
    segl_ref,
    bias_ref,
    out_ref,
    qkv_ref,
    n1_ref,
    wa_ref,
    wb_ref,
    n1_s,
):
    own_blocks = pl.num_programs(1)
    shift = shift_ref[0]
    length = n1_s.shape[0]

    @pl.when(jnp.logical_and(pl.program_id(0) == 0, pl.program_id(1) == 0))
    def _():
        groups, shard = a_own_ref.shape[:2]
        for whole, own, other in (
            (wa_ref, a_own_ref, a_other_ref),
            (wb_ref, b_own_ref, b_other_ref),
        ):
            for core in range(2):

                @pl.when(shift_ref[1] == core)
                def _():
                    for group in range(groups):
                        for side, ref in ((core, own), (1 - core, other)):
                            start = (2 * group + side) * shard
                            whole[start : start + shard, :] = ref[group]

    @pl.when(pl.program_id(1) == 0)
    def _():
        def normed(value):
            value = value.astype(F32)
            return (value * inverse_rms(value) * gain_ref[...]).astype(BF)

        def own(index, carry):
            value = normed(x_ref[0, place_of(index), :])
            n1_ref[0, place_of(index), :] = value
            n1_s[place_of(index + shift), :] = value
            return carry

        lax.fori_loop(0, own_blocks, own, 0)
        n1_s[place_of((1 - shift) * own_blocks), :] = normed(halo_ref[0])
        chunk = length // 2

        def project(index, carry):
            place = pl.ds(pl.multiple_of(index * chunk, chunk), chunk)
            for ref, start, at, used in column_pieces(wa_ref, wb_ref):
                part = dot_nn(n1_s[place, :], ref[:, start : start + used])
                qkv_ref[0, place, at : at + used] = part.astype(BF)
            return carry

        lax.fori_loop(0, 2, project, 0)

    block = pl.program_id(1) + shift
    blocks = key_blocks(block, last)
    mask = block_mask(segr_ref, segl_ref, block)
    columns = [pair_columns(pair, pairs // 2) for pair in range(pairs)]
    logits = [
        dot_nt(
            window_of(qkv_ref, blocks, col_k),
            stack_heads(qkv_ref[0, place_of(block), col_q : col_q + LANES]),
        )
        for col_q, col_k, _ in columns
    ]
    weights = [
        softmax_of(value + (bias_ref[pair] + mask)).astype(BF) for pair, value in enumerate(logits)
    ]
    mixed = [
        dot_tn(window_of(qkv_ref, blocks, col_v), value)
        for (_, _, col_v), value in zip(columns, weights)
    ]
    for pair, value in enumerate(mixed):
        out_ref[0, :, pair * LANES : (pair + 1) * LANES] = unstack_heads(value).astype(BF)


def attend_forward(place, x_own, x_halo, gain, halves, others, seg_rows, seg_lanes, bias):
    rows, half, model = x_own.shape
    own_blocks = half // BLOCK
    length = half + BLOCK
    pairs = bias.shape[0]
    last = length // BLOCK - 1
    widths = [h.shape[-1] for h in halves]
    width = sum(widths) - 2 * LANES
    steps = rows * own_blocks * pairs
    once = pl.Buffered(1)
    cost = pl.CostEstimate(
        flops=steps * 8 * BLOCK * 3 * BLOCK * LANES + 2 * rows * length * model * width,
        transcendentals=steps * 6 * BLOCK * BLOCK,
        bytes_accessed=rows * length * (width + 2 * model) * 2 + bias.size * 4 + model * width * 2,
    )
    return pl.pallas_call(
        functools.partial(attend_kernel, pairs, last),
        out_shape=(
            jax.ShapeDtypeStruct((rows, half, pairs * LANES), BF),
            jax.ShapeDtypeStruct((rows, length, width), BF),
            jax.ShapeDtypeStruct((rows, half, model), BF),
            jax.ShapeDtypeStruct((model, widths[0]), BF),
            jax.ShapeDtypeStruct((model, widths[1]), BF),
        ),
        grid_spec=pltpu.PrefetchScalarGridSpec(
            num_scalar_prefetch=1,
            grid=(rows, own_blocks),
            in_specs=[
                pl.BlockSpec((1, half, model), lambda r, i, s: (r, 0, 0)),
                pl.BlockSpec((1, BLOCK, model), lambda r, i, s: (r, 0, 0)),
                pl.BlockSpec((1, model), lambda r, i, s: (0, 0), pipeline_mode=once),
                pl.BlockSpec(halves[0].shape, lambda r, i, s: (0, 0, 0), pipeline_mode=once),
                pl.BlockSpec(others[0].shape, lambda r, i, s: (0, 0, 0), pipeline_mode=once),
                pl.BlockSpec(halves[1].shape, lambda r, i, s: (0, 0, 0), pipeline_mode=once),
                pl.BlockSpec(others[1].shape, lambda r, i, s: (0, 0, 0), pipeline_mode=once),
                pl.BlockSpec((1,) + seg_rows.shape[1:], lambda r, i, s: (r, 0, 0)),
                pl.BlockSpec((1,) + seg_lanes.shape[1:], lambda r, i, s: (r, 0, 0)),
                pl.BlockSpec(bias.shape, lambda r, i, s: (0, 0, 0), pipeline_mode=once),
            ],
            out_specs=[
                pl.BlockSpec((1, BLOCK, pairs * LANES), lambda r, i, s: (r, i, 0)),
                pl.BlockSpec((1, length, width), lambda r, i, s: (r, 0, 0)),
                pl.BlockSpec((1, half, model), lambda r, i, s: (r, 0, 0)),
                pl.BlockSpec((model, widths[0]), lambda r, i, s: (0, 0), pipeline_mode=once),
                pl.BlockSpec((model, widths[1]), lambda r, i, s: (0, 0), pipeline_mode=once),
            ],
            scratch_shapes=[pltpu.VMEM((length, model), BF)],
        ),
        compiler_params=pltpu.CompilerParams(
            dimension_semantics=("arbitrary", "arbitrary"), vmem_limit_bytes=48 << 20
        ),
        cost_estimate=cost,
        name="attend_forward",
    )(
        place,
        x_own,
        x_halo,
        gain,
        halves[0],
        others[0],
        halves[1],
        others[1],
        seg_rows,
        seg_lanes,
        bias,
    )


def fold_diagonals(block_sum):
    third = [block_sum[step * BLOCK : (step + 1) * BLOCK] for step in range(3)]
    cur = jnp.concatenate([third[2], third[1], third[0], jnp.zeros((BLOCK, BLOCK), F32)], axis=1)
    count = BLOCK // 2
    while count >= 8:
        cur = cur[count:] + pltpu.roll(cur[:count], count, 1)
        count //= 2
    return cur


def attend_back_kernel(
    pairs,
    last,
    own_blocks,
    shift_ref,
    qkv_ref,
    grad_ref,
    halo_ref,
    wo0_ref,
    wo1_ref,
    segr_ref,
    segl_ref,
    bias_ref,
    out_ref,
    diag_ref,
    heads_s,
    acc_ref,
    sum_ref,
):
    row, block = pl.program_id(0), pl.program_id(1)
    shift = shift_ref[0]
    blocks = key_blocks(block, last)
    mask = block_mask(segr_ref, segl_ref, block)
    owned = jnp.logical_and(block >= shift, block < shift + own_blocks)
    keep = jnp.where(owned, 1.0, 0.0)

    @pl.when(block == 0)
    def _():
        acc_ref[...] = jnp.zeros_like(acc_ref)
        wide = wo0_ref.shape[1]
        own = pl.ds(pl.multiple_of(shift * BLOCK, BLOCK), own_blocks * BLOCK)
        other = place_of((1 - shift) * own_blocks)
        for half, ref in enumerate((wo0_ref, wo1_ref)):
            columns = slice(half * wide, (half + 1) * wide)
            heads_s[own, columns] = dot_nn(grad_ref[0], ref[...]).astype(BF)
            heads_s[other, columns] = dot_nn(halo_ref[0], ref[...]).astype(BF)

    @pl.when(jnp.logical_and(block == 0, row == 0))
    def _():
        sum_ref[...] = jnp.zeros_like(sum_ref)

    columns = [pair_columns(pair, pairs // 2) for pair in range(pairs)]
    here = place_of(block)
    queries = [stack_heads(qkv_ref[0, here, c[0] : c[0] + LANES]) for c in columns]
    grads = [stack_heads(heads_s[here, p * LANES : (p + 1) * LANES]) for p in range(pairs)]
    keys = [window_of(qkv_ref, blocks, c[1]) for c in columns]
    logits = [dot_nt(k, q) for k, q in zip(keys, queries)]
    grads_w = [dot_nt(window_of(qkv_ref, blocks, c[2]), g) for c, g in zip(columns, grads)]
    probs = [softmax_of(value + (bias_ref[p] + mask)) for p, value in enumerate(logits)]
    grads_v = [dot_nn(p.astype(BF), g) for p, g in zip(probs, grads)]
    grads_l = [
        (p * (g - jnp.sum(p * g, axis=0, keepdims=True))).astype(BF)
        for p, g in zip(probs, grads_w)
    ]
    grads_k = [dot_nn(g, q) for g, q in zip(grads_l, queries)]
    grads_q = [dot_tn(k, g) for k, g in zip(keys, grads_l)]
    for pair, (col_q, col_k, col_v) in enumerate(columns):
        sum_ref[pair] += grads_l[pair].astype(F32) * keep
        acc_ref[here, col_q : col_q + LANES] = unstack_heads(grads_q[pair])
        for part in range(3):
            piece = slice(part * BLOCK, (part + 1) * BLOCK)
            acc_ref[place_of(blocks[part]), col_k : col_k + LANES] += grads_k[pair][piece]
            acc_ref[place_of(blocks[part]), col_v : col_v + LANES] += grads_v[pair][piece]

    @pl.when(block == last)
    def _():
        start = pl.multiple_of(shift * BLOCK, BLOCK)
        out_ref[0] = acc_ref[pl.ds(start, own_blocks * BLOCK), :].astype(BF)

    @pl.when(jnp.logical_and(block == last, row == pl.num_programs(0) - 1))
    def _():
        def fold(pair, carry):
            diag_ref[2 * pair] = fold_diagonals(sum_ref[pair, :, :BLOCK])
            diag_ref[2 * pair + 1] = fold_diagonals(sum_ref[pair, :, BLOCK:])
            return carry

        lax.fori_loop(0, pairs, fold, 0)


def attend_backward(
    shift, qkv, grad_attn, grad_halo, weights, out_cols, seg_rows, seg_lanes, bias
):
    rows, length, width = qkv.shape
    half, model = grad_attn.shape[1:]
    own_blocks = half // BLOCK
    pairs = bias.shape[0]
    last = length // BLOCK - 1
    steps = rows * (last + 1) * pairs
    out_at = weights.shape[1] // out_cols - 1
    once = pl.Buffered(1)
    cost = pl.CostEstimate(
        flops=steps * 20 * BLOCK * 3 * BLOCK * LANES + 4 * rows * length * model * out_cols,
        transcendentals=steps * 6 * BLOCK * BLOCK,
        bytes_accessed=qkv.size * 4 + grad_attn.size * 2 + bias.size * 4 + model * out_cols * 4,
    )
    return pl.pallas_call(
        functools.partial(attend_back_kernel, pairs, last, own_blocks),
        out_shape=(
            jax.ShapeDtypeStruct((rows, half, width), BF),
            jax.ShapeDtypeStruct((2 * pairs, 8, 4 * BLOCK), F32),
        ),
        grid_spec=pltpu.PrefetchScalarGridSpec(
            num_scalar_prefetch=1,
            grid=(rows, last + 1),
            in_specs=[
                pl.BlockSpec((1, length, width), lambda r, i, s: (r, 0, 0)),
                pl.BlockSpec((1, half, model), lambda r, i, s: (r, 0, 0)),
                pl.BlockSpec((1, BLOCK, model), lambda r, i, s: (r, 0, 0)),
                pl.BlockSpec((model, out_cols), lambda r, i, s: (0, out_at), pipeline_mode=once),
                pl.BlockSpec((model, out_cols), lambda r, i, s: (1, out_at), pipeline_mode=once),
                pl.BlockSpec((1,) + seg_rows.shape[1:], lambda r, i, s: (r, 0, 0)),
                pl.BlockSpec((1,) + seg_lanes.shape[1:], lambda r, i, s: (r, 0, 0)),
                pl.BlockSpec(bias.shape, lambda r, i, s: (0, 0, 0), pipeline_mode=once),
            ],
            out_specs=[
                pl.BlockSpec((1, half, width), lambda r, i, s: (r, 0, 0)),
                pl.BlockSpec((2 * pairs, 8, 4 * BLOCK), lambda r, i, s: (0, 0, 0)),
            ],
            scratch_shapes=[
                pltpu.VMEM((length, pairs * LANES), BF),
                pltpu.VMEM((length, width), F32),
                pltpu.VMEM(bias.shape, F32),
            ],
        ),
        compiler_params=pltpu.CompilerParams(
            dimension_semantics=("arbitrary", "arbitrary"), vmem_limit_bytes=56 << 20
        ),
        cost_estimate=cost,
        name="attend_backward",
    )(shift, qkv, grad_attn, grad_halo, weights, weights, seg_rows, seg_lanes, bias)


def input_kernel(grad_ref, wa_ref, wb_ref, x_ref, gain_ref, gmid_ref, out_ref, ggain_ref):
    grad_n1 = None
    for ref, start, at, used in column_pieces(wa_ref, wb_ref):
        part = dot_nt(grad_ref[:, at : at + used], ref[:, start : start + used])
        grad_n1 = part if grad_n1 is None else grad_n1 + part
    x = x_ref[...].astype(F32)
    r1 = inverse_rms(x)

    @pl.when(pl.program_id(0) == 0)
    def _():
        ggain_ref[...] = jnp.zeros_like(ggain_ref)

    ggain_ref[...] += jnp.sum(grad_n1 * x * r1, axis=0, keepdims=True)
    scaled = grad_n1 * gain_ref[...]
    inner = jnp.mean(scaled * x, axis=-1, keepdims=True)
    out_ref[...] = gmid_ref[...] + r1 * scaled - x * (r1 * r1 * r1 * inner)


def input_gradient(grad_qkv, part_a, part_b, x_own, gain, grad_middle):
    tokens, width = grad_qkv.shape
    model = x_own.shape[1]
    chunk = min(256, tokens)
    once = pl.Buffered(1)
    here = lambda i: (i, 0)
    whole = lambda i: (0, 0)
    return pl.pallas_call(
        input_kernel,
        out_shape=(
            jax.ShapeDtypeStruct((tokens, model), F32),
            jax.ShapeDtypeStruct((1, model), F32),
        ),
        grid=(tokens // chunk,),
        in_specs=[
            pl.BlockSpec((chunk, width), here),
            pl.BlockSpec(part_a.shape, whole, pipeline_mode=once),
            pl.BlockSpec(part_b.shape, whole, pipeline_mode=once),
            pl.BlockSpec((chunk, model), here),
            pl.BlockSpec((1, model), whole, pipeline_mode=once),
            pl.BlockSpec((chunk, model), here),
        ],
        out_specs=[pl.BlockSpec((chunk, model), here), pl.BlockSpec((1, model), whole)],
        compiler_params=pltpu.CompilerParams(
            dimension_semantics=("arbitrary",), vmem_limit_bytes=40 << 20
        ),
        cost_estimate=pl.CostEstimate(
            flops=2 * tokens * width * model,
            transcendentals=tokens,
            bytes_accessed=tokens * (2 * width + 10 * model) + 2 * width * model,
        ),
        name="input_gradient",
    )(grad_qkv, part_a, part_b, x_own, gain, grad_middle)


def bias_kernel(turned_ref, out_ref):
    for side in range(2):
        wide = jnp.broadcast_to(turned_ref[side], (3 * BLOCK, 4 * BLOCK))
        out = pltpu.roll(wide, BLOCK + 1, 1, stride=1, stride_axis=0)
        out_ref[0, :, side * BLOCK : (side + 1) * BLOCK] = out[:, :BLOCK]


def window_bias(turned):
    pairs = turned.shape[0] // 2
    return pl.pallas_call(
        bias_kernel,
        out_shape=jax.ShapeDtypeStruct((pairs, 3 * BLOCK, 2 * BLOCK), F32),
        grid=(pairs,),
        in_specs=[pl.BlockSpec((2, 1, 4 * BLOCK), lambda h: (h, 0, 0))],
        out_specs=pl.BlockSpec((1, 3 * BLOCK, 2 * BLOCK), lambda h: (h, 0, 0)),
        name="window_bias",
    )(turned[:, None, :])


def gelu_parts(gate):
    c, a = 0.7978845608028654, 0.044715
    square = gate * gate
    tanh = jnp.tanh(gate * (c + (c * a) * square))
    t = 0.5 + 0.5 * tanh
    slope = t + (0.5 * gate) * (1.0 - tanh * tanh) * (c + (3.0 * c * a) * square)
    return gate * t, slope


def split_rows(own_core, shard, grad, keep_ref, send_ref, where):
    for core in range(2):
        first, second = (keep_ref, send_ref) if core == 0 else (send_ref, keep_ref)

        @pl.when(own_core == core)
        def _():
            for group in range(grad.shape[0] // (2 * shard)):
                start = group * 2 * shard
                first[(0, group) + where] = grad[start : start + shard]
                second[(0, group) + where] = grad[start + shard : start + 2 * shard]


def feed_kernel(
    chunk,
    shard,
    core_ref,
    heads_ref,
    x_ref,
    gain_ref,
    cot_ref,
    wo0_ref,
    wo1_ref,
    wg_ref,
    wu_ref,
    wd_ref,
    out_ref,
    gmid_ref,
    gattn_ref,
    ggain_ref,
    keep_ref,
    send_ref,
    mid_s,
    n2_s,
    n2t_s,
    cott_s,
    hid_s,
    gg_s,
    gu_s,
    gn2_s,
):
    tokens, width = x_ref.shape
    step = pl.program_id(0) * pl.num_programs(1) + pl.program_id(1)
    final = pl.num_programs(0) * pl.num_programs(1) - 1
    half = heads_ref.shape[1] // 2

    def for_chunks(work):
        def one(index, carry):
            work(pl.ds(pl.multiple_of(index * chunk, chunk), chunk))
            return carry

        lax.fori_loop(0, tokens // chunk, one, 0)

    @pl.when(step == 0)
    def _():
        def work(place):
            middle = x_ref[place, :].astype(F32)
            middle = middle + dot_nt(heads_ref[place, :half], wo0_ref[...])
            middle = middle + dot_nt(heads_ref[place, half:], wo1_ref[...])
            mid_s[place, :] = middle
            out_ref[place, :] = middle
            normed = (middle * inverse_rms(middle) * gain_ref[...]).astype(BF)
            n2_s[place, :] = normed
            n2t_s[:, place] = normed.T
            cott_s[:, place] = cot_ref[place, :].T
            gn2_s[place, :] = jnp.zeros((chunk, width), F32)

        for_chunks(work)

    def work(place):
        n2, cot = n2_s[place, :], cot_ref[place, :]
        act, slope = gelu_parts(dot_nn(n2, wg_ref[...]))
        up = dot_nn(n2, wu_ref[...])
        grad_hidden = dot_nn(cot, wd_ref[...])
        hidden = (act * up).astype(BF)
        grad_gate = (grad_hidden * up * slope).astype(BF)
        grad_up = (grad_hidden * act).astype(BF)
        hid_s[place, :] = hidden
        gg_s[place, :] = grad_gate
        gu_s[place, :] = grad_up
        out_ref[place, :] += dot_nt(hidden, wd_ref[...])
        gn2_s[place, :] += dot_nt(grad_gate, wg_ref[...]) + dot_nt(grad_up, wu_ref[...])

    for_chunks(work)

    def store(kind, grad):
        split_rows(core_ref[0], shard, grad.astype(BF), keep_ref, send_ref, (kind,))

    store(0, dot_nn(n2t_s[...], gg_s[...]))
    store(1, dot_nn(n2t_s[...], gu_s[...]))
    store(2, dot_nn(cott_s[...], hid_s[...]))

    @pl.when(step == final)
    def _():
        ggain_ref[...] = jnp.zeros_like(ggain_ref)

        def work(place):
            middle, grad_n2 = mid_s[place, :], gn2_s[place, :]
            r2 = inverse_rms(middle)
            ggain_ref[...] += jnp.sum(grad_n2 * middle * r2, axis=0, keepdims=True)
            scaled = grad_n2 * gain_ref[...]
            inner = jnp.mean(scaled * middle, axis=-1, keepdims=True)
            grad = cot_ref[place, :].astype(F32) + r2 * scaled - middle * (r2 * r2 * r2 * inner)
            gmid_ref[place, :] = grad
            gattn_ref[place, :] = grad.astype(BF)

        for_chunks(work)


def feed_forward(core, heads_out, x_own, gain, cotangent, weights, hidden_cols, shard):
    tokens, width = x_own.shape
    wide = min(512, hidden_cols)
    steps = hidden_cols // wide
    out_cols = heads_out.shape[1] // 2
    out_at = 3 * hidden_cols // out_cols
    groups = width // (2 * shard)
    whole = lambda t, j, c: (0, 0)
    once = pl.Buffered(1)
    piece = jax.ShapeDtypeStruct((2, groups, 3, shard, hidden_cols), BF)
    piece_spec = pl.BlockSpec((1, groups, 3, shard, wide), lambda t, j, c: (t, 0, 0, 0, j))
    return pl.pallas_call(
        functools.partial(feed_kernel, min(FEED_CHUNK, tokens), shard),
        out_shape=(
            jax.ShapeDtypeStruct((tokens, width), F32),
            jax.ShapeDtypeStruct((tokens, width), F32),
            jax.ShapeDtypeStruct((tokens, width), BF),
            jax.ShapeDtypeStruct((1, width), F32),
            piece,
            piece,
        ),
        grid_spec=pltpu.PrefetchScalarGridSpec(
            num_scalar_prefetch=1,
            grid=(2, steps),
            in_specs=[
                pl.BlockSpec((tokens, 2 * out_cols), whole, pipeline_mode=once),
                pl.BlockSpec((tokens, width), whole, pipeline_mode=once),
                pl.BlockSpec((1, width), whole, pipeline_mode=once),
                pl.BlockSpec((tokens, width), whole, pipeline_mode=once),
                pl.BlockSpec((width, out_cols), lambda t, j, c: (0, out_at), pipeline_mode=once),
                pl.BlockSpec((width, out_cols), lambda t, j, c: (1, out_at), pipeline_mode=once),
                pl.BlockSpec((width, wide), lambda t, j, c: (t, j)),
                pl.BlockSpec((width, wide), lambda t, j, c: (t, steps + j)),
                pl.BlockSpec((width, wide), lambda t, j, c: (t, 2 * steps + j)),
            ],
            out_specs=[
                pl.BlockSpec((tokens, width), whole, pipeline_mode=once),
                pl.BlockSpec((tokens, width), whole, pipeline_mode=once),
                pl.BlockSpec((tokens, width), whole, pipeline_mode=once),
                pl.BlockSpec((1, width), whole, pipeline_mode=once),
                piece_spec,
                piece_spec,
            ],
            scratch_shapes=[
                pltpu.VMEM((tokens, width), F32),
                pltpu.VMEM((tokens, width), BF),
                pltpu.VMEM((width, tokens), BF),
                pltpu.VMEM((width, tokens), BF),
                pltpu.VMEM((tokens, wide), BF),
                pltpu.VMEM((tokens, wide), BF),
                pltpu.VMEM((tokens, wide), BF),
                pltpu.VMEM((tokens, width), F32),
            ],
        ),
        compiler_params=pltpu.CompilerParams(
            dimension_semantics=("arbitrary", "arbitrary"), vmem_limit_bytes=56 << 20
        ),
        cost_estimate=pl.CostEstimate(
            flops=2 * tokens * width * (18 * hidden_cols + 2 * out_cols),
            transcendentals=2 * tokens * hidden_cols,
            bytes_accessed=weights.size * 2 + tokens * width * 16 + 12 * width * hidden_cols,
        ),
        name="feed_forward",
    )(core, heads_out, x_own, gain, cotangent, weights, weights, weights, weights, weights)


def weight_kernel(shard, core_ref, n1_ref, gqkv_ref, gattn_ref, heads_ref, keep_ref, send_ref):
    wide = gqkv_ref.shape[1] // 3
    for index in range(4):
        columns = slice(index * wide, (index + 1) * wide)
        if index < 3:
            grad = dot_tn(n1_ref[...], gqkv_ref[:, columns])
        else:
            grad = dot_tn(gattn_ref[...], heads_ref[...])
        split_rows(
            core_ref[0], shard, grad.astype(BF), keep_ref, send_ref, (slice(None), columns)
        )


def weight_gradients(core, n1, grad_qkv, grad_attn, heads_out, shard):
    tokens, model = n1.shape
    wide = heads_out.shape[1] // 2
    groups = model // (2 * shard)
    whole = lambda t, c: (0, 0)
    half = lambda t, c: (0, t)
    once = pl.Buffered(1)
    piece = jax.ShapeDtypeStruct((2, groups, shard, 4 * wide), BF)
    piece_spec = pl.BlockSpec((1, groups, shard, 4 * wide), lambda t, c: (t, 0, 0, 0))
    return pl.pallas_call(
        functools.partial(weight_kernel, shard),
        out_shape=(piece, piece),
        grid_spec=pltpu.PrefetchScalarGridSpec(
            num_scalar_prefetch=1,
            grid=(2,),
            in_specs=[
                pl.BlockSpec((tokens, model), whole, pipeline_mode=once),
                pl.BlockSpec((tokens, 3 * wide), half),
                pl.BlockSpec((tokens, model), whole, pipeline_mode=once),
                pl.BlockSpec((tokens, wide), half),
            ],
            out_specs=[piece_spec, piece_spec],
        ),
        compiler_params=pltpu.CompilerParams(
            dimension_semantics=("arbitrary",), vmem_limit_bytes=40 << 20
        ),
        cost_estimate=pl.CostEstimate(
            flops=16 * tokens * model * wide,
            transcendentals=0,
            bytes_accessed=tokens * (4 * model + 16 * wide) + 16 * model * wide,
        ),
        name="weight_gradients",
    )(core, n1, grad_qkv, grad_attn, heads_out)


def body(
    hidden_in,
    segment_ids,
    bucket_of,
    attn_gain,
    w_query,
    w_key,
    w_value,
    w_attn_out,
    bias_table,
    ffn_gain,
    w_gate,
    w_up,
    w_down,
    cotangent,
):
    micro, local_rows, half, width = hidden_in.shape
    rows = micro * local_rows
    seq = segment_ids.shape[2]
    shard = attn_gain.shape[0]
    dp_count = lax.axis_size("dp")
    tp_index = lax.axis_index("tp")
    left_side = tp_index == 0
    local_heads = bias_table.shape[1]
    buckets = bias_table.shape[0]
    head_cols = w_query.shape[1]
    hidden_cols = w_gate.shape[1]
    own_blocks = half // BLOCK
    length = half + BLOCK

    def halo_of(own):
        send = jnp.where(left_side, own[:, half - BLOCK :], own[:, :BLOCK])
        return swap(send, "tp", 0)

    gains = jnp.pad(jnp.stack([attn_gain, ffn_gain], axis=1), ((0, 0), (0, LANES - 2)))
    first_shard = jnp.concatenate([w_query, w_key, w_value, gains], axis=1)
    second_shard = jnp.concatenate([w_gate, w_up, w_down.T, w_attn_out.T], axis=1)
    cut = first_shard.shape[1] // (2 * LANES) * LANES
    second = lax.all_gather(second_shard, ("tp", "dp"), axis=0, tiled=True)
    x_own = hidden_in.reshape(rows, half, width)
    x_halo = halo_of(x_own)
    seg = segment_ids.reshape(rows, seq)
    seg_ext = lax.dynamic_slice_in_dim(seg, tp_index * (half - BLOCK), length, 1)
    seg_pad = jnp.pad(seg_ext, ((0, 0), (BLOCK, BLOCK)), constant_values=-1)
    seg_rows = jnp.broadcast_to(seg_pad[:, :, None], seg_pad.shape + (LANES,))
    seg_lanes = seg_pad.reshape(rows, length // BLOCK + 2, BLOCK)
    other_table = swap(bias_table, "tp", 0)
    table = jnp.where(
        left_side,
        jnp.concatenate([bias_table, other_table], axis=1),
        jnp.concatenate([other_table, bias_table], axis=1),
    )
    near = bucket_of[seq - 2 * BLOCK - 1 : seq + 2 * BLOCK - 1][::-1]
    onehot = (near[None, :] == jnp.arange(buckets, dtype=jnp.int32)[:, None]).astype(F32)
    per_offset = lax.dot_general(
        table, onehot, (((0,), (0,)), ((), ())), precision=HIGHEST_PREC, preferred_element_type=F32
    )
    bias = window_bias(per_offset)
    shift = tp_index.astype(jnp.int32)[None]
    core = (lax.axis_index("dp") & 1).astype(jnp.int32)[None]

    near_halves, (bias, x_halo) = gather_halves(first_shard, cut, (bias, x_halo))
    far_halves = [swap(value, *stage_groups()[2]) for value in near_halves]
    gain_at = near_halves[1].shape[-1] // 2 - LANES
    gain_rows = [h[1][..., gain_at : gain_at + 2] for h in (near_halves, far_halves)]
    own_first = core[0] == 0
    gain_rows = jnp.stack(
        [
            jnp.where(own_first, gain_rows[0], gain_rows[1]),
            jnp.where(own_first, gain_rows[1], gain_rows[0]),
        ],
        axis=1,
    )
    both_gains = gain_rows.reshape(width, 2).T.astype(F32)
    gain1, gain2 = both_gains[:1], both_gains[1:]

    heads_out, qkv, n1, part_a, part_b = attend_forward(
        jnp.concatenate([shift, core]),
        x_own,
        x_halo,
        gain1,
        near_halves,
        far_halves,
        seg_rows,
        seg_lanes,
        bias,
    )
    heads_flat = heads_out.reshape(rows * half, 2 * head_cols)

    cot_flat = cotangent.reshape(rows * half, width)
    block_out, grad_middle, grad_attn, grad_gain2, keep, send = feed_forward(
        core,
        heads_flat,
        x_own.reshape(rows * half, width),
        gain2,
        cot_flat,
        second,
        hidden_cols,
        shard,
    )
    grad_attn_rows = grad_attn.reshape(rows, half, width)
    grad_halo = halo_of(grad_attn_rows)

    far, near, cores = stage_groups()
    stages = [("tp", 0)] + dp_stages()[:-1]

    def both_cores(keep, send, split):
        terms = [
            value.reshape((2,) * len(stages) + value.shape[2:]) for value in (keep, swap(send, *cores))
        ]
        total = keep.shape[-1]
        ranges = ((0, split), (split, total - split))
        return [Scatter([Term(t, stages, *cut) for t in terms]) for cut in ranges]

    feed = both_cores(keep, send, hidden_cols // 2)
    others, (grad_attn_rows, grad_halo) = start_near(feed, near, 0, (grad_attn_rows, grad_halo))

    grad_qkv, diagonals = attend_backward(
        shift, qkv, grad_attn_rows, grad_halo, second, head_cols, seg_rows, seg_lanes, bias
    )
    (grad_qkv,) = end_near(feed, others, (grad_qkv,))
    if len(near[0]) > 1:
        others, (grad_qkv,) = start_near(feed, near, 1, (grad_qkv,))
    grad_qkv = grad_qkv.reshape(rows * half, grad_qkv.shape[-1])
    keep_w, send_w = weight_gradients(
        core, n1.reshape(rows * half, width), grad_qkv, grad_attn, heads_flat, shard
    )
    tail = both_cores(keep_w, send_w, 2 * head_cols)
    if len(near[0]) > 1:
        end_near(feed, others)
    for stage in far[1:][::-1]:
        far_stage(feed, stage)
    others, (grad_qkv,) = start_near(tail, near, 0, (grad_qkv,))
    grad_in, grad_gain1 = input_gradient(
        grad_qkv, part_a, part_b, x_own.reshape(rows * half, width), gain1, grad_middle
    )
    end_near(tail, others)
    if len(near[0]) > 1:
        others, _ = start_near(tail, near, 1)
        end_near(tail, others)
    for stage in far[:1]:
        far_stage(feed, stage)
    for stage in far[::-1]:
        far_stage(tail, stage)
    feed_sums = jnp.concatenate([s.total() for s in feed], axis=-1)
    sums_a, sums_b = [s.total() for s in tail]

    diagonals_turned = [jnp.roll(diagonals[:, s], 7 - s, axis=1) for s in range(8)]
    offset_sums = diagonals_turned[0]
    for step in range(1, 8):
        offset_sums = offset_sums + diagonals_turned[step]
    table_sum = lax.dot_general(
        onehot,
        offset_sums,
        (((1,), (1,)), ((), ())),
        precision=HIGHEST_PREC,
        preferred_element_type=F32,
    )
    small = jnp.concatenate([grad_gain1[0], grad_gain2[0], table_sum.reshape(-1)])
    small = sum_everywhere(small.reshape(-1, LANES)).reshape(-1)
    dp_start = lax.axis_index("dp") * shard
    sum_gain1 = lax.dynamic_slice_in_dim(small[:width], dp_start, shard)
    sum_gain2 = lax.dynamic_slice_in_dim(small[width : 2 * width], dp_start, shard)
    sum_table = small[2 * width :].reshape(buckets, 2 * local_heads)
    sum_table = lax.dynamic_slice_in_dim(sum_table, tp_index * local_heads, local_heads, 1)

    shape = (micro, local_rows, half, width)
    return (
        block_out.reshape(shape),
        grad_in.reshape(shape),
        sum_gain1,
        sums_a[:, :head_cols],
        sums_a[:, head_cols:],
        sums_b[:, :head_cols],
        sums_b[:, head_cols:].T,
        sum_table,
        sum_gain2,
        feed_sums[0],
        feed_sums[1],
        feed_sums[2].T,
    )


def solution(mesh):
    in_specs = (
        P(None, "dp", "tp", None),
        P(None, "dp", None),
        P(),
        P("dp"),
        P("dp", "tp"),
        P("dp", "tp"),
        P("dp", "tp"),
        P("tp", "dp"),
        P(None, "tp"),
        P("dp"),
        P("dp", "tp"),
        P("dp", "tp"),
        P("tp", "dp"),
        P(None, "dp", "tp", None),
    )
    out_specs = (
        P(None, "dp", "tp", None),
        P(None, "dp", "tp", None),
        P("dp"),
        P("dp", "tp"),
        P("dp", "tp"),
        P("dp", "tp"),
        P("tp", "dp"),
        P(None, "tp"),
        P("dp"),
        P("dp", "tp"),
        P("dp", "tp"),
        P("tp", "dp"),
    )
    return jax.shard_map(body, mesh=mesh, in_specs=in_specs, out_specs=out_specs, check_vma=False)
```

```python
import functools

import jax
import jax.numpy as jnp
from jax import lax
from jax.experimental import pallas as pl
from jax.experimental.pallas import tpu as pltpu
from jax.sharding import PartitionSpec as P

EPSILON = 1e-06
MASKED = -1000000000.0
HIGHEST_PREC = lax.Precision.HIGHEST
BLOCK = 128
LANES = 128
FEED_CHUNK = 1024
BF = jnp.bfloat16
F32 = jnp.float32


def log2_of(count):
    return count.bit_length() - 1


def swap(value, axis, bit):
    count = lax.axis_size(axis)
    return lax.ppermute(value, axis, [(i, i ^ (1 << bit)) for i in range(count)])


def swap_flat(value, axis, bit):
    return swap(value.reshape(-1, value.shape[-1]), axis, bit).reshape(value.shape)


def own_bit(axis, bit):
    return (lax.axis_index(axis) >> bit) & 1


def dp_stages():
    return [("dp", b) for b in range(log2_of(lax.axis_size("dp")) - 1, -1, -1)]


def stage_groups():
    stages = dp_stages()
    near = stages[-2:-1]
    return stages[:-2], (near + [("tp", 0)], [("tp", 0)] + near), stages[-1]


def merge(buf, have, stage):
    axis, bit = stage
    other = swap(buf, axis, bit)
    first = own_bit(axis, bit) == 0
    low, high = jnp.where(first, buf, other), jnp.where(first, other, buf)
    if axis == "tp":
        return jnp.concatenate([low, high], axis=-1), have
    where = sum(1 for s in have if s[1] > bit)
    return jnp.stack([low, high], axis=where), have + [stage]


def tie(values, others):
    both = lax.optimization_barrier((tuple(values), tuple(others)))
    return both[0], both[1]


def gather_halves(piece, cut, before_last):
    far, orders, _ = stage_groups()
    have = []
    for stage in far:
        piece, have = merge(piece, have, stage)
    halves = [(piece[..., :cut], have), (piece[..., cut:], have)]
    for step in range(len(orders[0])):
        done = merge(*halves[0], orders[0][step])
        if step == 0:
            (value, first), before_last = tie([halves[1][0], done[0]], before_last)
            halves[1], done = (value, halves[1][1]), (first, done[1])
        halves = [done, merge(*halves[1], orders[1][step])]
    shape = (-1, piece.shape[-2])
    return [h[0].reshape(shape + h[0].shape[-1:]) for h in halves], before_last


def flips(group):
    chosen = [()]
    for stage in reversed(group):
        chosen += [c + (stage,) for c in chosen]
    return chosen[1:]


def swap_with(value, flip):
    flat = value.reshape(-1, value.shape[-1])
    across = sum(1 << bit for axis, bit in flip if axis == "tp")
    along = sum(1 << bit for axis, bit in flip if axis == "dp")
    if not across:
        axes, pairs = "dp", [(i, i ^ along) for i in range(lax.axis_size("dp"))]
    elif not along:
        axes, pairs = "tp", [(i, i ^ across) for i in range(lax.axis_size("tp"))]
    else:
        count = lax.axis_size("tp")
        axes = ("dp", "tp")
        pairs = [
            (i * count + j, (i ^ along) * count + (j ^ across))
            for i in range(lax.axis_size("dp"))
            for j in range(count)
        ]
    return lax.ppermute(flat, axes, pairs).reshape(value.shape)


class Term:
    def __init__(self, array, stages, first=0, count=None):
        self.array, self.stages, self.first = array, list(stages), first
        self.count = array.shape[-1] if count is None else count

    def part(self, fixed, flip):
        starts, sizes, kept = [], [], []
        for stage in self.stages:
            if stage in fixed:
                starts.append(1 - own_bit(*stage) if stage in flip else own_bit(*stage))
                sizes.append(1)
            else:
                starts.append(0)
                sizes.append(2)
                kept.append(2)
        rest = self.array.shape[len(self.stages) : -1]
        starts += [0] * len(rest) + [self.first]
        sizes += list(rest) + [self.count]
        part = lax.dynamic_slice(self.array, starts, sizes)
        return part.reshape(tuple(kept) + rest + (self.count,))


class Scatter:
    def __init__(self, terms):
        self.terms, self.done = terms, []
        self.stages = list(terms[0].stages)

    def sends(self, group):
        self.done = self.done + list(group)
        self.stages = [s for s in self.stages if s not in group]
        return [
            sum(t.part(self.done, flip).astype(F32) for t in self.terms).astype(BF)
            for flip in flips(group)
        ]

    def add(self, array, first=0, count=None):
        self.terms.append(Term(array, self.stages, first, count))

    def total(self):
        return sum(t.part(self.done, ()).astype(F32) for t in self.terms)


def start_sends(scatters, groups, later=()):
    sends = [s.sends(group) for s, group in zip(scatters, groups)]
    count = len(sends[0])
    if later:
        flat, later = tie([x for part in sends for x in part], later)
        sends = [flat[i * count : (i + 1) * count] for i in range(len(scatters))]
    others = [
        [swap_with(x, flip) for x, flip in zip(part, flips(group))]
        for part, group in zip(sends, groups)
    ]
    return others, later


def end_sends(scatters, others, later=()):
    count = len(others[0])
    flat = [x for part in others for x in part]
    if later:
        flat, later = tie(flat, later)
    for index, scatter in enumerate(scatters):
        for other in flat[index * count : (index + 1) * count]:
            scatter.add(other)
    return later


def start_joint(scatters, group, later=()):
    sends = [jnp.concatenate(parts, axis=-1) for parts in zip(*[s.sends(group) for s in scatters])]
    if later:
        sends, later = tie(sends, later)
    return [swap_with(x, flip) for x, flip in zip(sends, flips(group))], later


def end_joint(scatters, others, later=()):
    if later:
        others, later = tie(others, later)
    for other in others:
        at = 0
        for scatter in scatters:
            count = scatter.terms[0].count
            scatter.add(other, at, count)
            at += count
    return later


def inverse_rms(values):
    return lax.rsqrt(jnp.mean(values * values, axis=-1, keepdims=True) + EPSILON)


def key_blocks(block, last):
    return jnp.maximum(block - 1, 0), block, jnp.minimum(block + 1, last)


def block_mask(seg_rows_ref, seg_lanes_ref, block):
    seg_k = seg_rows_ref[0, pl.ds(pl.multiple_of(block * BLOCK, BLOCK), 3 * BLOCK), :]
    seg_q = seg_lanes_ref[0, pl.ds(block + 1, 1), :]
    mask = jnp.where(seg_k == seg_q, 0.0, MASKED)
    return jnp.concatenate([mask, mask], axis=1)


def place_of(block):
    return pl.ds(pl.multiple_of(block * BLOCK, BLOCK), BLOCK)


def lanes_of(column):
    return pl.ds(pl.multiple_of(column, LANES), LANES)


def window_of(ref, blocks, column):
    return jnp.concatenate([ref[0, place_of(b), lanes_of(column)] for b in blocks], axis=0)


def stack_heads(value):
    first = lax.broadcasted_iota(jnp.int32, value.shape, 1) < LANES // 2
    zero = jnp.zeros_like(value)
    return jnp.concatenate([jnp.where(first, value, zero), jnp.where(first, zero, value)], axis=0)


def unstack_heads(value):
    first = lax.broadcasted_iota(jnp.int32, (LANES, BLOCK), 0) < LANES // 2
    return jnp.where(first, value[:, :BLOCK], value[:, BLOCK:]).T


def dot_nt(left, right):
    return lax.dot_general(left, right, (((1,), (1,)), ((), ())), preferred_element_type=F32)


def dot_nn(left, right):
    return lax.dot_general(left, right, (((1,), (0,)), ((), ())), preferred_element_type=F32)


def dot_tn(left, right):
    return lax.dot_general(left, right, (((0,), (0,)), ((), ())), preferred_element_type=F32)


def pair_columns(pair, half_pairs):
    half, local = divmod(pair, half_pairs)
    width = half_pairs * LANES
    base = half * 3 * width + local * LANES
    return base, base + width, base + 2 * width


def softmax_of(logits):
    top = jnp.max(logits, axis=0, keepdims=True)
    powers = jnp.exp(logits - top)
    return powers * (1.0 / jnp.sum(powers, axis=0, keepdims=True))


def column_pieces(part_a, part_b):
    wide_a, wide_b = part_a.shape[1] // 2, part_b.shape[1] // 2
    at, pieces = 0, []
    for half in range(2):
        for ref, wide, used in ((part_a, wide_a, wide_a), (part_b, wide_b, wide_b - LANES)):
            pieces.append((ref, half * wide, at, used))
            at += used
    return pieces


def attend_kernel(
    pairs,
    last,
    shift_ref,
    x_ref,
    halo_ref,
    gain_ref,
    a_own_ref,
    a_other_ref,
    b_own_ref,
    b_other_ref,
    segr_ref,
    segl_ref,
    bias_ref,
    out_ref,
    qkv_ref,
    n1_ref,
    wa_ref,
    wb_ref,
    n1_s,
):
    own_blocks = pl.num_programs(1)
    shift = shift_ref[0]
    length = n1_s.shape[0]

    @pl.when(jnp.logical_and(pl.program_id(0) == 0, pl.program_id(1) == 0))
    def _():
        groups, shard = a_own_ref.shape[:2]
        for whole, own, other in (
            (wa_ref, a_own_ref, a_other_ref),
            (wb_ref, b_own_ref, b_other_ref),
        ):
            for core in range(2):

                @pl.when(shift_ref[1] == core)
                def _():
                    for group in range(groups):
                        for side, ref in ((core, own), (1 - core, other)):
                            start = (2 * group + side) * shard
                            whole[start : start + shard, :] = ref[group]

    @pl.when(pl.program_id(1) == 0)
    def _():
        def normed(value):
            value = value.astype(F32)
            return (value * inverse_rms(value) * gain_ref[...]).astype(BF)

        def own(index, carry):
            value = normed(x_ref[0, place_of(index), :])
            n1_ref[0, place_of(index), :] = value
            n1_s[place_of(index + shift), :] = value
            return carry

        lax.fori_loop(0, own_blocks, own, 0)
        n1_s[place_of((1 - shift) * own_blocks), :] = normed(halo_ref[0])
        chunk = length // 2

        def project(index, carry):
            place = pl.ds(pl.multiple_of(index * chunk, chunk), chunk)
            for ref, start, at, used in column_pieces(wa_ref, wb_ref):
                part = dot_nn(n1_s[place, :], ref[:, start : start + used])
                qkv_ref[0, place, at : at + used] = part.astype(BF)
            return carry

        lax.fori_loop(0, 2, project, 0)

    block = pl.program_id(1) + shift
    blocks = key_blocks(block, last)
    mask = block_mask(segr_ref, segl_ref, block)
    columns = [pair_columns(pair, pairs // 2) for pair in range(pairs)]
    logits = [
        dot_nt(
            window_of(qkv_ref, blocks, col_k),
            stack_heads(qkv_ref[0, place_of(block), col_q : col_q + LANES]),
        )
        for col_q, col_k, _ in columns
    ]
    weights = [
        softmax_of(value + (bias_ref[pair] + mask)).astype(BF) for pair, value in enumerate(logits)
    ]
    mixed = [
        dot_tn(window_of(qkv_ref, blocks, col_v), value)
        for (_, _, col_v), value in zip(columns, weights)
    ]
    for pair, value in enumerate(mixed):
        out_ref[0, :, pair * LANES : (pair + 1) * LANES] = unstack_heads(value).astype(BF)


def attend_forward(place, x_own, x_halo, gain, halves, others, seg_rows, seg_lanes, bias):
    rows, half, model = x_own.shape
    own_blocks = half // BLOCK
    length = half + BLOCK
    pairs = bias.shape[0]
    last = length // BLOCK - 1
    widths = [h.shape[-1] for h in halves]
    width = sum(widths) - 2 * LANES
    steps = rows * own_blocks * pairs
    once = pl.Buffered(1)
    cost = pl.CostEstimate(
        flops=steps * 8 * BLOCK * 3 * BLOCK * LANES + 2 * rows * length * model * width,
        transcendentals=steps * 6 * BLOCK * BLOCK,
        bytes_accessed=rows * length * (width + 2 * model) * 2 + bias.size * 4 + model * width * 2,
    )
    return pl.pallas_call(
        functools.partial(attend_kernel, pairs, last),
        out_shape=(
            jax.ShapeDtypeStruct((rows, half, pairs * LANES), BF),
            jax.ShapeDtypeStruct((rows, length, width), BF),
            jax.ShapeDtypeStruct((rows, half, model), BF),
            jax.ShapeDtypeStruct((model, widths[0]), BF),
            jax.ShapeDtypeStruct((model, widths[1]), BF),
        ),
        grid_spec=pltpu.PrefetchScalarGridSpec(
            num_scalar_prefetch=1,
            grid=(rows, own_blocks),
            in_specs=[
                pl.BlockSpec((1, half, model), lambda r, i, s: (r, 0, 0)),
                pl.BlockSpec((1, BLOCK, model), lambda r, i, s: (r, 0, 0)),
                pl.BlockSpec((1, model), lambda r, i, s: (0, 0), pipeline_mode=once),
                pl.BlockSpec(halves[0].shape, lambda r, i, s: (0, 0, 0), pipeline_mode=once),
                pl.BlockSpec(others[0].shape, lambda r, i, s: (0, 0, 0), pipeline_mode=once),
                pl.BlockSpec(halves[1].shape, lambda r, i, s: (0, 0, 0), pipeline_mode=once),
                pl.BlockSpec(others[1].shape, lambda r, i, s: (0, 0, 0), pipeline_mode=once),
                pl.BlockSpec((1,) + seg_rows.shape[1:], lambda r, i, s: (r, 0, 0)),
                pl.BlockSpec((1,) + seg_lanes.shape[1:], lambda r, i, s: (r, 0, 0)),
                pl.BlockSpec(bias.shape, lambda r, i, s: (0, 0, 0), pipeline_mode=once),
            ],
            out_specs=[
                pl.BlockSpec((1, BLOCK, pairs * LANES), lambda r, i, s: (r, i, 0)),
                pl.BlockSpec((1, length, width), lambda r, i, s: (r, 0, 0)),
                pl.BlockSpec((1, half, model), lambda r, i, s: (r, 0, 0)),
                pl.BlockSpec((model, widths[0]), lambda r, i, s: (0, 0), pipeline_mode=once),
                pl.BlockSpec((model, widths[1]), lambda r, i, s: (0, 0), pipeline_mode=once),
            ],
            scratch_shapes=[pltpu.VMEM((length, model), BF)],
        ),
        compiler_params=pltpu.CompilerParams(
            dimension_semantics=("arbitrary", "arbitrary"), vmem_limit_bytes=48 << 20
        ),
        cost_estimate=cost,
        name="attend_forward",
    )(
        place,
        x_own,
        x_halo,
        gain,
        halves[0],
        others[0],
        halves[1],
        others[1],
        seg_rows,
        seg_lanes,
        bias,
    )


def fold_diagonals(block_sum):
    third = [block_sum[step * BLOCK : (step + 1) * BLOCK] for step in range(3)]
    cur = jnp.concatenate([third[2], third[1], third[0], jnp.zeros((BLOCK, BLOCK), F32)], axis=1)
    count = BLOCK // 2
    while count >= 1:
        cur = cur[count:] + pltpu.roll(cur[:count], count, 1)
        count //= 2
    return cur


def attend_back_kernel(
    pairs,
    last,
    own_blocks,
    shift_ref,
    qkv_ref,
    grad_ref,
    halo_ref,
    wo_ref,
    segr_ref,
    segl_ref,
    bias_ref,
    out_ref,
    diag_ref,
    heads_s,
    acc_ref,
    sum_ref,
):
    row, block = pl.program_id(0), pl.program_id(1)
    shift = shift_ref[0]
    blocks = key_blocks(block, last)
    mask = block_mask(segr_ref, segl_ref, block)
    owned = jnp.logical_and(block >= shift, block < shift + own_blocks)
    keep = jnp.where(owned, 1.0, 0.0)

    @pl.when(block == 0)
    def _():
        acc_ref[...] = jnp.zeros_like(acc_ref)
        own = pl.ds(pl.multiple_of(shift * BLOCK, BLOCK), own_blocks * BLOCK)
        heads_s[own, :] = grad_ref[0]
        other = place_of((1 - shift) * own_blocks)
        heads_s[other, :] = dot_nn(halo_ref[0], wo_ref[...]).astype(BF)

    @pl.when(jnp.logical_and(block == 0, row == 0))
    def _():
        sum_ref[...] = jnp.zeros_like(sum_ref)

    columns = [pair_columns(pair, pairs // 2) for pair in range(pairs)]
    here = place_of(block)
    queries = [stack_heads(qkv_ref[0, here, c[0] : c[0] + LANES]) for c in columns]
    grads = [stack_heads(heads_s[here, p * LANES : (p + 1) * LANES]) for p in range(pairs)]
    keys = [window_of(qkv_ref, blocks, c[1]) for c in columns]
    logits = [dot_nt(k, q) for k, q in zip(keys, queries)]
    grads_w = [dot_nt(window_of(qkv_ref, blocks, c[2]), g) for c, g in zip(columns, grads)]
    probs = [softmax_of(value + (bias_ref[p] + mask)) for p, value in enumerate(logits)]
    grads_v = [dot_nn(p.astype(BF), g) for p, g in zip(probs, grads)]
    grads_l = [
        (p * (g - jnp.sum(p * g, axis=0, keepdims=True))).astype(BF)
        for p, g in zip(probs, grads_w)
    ]
    grads_k = [dot_nn(g, q) for g, q in zip(grads_l, queries)]
    grads_q = [dot_tn(k, g) for k, g in zip(keys, grads_l)]
    for pair, (col_q, col_k, col_v) in enumerate(columns):
        sum_ref[pair] += grads_l[pair].astype(F32) * keep
        acc_ref[here, col_q : col_q + LANES] = unstack_heads(grads_q[pair])
        for part in range(3):
            piece = slice(part * BLOCK, (part + 1) * BLOCK)
            acc_ref[place_of(blocks[part]), col_k : col_k + LANES] += grads_k[pair][piece]
            acc_ref[place_of(blocks[part]), col_v : col_v + LANES] += grads_v[pair][piece]

    @pl.when(block == last)
    def _():
        start = pl.multiple_of(shift * BLOCK, BLOCK)
        out_ref[0] = acc_ref[pl.ds(start, own_blocks * BLOCK), :].astype(BF)

    @pl.when(jnp.logical_and(block == last, row == pl.num_programs(0) - 1))
    def _():
        def fold(pair, carry):
            diag_ref[2 * pair] = fold_diagonals(sum_ref[pair, :, :BLOCK])
            diag_ref[2 * pair + 1] = fold_diagonals(sum_ref[pair, :, BLOCK:])
            return carry

        lax.fori_loop(0, pairs, fold, 0)


def attend_backward(
    shift, qkv, grad_heads, grad_halo, out_weight, seg_rows, seg_lanes, bias
):
    rows, length, width = qkv.shape
    half, cols = grad_heads.shape[1:]
    model = grad_halo.shape[2]
    own_blocks = half // BLOCK
    pairs = bias.shape[0]
    last = length // BLOCK - 1
    steps = rows * (last + 1) * pairs
    once = pl.Buffered(1)
    cost = pl.CostEstimate(
        flops=steps * 120 * BLOCK * 3 * BLOCK * LANES + 2 * rows * BLOCK * model * cols,
        transcendentals=steps * 6 * BLOCK * BLOCK,
        bytes_accessed=qkv.size * 4 + grad_heads.size * 2 + bias.size * 4 + model * cols * 2,
    )
    return pl.pallas_call(
        functools.partial(attend_back_kernel, pairs, last, own_blocks),
        out_shape=(
            jax.ShapeDtypeStruct((rows, half, width), BF),
            jax.ShapeDtypeStruct((2 * pairs, 1, 4 * BLOCK), F32),
        ),
        grid_spec=pltpu.PrefetchScalarGridSpec(
            num_scalar_prefetch=1,
            grid=(rows, last + 1),
            in_specs=[
                pl.BlockSpec((1, length, width), lambda r, i, s: (r, 0, 0)),
                pl.BlockSpec((1, half, cols), lambda r, i, s: (r, 0, 0)),
                pl.BlockSpec((1, BLOCK, model), lambda r, i, s: (r, 0, 0)),
                pl.BlockSpec((model, cols), lambda r, i, s: (0, 0), pipeline_mode=once),
                pl.BlockSpec((1,) + seg_rows.shape[1:], lambda r, i, s: (r, 0, 0)),
                pl.BlockSpec((1,) + seg_lanes.shape[1:], lambda r, i, s: (r, 0, 0)),
                pl.BlockSpec(bias.shape, lambda r, i, s: (0, 0, 0), pipeline_mode=once),
            ],
            out_specs=[
                pl.BlockSpec((1, half, width), lambda r, i, s: (r, 0, 0)),
                pl.BlockSpec((2 * pairs, 1, 4 * BLOCK), lambda r, i, s: (0, 0, 0)),
            ],
            scratch_shapes=[
                pltpu.VMEM((length, pairs * LANES), BF),
                pltpu.VMEM((length, width), F32),
                pltpu.VMEM(bias.shape, F32),
            ],
        ),
        compiler_params=pltpu.CompilerParams(
            dimension_semantics=("arbitrary", "arbitrary"), vmem_limit_bytes=56 << 20
        ),
        cost_estimate=cost,
        name="attend_backward",
    )(shift, qkv, grad_heads, grad_halo, out_weight, seg_rows, seg_lanes, bias)


def input_kernel(grad_ref, wa_ref, wb_ref, x_ref, gain_ref, gmid_ref, out_ref):
    grad_n1 = None
    for ref, start, at, used in column_pieces(wa_ref, wb_ref):
        part = dot_nt(grad_ref[:, at : at + used], ref[:, start : start + used])
        grad_n1 = part if grad_n1 is None else grad_n1 + part
    x = x_ref[...].astype(F32)
    r1 = inverse_rms(x)
    scaled = grad_n1 * gain_ref[...]
    inner = jnp.mean(scaled * x, axis=-1, keepdims=True)
    out_ref[...] = gmid_ref[...] + r1 * scaled - x * (r1 * r1 * r1 * inner)


def input_gradient(grad_qkv, part_a, part_b, x_own, gain, grad_middle):
    tokens, width = grad_qkv.shape
    model = x_own.shape[1]
    chunk = min(256, tokens)
    once = pl.Buffered(1)
    here = lambda i: (i, 0)
    whole = lambda i: (0, 0)
    return pl.pallas_call(
        input_kernel,
        out_shape=jax.ShapeDtypeStruct((tokens, model), F32),
        grid=(tokens // chunk,),
        in_specs=[
            pl.BlockSpec((chunk, width), here),
            pl.BlockSpec(part_a.shape, whole, pipeline_mode=once),
            pl.BlockSpec(part_b.shape, whole, pipeline_mode=once),
            pl.BlockSpec((chunk, model), here),
            pl.BlockSpec((1, model), whole, pipeline_mode=once),
            pl.BlockSpec((chunk, model), here),
        ],
        out_specs=pl.BlockSpec((chunk, model), here),
        compiler_params=pltpu.CompilerParams(
            dimension_semantics=("arbitrary",), vmem_limit_bytes=40 << 20
        ),
        cost_estimate=pl.CostEstimate(
            flops=tokens * model, transcendentals=tokens, bytes_accessed=tokens
        ),
        name="input_gradient",
    )(grad_qkv, part_a, part_b, x_own, gain, grad_middle)


def bias_kernel(turned_ref, out_ref):
    for side in range(2):
        wide = jnp.broadcast_to(turned_ref[side], (3 * BLOCK, 4 * BLOCK))
        out = pltpu.roll(wide, BLOCK + 1, 1, stride=1, stride_axis=0)
        out_ref[0, :, side * BLOCK : (side + 1) * BLOCK] = out[:, :BLOCK]


def window_bias(turned):
    pairs = turned.shape[0] // 2
    return pl.pallas_call(
        bias_kernel,
        out_shape=jax.ShapeDtypeStruct((pairs, 3 * BLOCK, 2 * BLOCK), F32),
        grid=(pairs,),
        in_specs=[pl.BlockSpec((2, 1, 4 * BLOCK), lambda h: (h, 0, 0))],
        out_specs=pl.BlockSpec((1, 3 * BLOCK, 2 * BLOCK), lambda h: (h, 0, 0)),
        name="window_bias",
    )(turned[:, None, :])


def gelu_parts(gate):
    c, a = 0.7978845608028654, 0.044715
    square = gate * gate
    tanh = jnp.tanh(gate * (c + (c * a) * square))
    t = 0.5 + 0.5 * tanh
    slope = t + (0.5 * gate) * (1.0 - tanh * tanh) * (c + (3.0 * c * a) * square)
    return gate * t, slope


def split_rows(own_core, shard, grad, keep_ref, send_ref, where):
    for core in range(2):
        first, second = (keep_ref, send_ref) if core == 0 else (send_ref, keep_ref)

        @pl.when(own_core == core)
        def _():
            for group in range(grad.shape[0] // (2 * shard)):
                start = group * 2 * shard
                first[(0, group) + where] = grad[start : start + shard]
                second[(0, group) + where] = grad[start + shard : start + 2 * shard]


def feed_kernel(
    chunk,
    shard,
    core_ref,
    heads_ref,
    x_ref,
    gain_ref,
    cot_ref,
    wo0_ref,
    wo1_ref,
    wg_ref,
    wu_ref,
    wd_ref,
    out_ref,
    gmid_ref,
    gattn_ref,
    ggain_ref,
    keep_ref,
    send_ref,
    wo_ref,
    mid_s,
    n2_s,
    n2t_s,
    cott_s,
    hid_s,
    gg_s,
    gu_s,
    gn2_s,
):
    tokens, width = x_ref.shape
    step = pl.program_id(0) * pl.num_programs(1) + pl.program_id(1)
    final = pl.num_programs(0) * pl.num_programs(1) - 1
    half = heads_ref.shape[1] // 2

    def for_chunks(work):
        def one(index, carry):
            work(pl.ds(pl.multiple_of(index * chunk, chunk), chunk))
            return carry

        lax.fori_loop(0, tokens // chunk, one, 0)

    @pl.when(step == 0)
    def _():
        wo_ref[:, :half] = wo0_ref[...]
        wo_ref[:, half:] = wo1_ref[...]

        def work(place):
            middle = x_ref[place, :].astype(F32)
            middle = middle + dot_nt(heads_ref[place, :half], wo0_ref[...])
            middle = middle + dot_nt(heads_ref[place, half:], wo1_ref[...])
            mid_s[place, :] = middle
            out_ref[place, :] = middle
            normed = (middle * inverse_rms(middle) * gain_ref[...]).astype(BF)
            n2_s[place, :] = normed
            n2t_s[:, place] = normed.T
            cott_s[:, place] = cot_ref[place, :].T
            gn2_s[place, :] = jnp.zeros((chunk, width), F32)

        for_chunks(work)

    def work(place):
        n2, cot = n2_s[place, :], cot_ref[place, :]
        act, slope = gelu_parts(dot_nn(n2, wg_ref[...]))
        up = dot_nn(n2, wu_ref[...])
        grad_hidden = dot_nn(cot, wd_ref[...])
        hidden = (act * up).astype(BF)
        grad_gate = (grad_hidden * up * slope).astype(BF)
        grad_up = (grad_hidden * act).astype(BF)
        hid_s[place, :] = hidden
        gg_s[place, :] = grad_gate
        gu_s[place, :] = grad_up
        out_ref[place, :] += dot_nt(hidden, wd_ref[...])
        gn2_s[place, :] += dot_nt(grad_gate, wg_ref[...]) + dot_nt(grad_up, wu_ref[...])

    for_chunks(work)

    def store(kind, grad):
        split_rows(core_ref[0], shard, grad.astype(BF), keep_ref, send_ref, (kind,))

    store(0, dot_nn(n2t_s[...], gg_s[...]))
    store(1, dot_nn(n2t_s[...], gu_s[...]))
    store(2, dot_nn(cott_s[...], hid_s[...]))

    @pl.when(step == final)
    def _():
        ggain_ref[...] = jnp.zeros_like(ggain_ref)

        def work(place):
            middle, grad_n2 = mid_s[place, :], gn2_s[place, :]
            r2 = inverse_rms(middle)
            ggain_ref[...] += jnp.sum(grad_n2 * middle * r2, axis=0, keepdims=True)
            scaled = grad_n2 * gain_ref[...]
            inner = jnp.mean(scaled * middle, axis=-1, keepdims=True)
            grad = cot_ref[place, :].astype(F32) + r2 * scaled - middle * (r2 * r2 * r2 * inner)
            gmid_ref[place, :] = grad
            gattn_ref[place, :] = grad.astype(BF)

        for_chunks(work)


def feed_forward(core, heads_out, x_own, gain, cotangent, weights, hidden_cols, shard):
    tokens, width = x_own.shape
    wide = min(512, hidden_cols)
    steps = hidden_cols // wide
    out_cols = heads_out.shape[1] // 2
    out_at = 3 * hidden_cols // out_cols
    groups = width // (2 * shard)
    whole = lambda t, j, c: (0, 0)
    once = pl.Buffered(1)
    piece = jax.ShapeDtypeStruct((2, groups, 3, shard, hidden_cols), BF)
    piece_spec = pl.BlockSpec((1, groups, 3, shard, wide), lambda t, j, c: (t, 0, 0, 0, j))
    return pl.pallas_call(
        functools.partial(feed_kernel, min(FEED_CHUNK, tokens), shard),
        out_shape=(
            jax.ShapeDtypeStruct((tokens, width), F32),
            jax.ShapeDtypeStruct((tokens, width), F32),
            jax.ShapeDtypeStruct((tokens, width), BF),
            jax.ShapeDtypeStruct((1, width), F32),
            piece,
            piece,
            jax.ShapeDtypeStruct((width, 2 * out_cols), BF),
        ),
        grid_spec=pltpu.PrefetchScalarGridSpec(
            num_scalar_prefetch=1,
            grid=(2, steps),
            in_specs=[
                pl.BlockSpec((tokens, 2 * out_cols), whole, pipeline_mode=once),
                pl.BlockSpec((tokens, width), whole, pipeline_mode=once),
                pl.BlockSpec((1, width), whole, pipeline_mode=once),
                pl.BlockSpec((tokens, width), whole, pipeline_mode=once),
                pl.BlockSpec((width, out_cols), lambda t, j, c: (0, out_at), pipeline_mode=once),
                pl.BlockSpec((width, out_cols), lambda t, j, c: (1, out_at), pipeline_mode=once),
                pl.BlockSpec((width, wide), lambda t, j, c: (t, j)),
                pl.BlockSpec((width, wide), lambda t, j, c: (t, steps + j)),
                pl.BlockSpec((width, wide), lambda t, j, c: (t, 2 * steps + j)),
            ],
            out_specs=[
                pl.BlockSpec((tokens, width), whole, pipeline_mode=once),
                pl.BlockSpec((tokens, width), whole, pipeline_mode=once),
                pl.BlockSpec((tokens, width), whole, pipeline_mode=once),
                pl.BlockSpec((1, width), whole, pipeline_mode=once),
                piece_spec,
                piece_spec,
                pl.BlockSpec((width, 2 * out_cols), whole, pipeline_mode=once),
            ],
            scratch_shapes=[
                pltpu.VMEM((tokens, width), F32),
                pltpu.VMEM((tokens, width), BF),
                pltpu.VMEM((width, tokens), BF),
                pltpu.VMEM((width, tokens), BF),
                pltpu.VMEM((tokens, wide), BF),
                pltpu.VMEM((tokens, wide), BF),
                pltpu.VMEM((tokens, wide), BF),
                pltpu.VMEM((tokens, width), F32),
            ],
        ),
        compiler_params=pltpu.CompilerParams(
            dimension_semantics=("arbitrary", "arbitrary"), vmem_limit_bytes=56 << 20
        ),
        cost_estimate=pl.CostEstimate(
            flops=2 * tokens * width * (18 * hidden_cols + 2 * out_cols),
            transcendentals=2 * tokens * hidden_cols,
            bytes_accessed=weights.size * 2 + tokens * width * 16 + 12 * width * hidden_cols,
        ),
        name="feed_forward",
    )(core, heads_out, x_own, gain, cotangent, weights, weights, weights, weights, weights)


def split_rows_at(own_core, half, shard, grad, keep_ref, send_ref, columns):
    for core in range(2):
        first, second = (keep_ref, send_ref) if core == 0 else (send_ref, keep_ref)

        @pl.when(own_core == core)
        def _():
            for group in range(grad.shape[0] // (2 * shard)):
                start = group * 2 * shard
                first[half, group, :, columns] = grad[start : start + shard]
                second[half, group, :, columns] = grad[start + shard : start + 2 * shard]


def weight_kernel(
    shard,
    core_ref,
    n1_ref,
    gqkv_ref,
    gout_ref,
    wa_ref,
    wb_ref,
    gain_ref,
    ggain_ref,
    diag_ref,
    onehot_ref,
    keep_ref,
    send_ref,
    gain_s,
):
    model = n1_ref.shape[1]
    wide = gqkv_ref.shape[1] // 3
    half = pl.program_id(0)

    @pl.when(half == 0)
    def _():
        gain_s[...] = jnp.zeros_like(gain_s)

    wide_a, wide_b = wa_ref.shape[1] // 2, wb_ref.shape[1] // 2
    for index in range(4):
        columns = slice(index * wide, (index + 1) * wide)
        if index < 3:
            grad = dot_tn(n1_ref[...], gqkv_ref[:, columns])
            for at in range(index * wide, (index + 1) * wide, LANES):
                if at < wide_a:
                    weight = wa_ref[:, lanes_of(half * wide_a + at)]
                else:
                    weight = wb_ref[:, lanes_of(half * wide_b + at - wide_a)]
                here = at - index * wide
                gain_s[...] += weight.astype(F32) * grad[:, here : here + LANES]
        else:
            grad = gout_ref[...]
        split_rows_at(core_ref[0], half, shard, grad.astype(BF), keep_ref, send_ref, columns)

    @pl.when(half == 1)
    def _():
        ggain1 = jnp.sum(gain_s[...].T, axis=0, keepdims=True) / gain_ref[...]
        table = lax.dot_general(
            diag_ref[...],
            onehot_ref[...],
            (((1,), (1,)), ((), ())),
            precision=HIGHEST_PREC,
            preferred_element_type=F32,
        )
        rows = []
        for value in (ggain1, ggain_ref[...]):
            rows += [value[:, at : at + LANES] for at in range(0, model, LANES)]
        table = jnp.concatenate(
            [table, jnp.zeros((table.shape[0], LANES - table.shape[1]), F32)], axis=1
        )
        small = jnp.concatenate(rows + [table], axis=0).astype(BF)
        for ref in (keep_ref, send_ref):
            ref[:, :, :, 4 * wide :] = jnp.zeros(ref.shape[:3] + (ref.shape[3] - 4 * wide,), BF)
            for at in range(0, small.shape[0], shard):
                lines = small[at : at + shard]
                place = slice(4 * wide + at // shard * LANES, 4 * wide + (at // shard + 1) * LANES)
                for side in range(2):
                    for group in range(ref.shape[1]):
                        ref[side, group, : lines.shape[0], place] = lines


def weight_gradients(
    core, n1, grad_qkv, grad_out_w, part_a, part_b, gain, grad_gain2, diagonals, onehot, shard
):
    tokens, model = n1.shape
    wide = grad_out_w.shape[1] // 2
    groups = model // (2 * shard)
    whole = lambda t, c: (0, 0)
    half = lambda t, c: (0, t)
    once = pl.Buffered(1)
    lines = 2 * model // LANES + diagonals.shape[0]
    piece = jax.ShapeDtypeStruct((2, groups, shard, 4 * wide + pl.cdiv(lines, shard) * LANES), BF)
    piece_spec = pl.BlockSpec(piece.shape, lambda t, c: (0, 0, 0, 0), pipeline_mode=once)
    return pl.pallas_call(
        functools.partial(weight_kernel, shard),
        out_shape=(piece, piece),
        grid_spec=pltpu.PrefetchScalarGridSpec(
            num_scalar_prefetch=1,
            grid=(2,),
            in_specs=[
                pl.BlockSpec((tokens, model), whole, pipeline_mode=once),
                pl.BlockSpec((tokens, 3 * wide), half),
                pl.BlockSpec((model, wide), half),
                pl.BlockSpec(part_a.shape, whole, pipeline_mode=once),
                pl.BlockSpec(part_b.shape, whole, pipeline_mode=once),
                pl.BlockSpec(gain.shape, whole, pipeline_mode=once),
                pl.BlockSpec(grad_gain2.shape, whole, pipeline_mode=once),
                pl.BlockSpec(diagonals.shape, whole, pipeline_mode=once),
                pl.BlockSpec(onehot.shape, whole, pipeline_mode=once),
            ],
            out_specs=[piece_spec, piece_spec],
            scratch_shapes=[pltpu.VMEM((model, LANES), F32)],
        ),
        compiler_params=pltpu.CompilerParams(
            dimension_semantics=("arbitrary",), vmem_limit_bytes=40 << 20
        ),
        cost_estimate=pl.CostEstimate(
            flops=tokens * model,
            transcendentals=0,
            bytes_accessed=tokens,
        ),
        name="weight_gradients",
    )(
        core,
        n1,
        grad_qkv,
        grad_out_w,
        part_a,
        part_b,
        gain,
        grad_gain2,
        diagonals,
        onehot,
    )


def body(
    hidden_in,
    segment_ids,
    bucket_of,
    attn_gain,
    w_query,
    w_key,
    w_value,
    w_attn_out,
    bias_table,
    ffn_gain,
    w_gate,
    w_up,
    w_down,
    cotangent,
):
    micro, local_rows, half, width = hidden_in.shape
    rows = micro * local_rows
    seq = segment_ids.shape[2]
    shard = attn_gain.shape[0]
    dp_count = lax.axis_size("dp")
    tp_index = lax.axis_index("tp")
    left_side = tp_index == 0
    local_heads = bias_table.shape[1]
    buckets = bias_table.shape[0]
    head_cols = w_query.shape[1]
    hidden_cols = w_gate.shape[1]
    own_blocks = half // BLOCK
    length = half + BLOCK

    def halo_of(own):
        send = jnp.where(left_side, own[:, half - BLOCK :], own[:, :BLOCK])
        return swap(send, "tp", 0)

    gains = jnp.pad(jnp.stack([attn_gain, ffn_gain], axis=1), ((0, 0), (0, LANES - 2)))
    first_shard = jnp.concatenate([w_query, w_key, w_value, gains], axis=1)
    second_shard = jnp.concatenate([w_gate, w_up, w_down.T, w_attn_out.T], axis=1)
    cut = first_shard.shape[1] // (2 * LANES) * LANES
    second = lax.all_gather(second_shard, ("tp", "dp"), axis=0, tiled=True)
    x_own = hidden_in.reshape(rows, half, width)
    x_halo = halo_of(x_own)
    seg = segment_ids.reshape(rows, seq)
    seg_ext = lax.dynamic_slice_in_dim(seg, tp_index * (half - BLOCK), length, 1)
    seg_pad = jnp.pad(seg_ext, ((0, 0), (BLOCK, BLOCK)), constant_values=-1)
    seg_rows = jnp.broadcast_to(seg_pad[:, :, None], seg_pad.shape + (LANES,))
    seg_lanes = seg_pad.reshape(rows, length // BLOCK + 2, BLOCK)
    other_table = swap(bias_table, "tp", 0)
    table = jnp.where(
        left_side,
        jnp.concatenate([bias_table, other_table], axis=1),
        jnp.concatenate([other_table, bias_table], axis=1),
    )
    near = bucket_of[seq - 2 * BLOCK - 1 : seq + 2 * BLOCK - 1][::-1]
    onehot = (near[None, :] == jnp.arange(buckets, dtype=jnp.int32)[:, None]).astype(F32)
    per_offset = lax.dot_general(
        table, onehot, (((0,), (0,)), ((), ())), precision=HIGHEST_PREC, preferred_element_type=F32
    )
    bias = window_bias(per_offset)
    shift = tp_index.astype(jnp.int32)[None]
    core = (lax.axis_index("dp") & 1).astype(jnp.int32)[None]

    near_halves, (bias, x_halo) = gather_halves(first_shard, cut, (bias, x_halo))
    far_halves = [swap(value, *stage_groups()[2]) for value in near_halves]
    gain_at = near_halves[1].shape[-1] // 2 - LANES
    gain_rows = [h[1][..., gain_at : gain_at + 2] for h in (near_halves, far_halves)]
    own_first = core[0] == 0
    gain_rows = jnp.stack(
        [
            jnp.where(own_first, gain_rows[0], gain_rows[1]),
            jnp.where(own_first, gain_rows[1], gain_rows[0]),
        ],
        axis=1,
    )
    both_gains = gain_rows.reshape(width, 2).T.astype(F32)
    gain1, gain2 = both_gains[:1], both_gains[1:]

    heads_out, qkv, n1, part_a, part_b = attend_forward(
        jnp.concatenate([shift, core]),
        x_own,
        x_halo,
        gain1,
        near_halves,
        far_halves,
        seg_rows,
        seg_lanes,
        bias,
    )
    heads_flat = heads_out.reshape(rows * half, 2 * head_cols)

    cot_flat = cotangent.reshape(rows * half, width)
    block_out, grad_middle, grad_attn, grad_gain2, keep, send, out_weight = feed_forward(
        core,
        heads_flat,
        x_own.reshape(rows * half, width),
        gain2,
        cot_flat,
        second,
        hidden_cols,
        shard,
    )
    grad_attn_rows = grad_attn.reshape(rows, half, width)
    grad_halo = halo_of(grad_attn_rows)
    grad_out_w = dot_tn(grad_attn, heads_flat).astype(BF)
    grad_heads = dot_nn(grad_attn, out_weight).astype(BF).reshape(heads_out.shape)

    far, near, cores = stage_groups()
    far_groups = [far[max(i - 2, 0) : i] for i in range(len(far), 0, -2)]
    stages = [("tp", 0)] + dp_stages()[:-1]
    twice = len(near[0]) > 1

    def both_cores(keep, send, cuts):
        terms = [
            value.reshape((2,) * len(stages) + value.shape[2:])
            for value in (keep, swap_with(send, (cores,)))
        ]
        ends = cuts[1:] + [keep.shape[-1]]
        return [Scatter([Term(t, stages, c, e - c) for t in terms]) for c, e in zip(cuts, ends)]

    feed = both_cores(keep, send, [0])
    others, (grad_heads, grad_halo, grad_out_w) = start_sends(
        feed, [near[0]], (grad_heads, grad_halo, grad_out_w)
    )

    grad_qkv, diagonals = attend_backward(
        shift, qkv, grad_heads, grad_halo, out_weight, seg_rows, seg_lanes, bias
    )
    grad_qkv = grad_qkv.reshape(rows * half, grad_qkv.shape[-1])
    keep_w, send_w = weight_gradients(
        core,
        n1.reshape(rows * half, width),
        grad_qkv,
        grad_out_w,
        part_a,
        part_b,
        gain1,
        grad_gain2,
        diagonals[:, 0],
        onehot,
        shard,
    )
    keep_w, send_w = end_sends(feed, others, (keep_w, send_w))
    tail = both_cores(keep_w, send_w, [0, 2 * head_cols])
    late = list(far)
    waiting = []
    if late:
        waiting, (tail[0].terms[0].array,) = start_joint(
            feed, [late.pop()], (tail[0].terms[0].array,)
        )
    others, (grad_qkv,) = start_sends(tail, [order[:1] for order in near], (grad_qkv,))
    grad_in = input_gradient(
        grad_qkv, part_a, part_b, x_own.reshape(rows * half, width), gain1, grad_middle
    )
    if waiting:
        waiting, (grad_in,) = tie(waiting, (grad_in,))
        end_joint(feed, waiting)
    while late:
        waiting, (grad_in,) = start_joint(feed, [late.pop()], (grad_in,))
        if late:
            end_joint(feed, waiting)
    (grad_in,) = end_sends(tail, others, (grad_in,))
    if twice:
        others, _ = start_sends(tail, [order[1:] for order in near])
        end_sends(tail, others)
    for index, group in enumerate(far_groups):
        others, _ = start_joint(tail, group)
        if index == 0 and len(far) > 1:
            waiting, others = tie(waiting, others)
            end_joint(feed, waiting)
        end_joint(tail, others)
    feed_sums = jnp.concatenate([s.total() for s in feed], axis=-1)
    sums_a, sums_b = [s.total() for s in tail]

    small = sums_b[:, 2 * head_cols :]
    small = jnp.concatenate(
        [small[:, at : at + LANES] for at in range(0, small.shape[1], LANES)], axis=0
    )
    lines = width // LANES
    dp_start = lax.axis_index("dp") * shard
    sum_gain1 = lax.dynamic_slice_in_dim(small[:lines].reshape(-1), dp_start, shard)
    sum_gain2 = lax.dynamic_slice_in_dim(small[lines : 2 * lines].reshape(-1), dp_start, shard)
    sum_table = small[2 * lines : 2 * lines + 2 * local_heads, :buckets]
    sum_table = lax.dynamic_slice_in_dim(sum_table, tp_index * local_heads, local_heads, 0).T

    shape = (micro, local_rows, half, width)
    return (
        block_out.reshape(shape),
        grad_in.reshape(shape),
        sum_gain1,
        sums_a[:, :head_cols],
        sums_a[:, head_cols:],
        sums_b[:, :head_cols],
        sums_b[:, head_cols : 2 * head_cols].T,
        sum_table,
        sum_gain2,
        feed_sums[0],
        feed_sums[1],
        feed_sums[2].T,
    )


def solution(mesh):
    in_specs = (
        P(None, "dp", "tp", None),
        P(None, "dp", None),
        P(),
        P("dp"),
        P("dp", "tp"),
        P("dp", "tp"),
        P("dp", "tp"),
        P("tp", "dp"),
        P(None, "tp"),
        P("dp"),
        P("dp", "tp"),
        P("dp", "tp"),
        P("tp", "dp"),
        P(None, "dp", "tp", None),
    )
    out_specs = (
        P(None, "dp", "tp", None),
        P(None, "dp", "tp", None),
        P("dp"),
        P("dp", "tp"),
        P("dp", "tp"),
        P("dp", "tp"),
        P("tp", "dp"),
        P(None, "tp"),
        P("dp"),
        P("dp", "tp"),
        P("dp", "tp"),
        P("tp", "dp"),
    )
    return jax.shard_map(body, mesh=mesh, in_specs=in_specs, out_specs=out_specs, check_vma=False)
```

```python
import functools

import jax
import jax.numpy as jnp
from jax import lax
from jax.experimental import pallas as pl
from jax.experimental.pallas import tpu as pltpu
from jax.sharding import PartitionSpec as P

EPSILON = 1e-06
MASKED = -1000000000.0
HIGHEST_PREC = lax.Precision.HIGHEST
BLOCK = 128
LANES = 128
FEED_CHUNK = 1024
EDGE_CHUNK = 256
BF = jnp.bfloat16
F32 = jnp.float32


def log2_of(count):
    return count.bit_length() - 1


def swap(value, axis, bit):
    count = lax.axis_size(axis)
    return lax.ppermute(value, axis, [(i, i ^ (1 << bit)) for i in range(count)])


def swap_flat(value, axis, bit):
    return swap(value.reshape(-1, value.shape[-1]), axis, bit).reshape(value.shape)


def own_bit(axis, bit):
    return (lax.axis_index(axis) >> bit) & 1


def dp_stages():
    return [("dp", b) for b in range(log2_of(lax.axis_size("dp")) - 1, -1, -1)]


def stage_groups():
    stages = dp_stages()
    near = stages[-2:-1]
    return stages[:-2], (near + [("tp", 0)], [("tp", 0)] + near), stages[-1]


def merge(buf, have, stage):
    axis, bit = stage
    other = swap(buf, axis, bit)
    first = own_bit(axis, bit) == 0
    low, high = jnp.where(first, buf, other), jnp.where(first, other, buf)
    if axis == "tp":
        return jnp.concatenate([low, high], axis=-1), have
    where = sum(1 for s in have if s[1] > bit)
    return jnp.stack([low, high], axis=where), have + [stage]


def tie(values, others):
    both = lax.optimization_barrier((tuple(values), tuple(others)))
    return both[0], both[1]


def gather_halves(piece, cut, before_last):
    far, orders, _ = stage_groups()
    have = []
    for stage in far:
        piece, have = merge(piece, have, stage)
    halves = [(piece[..., :cut], have), (piece[..., cut:], have)]
    for step in range(len(orders[0])):
        done = merge(*halves[0], orders[0][step])
        if step == 0:
            (value, first), before_last = tie([halves[1][0], done[0]], before_last)
            halves[1], done = (value, halves[1][1]), (first, done[1])
        halves = [done, merge(*halves[1], orders[1][step])]
    shape = (-1, piece.shape[-2])
    return [h[0].reshape(shape + h[0].shape[-1:]) for h in halves], before_last


def flips(group):
    chosen = [()]
    for stage in reversed(group):
        chosen += [c + (stage,) for c in chosen]
    return chosen[1:]


def swap_with(value, flip):
    flat = value.reshape(-1, value.shape[-1])
    across = sum(1 << bit for axis, bit in flip if axis == "tp")
    along = sum(1 << bit for axis, bit in flip if axis == "dp")
    if not across:
        axes, pairs = "dp", [(i, i ^ along) for i in range(lax.axis_size("dp"))]
    elif not along:
        axes, pairs = "tp", [(i, i ^ across) for i in range(lax.axis_size("tp"))]
    else:
        count = lax.axis_size("tp")
        axes = ("dp", "tp")
        pairs = [
            (i * count + j, (i ^ along) * count + (j ^ across))
            for i in range(lax.axis_size("dp"))
            for j in range(count)
        ]
    return lax.ppermute(flat, axes, pairs).reshape(value.shape)


class Term:
    def __init__(self, array, stages, first=0, count=None):
        self.array, self.stages, self.first = array, list(stages), first
        self.count = array.shape[-1] if count is None else count

    def part(self, fixed, flip):
        starts, sizes, kept = [], [], []
        for stage in self.stages:
            if stage in fixed:
                starts.append(1 - own_bit(*stage) if stage in flip else own_bit(*stage))
                sizes.append(1)
            else:
                starts.append(0)
                sizes.append(2)
                kept.append(2)
        rest = self.array.shape[len(self.stages) : -1]
        starts += [0] * len(rest) + [self.first]
        sizes += list(rest) + [self.count]
        part = lax.dynamic_slice(self.array, starts, sizes)
        return part.reshape(tuple(kept) + rest + (self.count,))


class Scatter:
    def __init__(self, terms):
        self.terms, self.done = terms, []
        self.stages = list(terms[0].stages)

    def sends(self, group):
        self.done = self.done + list(group)
        self.stages = [s for s in self.stages if s not in group]
        return [
            sum(t.part(self.done, flip).astype(F32) for t in self.terms).astype(BF)
            for flip in flips(group)
        ]

    def add(self, array, first=0, count=None):
        self.terms.append(Term(array, self.stages, first, count))

    def total(self):
        return sum(t.part(self.done, ()).astype(F32) for t in self.terms)


def start_sends(scatters, groups, later=()):
    sends = [s.sends(group) for s, group in zip(scatters, groups)]
    count = len(sends[0])
    if later:
        flat, later = tie([x for part in sends for x in part], later)
        sends = [flat[i * count : (i + 1) * count] for i in range(len(scatters))]
    others = [
        [swap_with(x, flip) for x, flip in zip(part, flips(group))]
        for part, group in zip(sends, groups)
    ]
    return others, later


def end_sends(scatters, others, later=()):
    count = len(others[0])
    flat = [x for part in others for x in part]
    if later:
        flat, later = tie(flat, later)
    for index, scatter in enumerate(scatters):
        for other in flat[index * count : (index + 1) * count]:
            scatter.add(other)
    return later


def start_joint(scatters, group, later=()):
    sends = [jnp.concatenate(parts, axis=-1) for parts in zip(*[s.sends(group) for s in scatters])]
    if later:
        sends, later = tie(sends, later)
    return [swap_with(x, flip) for x, flip in zip(sends, flips(group))], later


def end_joint(scatters, others, later=()):
    if later:
        others, later = tie(others, later)
    for other in others:
        at = 0
        for scatter in scatters:
            count = scatter.terms[0].count
            scatter.add(other, at, count)
            at += count
    return later


def inverse_rms(values):
    return lax.rsqrt(jnp.mean(values * values, axis=-1, keepdims=True) + EPSILON)


def key_blocks(block, last):
    return jnp.maximum(block - 1, 0), block, jnp.minimum(block + 1, last)


def block_mask(seg_rows_ref, seg_lanes_ref, block):
    seg_k = seg_rows_ref[0, pl.ds(pl.multiple_of(block * BLOCK, BLOCK), 3 * BLOCK), :]
    seg_q = seg_lanes_ref[0, pl.ds(block + 1, 1), :]
    mask = jnp.where(seg_k == seg_q, 0.0, MASKED)
    return jnp.concatenate([mask, mask], axis=1)


def place_of(block):
    return pl.ds(pl.multiple_of(block * BLOCK, BLOCK), BLOCK)


def lanes_of(column):
    return pl.ds(pl.multiple_of(column, LANES), LANES)


def window_of(ref, blocks, column):
    return jnp.concatenate([ref[0, place_of(b), lanes_of(column)] for b in blocks], axis=0)


def stack_heads(value):
    first = lax.broadcasted_iota(jnp.int32, value.shape, 1) < LANES // 2
    zero = jnp.zeros_like(value)
    return jnp.concatenate([jnp.where(first, value, zero), jnp.where(first, zero, value)], axis=0)


def unstack_heads(value):
    first = lax.broadcasted_iota(jnp.int32, (LANES, BLOCK), 0) < LANES // 2
    return jnp.where(first, value[:, :BLOCK], value[:, BLOCK:]).T


def dot_nt(left, right):
    return lax.dot_general(left, right, (((1,), (1,)), ((), ())), preferred_element_type=F32)


def dot_nn(left, right):
    return lax.dot_general(left, right, (((1,), (0,)), ((), ())), preferred_element_type=F32)


def dot_tn(left, right):
    return lax.dot_general(left, right, (((0,), (0,)), ((), ())), preferred_element_type=F32)


def pair_columns(pair, half_pairs):
    half, local = divmod(pair, half_pairs)
    width = half_pairs * LANES
    base = half * 3 * width + local * LANES
    return base, base + width, base + 2 * width


def softmax_of(logits):
    top = jnp.max(logits, axis=0, keepdims=True)
    powers = jnp.exp(logits - top)
    return powers * (1.0 / jnp.sum(powers, axis=0, keepdims=True))


def column_pieces(part_a, part_b):
    wide_a, wide_b = part_a.shape[1] // 2, part_b.shape[1] // 2
    at, pieces = 0, []
    for half in range(2):
        for ref, wide, used in ((part_a, wide_a, wide_a), (part_b, wide_b, wide_b - LANES)):
            pieces.append((ref, half * wide, at, used))
            at += used
    return pieces


def attend_kernel(
    pairs,
    last,
    shift_ref,
    x_ref,
    halo_ref,
    gain_ref,
    a_own_ref,
    a_other_ref,
    b_own_ref,
    b_other_ref,
    segr_ref,
    segl_ref,
    bias_ref,
    out_ref,
    qkv_ref,
    n1_ref,
    wa_ref,
    wb_ref,
    n1_s,
):
    own_blocks = pl.num_programs(1)
    shift = shift_ref[0]
    length = n1_s.shape[0]

    @pl.when(jnp.logical_and(pl.program_id(0) == 0, pl.program_id(1) == 0))
    def _():
        groups, shard = a_own_ref.shape[:2]
        for whole, own, other in (
            (wa_ref, a_own_ref, a_other_ref),
            (wb_ref, b_own_ref, b_other_ref),
        ):
            for core in range(2):

                @pl.when(shift_ref[1] == core)
                def _():
                    for group in range(groups):
                        for side, ref in ((core, own), (1 - core, other)):
                            start = (2 * group + side) * shard
                            whole[start : start + shard, :] = ref[group]

    @pl.when(pl.program_id(1) == 0)
    def _():
        def normed(value):
            value = value.astype(F32)
            return (value * inverse_rms(value) * gain_ref[...]).astype(BF)

        def own(index, carry):
            value = normed(x_ref[0, place_of(index), :])
            n1_ref[0, :, place_of(index)] = value.T
            n1_s[place_of(index + shift), :] = value
            return carry

        lax.fori_loop(0, own_blocks, own, 0)
        n1_s[place_of((1 - shift) * own_blocks), :] = normed(halo_ref[0])
        chunk = length // 2

        def project(index, carry):
            place = pl.ds(pl.multiple_of(index * chunk, chunk), chunk)
            for ref, start, at, used in column_pieces(wa_ref, wb_ref):
                part = dot_nn(n1_s[place, :], ref[:, start : start + used])
                qkv_ref[0, place, at : at + used] = part.astype(BF)
            return carry

        lax.fori_loop(0, 2, project, 0)

    block = pl.program_id(1) + shift
    blocks = key_blocks(block, last)
    mask = block_mask(segr_ref, segl_ref, block)
    columns = [pair_columns(pair, pairs // 2) for pair in range(pairs)]
    logits = [
        dot_nt(
            window_of(qkv_ref, blocks, col_k),
            stack_heads(qkv_ref[0, place_of(block), col_q : col_q + LANES]),
        )
        for col_q, col_k, _ in columns
    ]
    weights = [
        softmax_of(value + (bias_ref[pair] + mask)).astype(BF) for pair, value in enumerate(logits)
    ]
    mixed = [
        dot_tn(window_of(qkv_ref, blocks, col_v), value)
        for (_, _, col_v), value in zip(columns, weights)
    ]
    for pair, value in enumerate(mixed):
        out_ref[0, :, pair * LANES : (pair + 1) * LANES] = unstack_heads(value).astype(BF)


def attend_forward(place, x_own, x_halo, gain, halves, others, seg_rows, seg_lanes, bias):
    rows, half, model = x_own.shape
    own_blocks = half // BLOCK
    length = half + BLOCK
    pairs = bias.shape[0]
    last = length // BLOCK - 1
    widths = [h.shape[-1] for h in halves]
    width = sum(widths) - 2 * LANES
    steps = rows * own_blocks * pairs
    once = pl.Buffered(1)
    cost = pl.CostEstimate(
        flops=steps * 8 * BLOCK * 3 * BLOCK * LANES + 2 * rows * length * model * width,
        transcendentals=steps * 6 * BLOCK * BLOCK,
        bytes_accessed=rows * length * (width + 2 * model) * 2 + bias.size * 4 + model * width * 2,
    )
    return pl.pallas_call(
        functools.partial(attend_kernel, pairs, last),
        out_shape=(
            jax.ShapeDtypeStruct((rows, half, pairs * LANES), BF),
            jax.ShapeDtypeStruct((rows, length, width), BF),
            jax.ShapeDtypeStruct((rows, model, half), BF),
            jax.ShapeDtypeStruct((model, widths[0]), BF),
            jax.ShapeDtypeStruct((model, widths[1]), BF),
        ),
        grid_spec=pltpu.PrefetchScalarGridSpec(
            num_scalar_prefetch=1,
            grid=(rows, own_blocks),
            in_specs=[
                pl.BlockSpec((1, half, model), lambda r, i, s: (r, 0, 0)),
                pl.BlockSpec((1, BLOCK, model), lambda r, i, s: (r, 0, 0)),
                pl.BlockSpec((1, model), lambda r, i, s: (0, 0), pipeline_mode=once),
                pl.BlockSpec(halves[0].shape, lambda r, i, s: (0, 0, 0), pipeline_mode=once),
                pl.BlockSpec(others[0].shape, lambda r, i, s: (0, 0, 0), pipeline_mode=once),
                pl.BlockSpec(halves[1].shape, lambda r, i, s: (0, 0, 0), pipeline_mode=once),
                pl.BlockSpec(others[1].shape, lambda r, i, s: (0, 0, 0), pipeline_mode=once),
                pl.BlockSpec((1,) + seg_rows.shape[1:], lambda r, i, s: (r, 0, 0)),
                pl.BlockSpec((1,) + seg_lanes.shape[1:], lambda r, i, s: (r, 0, 0)),
                pl.BlockSpec(bias.shape, lambda r, i, s: (0, 0, 0), pipeline_mode=once),
            ],
            out_specs=[
                pl.BlockSpec((1, BLOCK, pairs * LANES), lambda r, i, s: (r, i, 0)),
                pl.BlockSpec((1, length, width), lambda r, i, s: (r, 0, 0)),
                pl.BlockSpec((1, model, half), lambda r, i, s: (r, 0, 0)),
                pl.BlockSpec((model, widths[0]), lambda r, i, s: (0, 0), pipeline_mode=once),
                pl.BlockSpec((model, widths[1]), lambda r, i, s: (0, 0), pipeline_mode=once),
            ],
            scratch_shapes=[pltpu.VMEM((length, model), BF)],
        ),
        compiler_params=pltpu.CompilerParams(
            dimension_semantics=("arbitrary", "arbitrary"), vmem_limit_bytes=48 << 20
        ),
        cost_estimate=cost,
        name="attend_forward",
    )(
        place,
        x_own,
        x_halo,
        gain,
        halves[0],
        others[0],
        halves[1],
        others[1],
        seg_rows,
        seg_lanes,
        bias,
    )


def fold_diagonals(block_sum):
    third = [block_sum[step * BLOCK : (step + 1) * BLOCK] for step in range(3)]
    cur = jnp.concatenate([third[2], third[1], third[0], jnp.zeros((BLOCK, BLOCK), F32)], axis=1)
    count = BLOCK // 2
    while count >= 1:
        cur = cur[count:] + pltpu.roll(cur[:count], count, 1)
        count //= 2
    return cur


def attend_back_kernel(
    pairs,
    last,
    own_blocks,
    shift_ref,
    qkv_ref,
    grad_ref,
    halo_ref,
    wo_ref,
    segr_ref,
    segl_ref,
    bias_ref,
    out_ref,
    diag_ref,
    heads_s,
    acc_ref,
    sum_ref,
):
    row, block = pl.program_id(0), pl.program_id(1)
    shift = shift_ref[0]
    blocks = key_blocks(block, last)
    mask = block_mask(segr_ref, segl_ref, block)
    owned = jnp.logical_and(block >= shift, block < shift + own_blocks)
    keep = jnp.where(owned, 1.0, 0.0)

    @pl.when(block == 0)
    def _():
        acc_ref[...] = jnp.zeros_like(acc_ref)
        own = pl.ds(pl.multiple_of(shift * BLOCK, BLOCK), own_blocks * BLOCK)
        heads_s[own, :] = grad_ref[0]
        other = place_of((1 - shift) * own_blocks)
        heads_s[other, :] = dot_nn(halo_ref[0], wo_ref[...]).astype(BF)

    @pl.when(jnp.logical_and(block == 0, row == 0))
    def _():
        sum_ref[...] = jnp.zeros_like(sum_ref)

    columns = [pair_columns(pair, pairs // 2) for pair in range(pairs)]
    here = place_of(block)
    queries = [stack_heads(qkv_ref[0, here, c[0] : c[0] + LANES]) for c in columns]
    grads = [stack_heads(heads_s[here, p * LANES : (p + 1) * LANES]) for p in range(pairs)]
    keys = [window_of(qkv_ref, blocks, c[1]) for c in columns]
    logits = [dot_nt(k, q) for k, q in zip(keys, queries)]
    grads_w = [dot_nt(window_of(qkv_ref, blocks, c[2]), g) for c, g in zip(columns, grads)]
    probs = [softmax_of(value + (bias_ref[p] + mask)) for p, value in enumerate(logits)]
    grads_v = [dot_nn(p.astype(BF), g) for p, g in zip(probs, grads)]
    grads_l = [
        (p * (g - jnp.sum(p * g, axis=0, keepdims=True))).astype(BF)
        for p, g in zip(probs, grads_w)
    ]
    grads_k = [dot_nn(g, q) for g, q in zip(grads_l, queries)]
    grads_q = [dot_tn(k, g) for k, g in zip(keys, grads_l)]
    for pair, (col_q, col_k, col_v) in enumerate(columns):
        sum_ref[pair] += grads_l[pair].astype(F32) * keep
        acc_ref[here, col_q : col_q + LANES] = unstack_heads(grads_q[pair])
        for part in range(3):
            piece = slice(part * BLOCK, (part + 1) * BLOCK)
            acc_ref[place_of(blocks[part]), col_k : col_k + LANES] += grads_k[pair][piece]
            acc_ref[place_of(blocks[part]), col_v : col_v + LANES] += grads_v[pair][piece]

    @pl.when(block == last)
    def _():
        start = pl.multiple_of(shift * BLOCK, BLOCK)
        out_ref[0] = acc_ref[pl.ds(start, own_blocks * BLOCK), :].astype(BF)

    @pl.when(jnp.logical_and(block == last, row == pl.num_programs(0) - 1))
    def _():
        def fold(pair, carry):
            diag_ref[2 * pair] = fold_diagonals(sum_ref[pair, :, :BLOCK])
            diag_ref[2 * pair + 1] = fold_diagonals(sum_ref[pair, :, BLOCK:])
            return carry

        lax.fori_loop(0, pairs, fold, 0)


def attend_backward(
    shift, qkv, grad_heads, grad_halo, out_weight, seg_rows, seg_lanes, bias
):
    rows, length, width = qkv.shape
    half, cols = grad_heads.shape[1:]
    model = grad_halo.shape[2]
    own_blocks = half // BLOCK
    pairs = bias.shape[0]
    last = length // BLOCK - 1
    steps = rows * (last + 1) * pairs
    once = pl.Buffered(1)
    cost = pl.CostEstimate(
        flops=steps * 120 * BLOCK * 3 * BLOCK * LANES + 2 * rows * BLOCK * model * cols,
        transcendentals=steps * 6 * BLOCK * BLOCK,
        bytes_accessed=qkv.size * 4 + grad_heads.size * 2 + bias.size * 4 + model * cols * 2,
    )
    return pl.pallas_call(
        functools.partial(attend_back_kernel, pairs, last, own_blocks),
        out_shape=(
            pltpu.HBM((rows, half, width), BF),
            jax.ShapeDtypeStruct((2 * pairs, 1, 4 * BLOCK), F32),
        ),
        grid_spec=pltpu.PrefetchScalarGridSpec(
            num_scalar_prefetch=1,
            grid=(rows, last + 1),
            in_specs=[
                pl.BlockSpec((1, length, width), lambda r, i, s: (r, 0, 0)),
                pl.BlockSpec((1, half, cols), lambda r, i, s: (r, 0, 0)),
                pl.BlockSpec((1, BLOCK, model), lambda r, i, s: (r, 0, 0)),
                pl.BlockSpec((model, cols), lambda r, i, s: (0, 0), pipeline_mode=once),
                pl.BlockSpec((1,) + seg_rows.shape[1:], lambda r, i, s: (r, 0, 0)),
                pl.BlockSpec((1,) + seg_lanes.shape[1:], lambda r, i, s: (r, 0, 0)),
                pl.BlockSpec(bias.shape, lambda r, i, s: (0, 0, 0), pipeline_mode=once),
            ],
            out_specs=[
                pl.BlockSpec((1, half, width), lambda r, i, s: (r, 0, 0)),
                pl.BlockSpec((2 * pairs, 1, 4 * BLOCK), lambda r, i, s: (0, 0, 0)),
            ],
            scratch_shapes=[
                pltpu.VMEM((length, pairs * LANES), BF),
                pltpu.VMEM((length, width), F32),
                pltpu.VMEM(bias.shape, F32),
            ],
        ),
        compiler_params=pltpu.CompilerParams(
            dimension_semantics=("arbitrary", "arbitrary"), vmem_limit_bytes=38 << 20
        ),
        cost_estimate=cost,
        name="attend_backward",
    )(shift, qkv, grad_heads, grad_halo, out_weight, seg_rows, seg_lanes, bias)


def input_kernel(grad_ref, wa_ref, wb_ref, x_ref, gain_ref, gmid_ref, out_ref):
    grad_n1 = None
    for ref, start, at, used in column_pieces(wa_ref, wb_ref):
        part = dot_nt(grad_ref[:, at : at + used], ref[:, start : start + used])
        grad_n1 = part if grad_n1 is None else grad_n1 + part
    x = x_ref[...].astype(F32)
    r1 = inverse_rms(x)
    scaled = grad_n1 * gain_ref[...]
    inner = jnp.mean(scaled * x, axis=-1, keepdims=True)
    out_ref[...] = gmid_ref[...] + r1 * scaled - x * (r1 * r1 * r1 * inner)


def input_gradient(grad_qkv, part_a, part_b, x_own, gain, grad_middle):
    tokens, width = grad_qkv.shape
    model = x_own.shape[1]
    chunk = min(256, tokens)
    once = pl.Buffered(1)
    here = lambda i: (i, 0)
    whole = lambda i: (0, 0)
    return pl.pallas_call(
        input_kernel,
        out_shape=jax.ShapeDtypeStruct((tokens, model), F32),
        grid=(tokens // chunk,),
        in_specs=[
            pl.BlockSpec((chunk, width), here),
            pl.BlockSpec(part_a.shape, whole, pipeline_mode=once),
            pl.BlockSpec(part_b.shape, whole, pipeline_mode=once),
            pl.BlockSpec((chunk, model), here),
            pl.BlockSpec((1, model), whole, pipeline_mode=once),
            pl.BlockSpec((chunk, model), here),
        ],
        out_specs=pl.BlockSpec((chunk, model), here),
        compiler_params=pltpu.CompilerParams(
            dimension_semantics=("arbitrary",), vmem_limit_bytes=60 << 20
        ),
        cost_estimate=pl.CostEstimate(
            flops=tokens * model, transcendentals=tokens, bytes_accessed=tokens
        ),
        name="input_gradient",
    )(grad_qkv, part_a, part_b, x_own, gain, grad_middle)


def bias_kernel(turned_ref, out_ref):
    for side in range(2):
        wide = jnp.broadcast_to(turned_ref[side], (3 * BLOCK, 4 * BLOCK))
        out = pltpu.roll(wide, BLOCK + 1, 1, stride=1, stride_axis=0)
        out_ref[0, :, side * BLOCK : (side + 1) * BLOCK] = out[:, :BLOCK]


def window_bias(turned):
    pairs = turned.shape[0] // 2
    return pl.pallas_call(
        bias_kernel,
        out_shape=jax.ShapeDtypeStruct((pairs, 3 * BLOCK, 2 * BLOCK), F32),
        grid=(pairs,),
        in_specs=[pl.BlockSpec((2, 1, 4 * BLOCK), lambda h: (h, 0, 0))],
        out_specs=pl.BlockSpec((1, 3 * BLOCK, 2 * BLOCK), lambda h: (h, 0, 0)),
        name="window_bias",
    )(turned[:, None, :])


def gelu_parts(gate):
    c, a = 0.7978845608028654, 0.044715
    square = gate * gate
    tanh = jnp.tanh(gate * (c + (c * a) * square))
    t = 0.5 + 0.5 * tanh
    slope = t + (0.5 * gate) * (1.0 - tanh * tanh) * (c + (3.0 * c * a) * square)
    return gate * t, slope


def split_rows(own_core, shard, grad, keep_ref, send_ref, where):
    for core in range(2):
        first, second = (keep_ref, send_ref) if core == 0 else (send_ref, keep_ref)

        @pl.when(own_core == core)
        def _():
            for group in range(grad.shape[0] // (2 * shard)):
                start = group * 2 * shard
                first[(0, group) + where] = grad[start : start + shard]
                second[(0, group) + where] = grad[start + shard : start + 2 * shard]


def feed_kernel(
    chunk,
    shard,
    core_ref,
    heads_ref,
    x_ref,
    gain_ref,
    cot_ref,
    wo0_ref,
    wo1_ref,
    wg_ref,
    wu_ref,
    wd_ref,
    out_ref,
    gmid_ref,
    gattn_ref,
    ggain_ref,
    keep_ref,
    send_ref,
    wo_ref,
    mid_s,
    n2_s,
    n2t_s,
    cott_s,
    hid_s,
    gg_s,
    gu_s,
    gn2_s,
):
    tokens, width = x_ref.shape
    step = pl.program_id(0) * pl.num_programs(1) + pl.program_id(1)
    final = pl.num_programs(0) * pl.num_programs(1) - 1
    half = heads_ref.shape[1] // 2

    def for_chunks(work, count):
        def one(index, carry):
            work(pl.ds(pl.multiple_of(index * count, count), count))
            return carry

        lax.fori_loop(0, tokens // count, one, 0)

    edge = min(EDGE_CHUNK, tokens)

    @pl.when(step == 0)
    def _():
        wo_ref[:, :half] = wo0_ref[...]
        wo_ref[:, half:] = wo1_ref[...]

        def work(place):
            middle = x_ref[place, :].astype(F32)
            middle = middle + dot_nt(heads_ref[place, :half], wo0_ref[...])
            middle = middle + dot_nt(heads_ref[place, half:], wo1_ref[...])
            mid_s[place, :] = middle
            out_ref[place, :] = middle
            normed = (middle * inverse_rms(middle) * gain_ref[...]).astype(BF)
            n2_s[place, :] = normed
            n2t_s[:, place] = normed.T
            cott_s[:, place] = cot_ref[place, :].T
            gn2_s[place, :] = jnp.zeros((edge, width), F32)

        for_chunks(work, edge)

    def work(place):
        n2, cot = n2_s[place, :], cot_ref[place, :]
        act, slope = gelu_parts(dot_nn(n2, wg_ref[...]))
        up = dot_nn(n2, wu_ref[...])
        grad_hidden = dot_nn(cot, wd_ref[...])
        hidden = (act * up).astype(BF)
        grad_gate = (grad_hidden * up * slope).astype(BF)
        grad_up = (grad_hidden * act).astype(BF)
        hid_s[place, :] = hidden
        gg_s[place, :] = grad_gate
        gu_s[place, :] = grad_up
        out_ref[place, :] += dot_nt(hidden, wd_ref[...])
        gn2_s[place, :] += dot_nt(grad_gate, wg_ref[...]) + dot_nt(grad_up, wu_ref[...])

    for_chunks(work, chunk)

    def store(kind, grad):
        split_rows(core_ref[0], shard, grad.astype(BF), keep_ref, send_ref, (kind,))

    store(0, dot_nn(n2t_s[...], gg_s[...]))
    store(1, dot_nn(n2t_s[...], gu_s[...]))
    store(2, dot_nn(cott_s[...], hid_s[...]))

    @pl.when(step == final)
    def _():
        ggain_ref[...] = jnp.zeros_like(ggain_ref)

        def work(place):
            middle, grad_n2 = mid_s[place, :], gn2_s[place, :]
            r2 = inverse_rms(middle)
            ggain_ref[...] += jnp.sum(grad_n2 * middle * r2, axis=0, keepdims=True)
            scaled = grad_n2 * gain_ref[...]
            inner = jnp.mean(scaled * middle, axis=-1, keepdims=True)
            grad = cot_ref[place, :].astype(F32) + r2 * scaled - middle * (r2 * r2 * r2 * inner)
            gmid_ref[place, :] = grad
            gattn_ref[place, :] = grad.astype(BF)

        for_chunks(work, edge)


def feed_forward(core, heads_out, x_own, gain, cotangent, weights, hidden_cols, shard):
    tokens, width = x_own.shape
    wide = min(512, hidden_cols)
    steps = hidden_cols // wide
    out_cols = heads_out.shape[1] // 2
    out_at = 3 * hidden_cols // out_cols
    groups = width // (2 * shard)
    whole = lambda t, j, c: (0, 0)
    once = pl.Buffered(1)
    piece = jax.ShapeDtypeStruct((2, groups, 3, shard, hidden_cols), BF)
    piece_spec = pl.BlockSpec((1, groups, 3, shard, wide), lambda t, j, c: (t, 0, 0, 0, j))
    return pl.pallas_call(
        functools.partial(feed_kernel, min(FEED_CHUNK, tokens), shard),
        out_shape=(
            jax.ShapeDtypeStruct((tokens, width), F32),
            jax.ShapeDtypeStruct((tokens, width), F32),
            jax.ShapeDtypeStruct((tokens, width), BF),
            jax.ShapeDtypeStruct((1, width), F32),
            piece,
            piece,
            jax.ShapeDtypeStruct((width, 2 * out_cols), BF),
        ),
        grid_spec=pltpu.PrefetchScalarGridSpec(
            num_scalar_prefetch=1,
            grid=(2, steps),
            in_specs=[
                pl.BlockSpec((tokens, 2 * out_cols), whole, pipeline_mode=once),
                pl.BlockSpec((tokens, width), whole, pipeline_mode=once),
                pl.BlockSpec((1, width), whole, pipeline_mode=once),
                pl.BlockSpec((tokens, width), whole, pipeline_mode=once),
                pl.BlockSpec((width, out_cols), lambda t, j, c: (0, out_at), pipeline_mode=once),
                pl.BlockSpec((width, out_cols), lambda t, j, c: (1, out_at), pipeline_mode=once),
                pl.BlockSpec((width, wide), lambda t, j, c: (t, j)),
                pl.BlockSpec((width, wide), lambda t, j, c: (t, steps + j)),
                pl.BlockSpec((width, wide), lambda t, j, c: (t, 2 * steps + j)),
            ],
            out_specs=[
                pl.BlockSpec((tokens, width), whole, pipeline_mode=once),
                pl.BlockSpec((tokens, width), whole, pipeline_mode=once),
                pl.BlockSpec((tokens, width), whole, pipeline_mode=once),
                pl.BlockSpec((1, width), whole, pipeline_mode=once),
                piece_spec,
                piece_spec,
                pl.BlockSpec((width, 2 * out_cols), whole, pipeline_mode=once),
            ],
            scratch_shapes=[
                pltpu.VMEM((tokens, width), F32),
                pltpu.VMEM((tokens, width), BF),
                pltpu.VMEM((width, tokens), BF),
                pltpu.VMEM((width, tokens), BF),
                pltpu.VMEM((tokens, wide), BF),
                pltpu.VMEM((tokens, wide), BF),
                pltpu.VMEM((tokens, wide), BF),
                pltpu.VMEM((tokens, width), F32),
            ],
        ),
        compiler_params=pltpu.CompilerParams(
            dimension_semantics=("arbitrary", "arbitrary"), vmem_limit_bytes=56 << 20
        ),
        cost_estimate=pl.CostEstimate(
            flops=2 * tokens * width * (18 * hidden_cols + 2 * out_cols),
            transcendentals=2 * tokens * hidden_cols,
            bytes_accessed=weights.size * 2 + tokens * width * 16 + 12 * width * hidden_cols,
        ),
        name="feed_forward",
    )(core, heads_out, x_own, gain, cotangent, weights, weights, weights, weights, weights)


def split_rows_at(own_core, half, shard, grad, keep_ref, send_ref, columns):
    for core in range(2):
        first, second = (keep_ref, send_ref) if core == 0 else (send_ref, keep_ref)

        @pl.when(own_core == core)
        def _():
            for group in range(grad.shape[0] // (2 * shard)):
                start = group * 2 * shard
                first[half, group, :, columns] = grad[start : start + shard]
                second[half, group, :, columns] = grad[start + shard : start + 2 * shard]


def weight_kernel(
    shard,
    core_ref,
    n1_ref,
    gqkv_ref,
    gout_ref,
    wa_ref,
    wb_ref,
    gain_ref,
    ggain_ref,
    diag_ref,
    onehot_ref,
    keep_ref,
    send_ref,
    gain_s,
):
    rows, model, length = n1_ref.shape
    wide = gqkv_ref.shape[1] // 3
    half = pl.program_id(0)

    @pl.when(half == 0)
    def _():
        gain_s[...] = jnp.zeros_like(gain_s)

    wide_a, wide_b = wa_ref.shape[1] // 2, wb_ref.shape[1] // 2
    for index in range(4):
        columns = slice(index * wide, (index + 1) * wide)
        if index < 3:
            grad = sum(
                dot_nn(n1_ref[row], gqkv_ref[row * length : (row + 1) * length, columns])
                for row in range(rows)
            )
            for at in range(index * wide, (index + 1) * wide, LANES):
                if at < wide_a:
                    weight = wa_ref[:, lanes_of(half * wide_a + at)]
                else:
                    weight = wb_ref[:, lanes_of(half * wide_b + at - wide_a)]
                here = at - index * wide
                gain_s[...] += weight.astype(F32) * grad[:, here : here + LANES]
        else:
            grad = gout_ref[...]
        split_rows_at(core_ref[0], half, shard, grad.astype(BF), keep_ref, send_ref, columns)

    @pl.when(half == 1)
    def _():
        ggain1 = jnp.sum(gain_s[...].T, axis=0, keepdims=True) / gain_ref[...]
        table = lax.dot_general(
            diag_ref[...],
            onehot_ref[...],
            (((1,), (1,)), ((), ())),
            precision=HIGHEST_PREC,
            preferred_element_type=F32,
        )
        rows = []
        for value in (ggain1, ggain_ref[...]):
            rows += [value[:, at : at + LANES] for at in range(0, model, LANES)]
        table = jnp.concatenate(
            [table, jnp.zeros((table.shape[0], LANES - table.shape[1]), F32)], axis=1
        )
        small = jnp.concatenate(rows + [table], axis=0).astype(BF)
        for ref in (keep_ref, send_ref):
            ref[:, :, :, 4 * wide :] = jnp.zeros(ref.shape[:3] + (ref.shape[3] - 4 * wide,), BF)
            for at in range(0, small.shape[0], shard):
                lines = small[at : at + shard]
                place = slice(4 * wide + at // shard * LANES, 4 * wide + (at // shard + 1) * LANES)
                for side in range(2):
                    for group in range(ref.shape[1]):
                        ref[side, group, : lines.shape[0], place] = lines


def weight_gradients(
    core, n1, grad_qkv, grad_out_w, part_a, part_b, gain, grad_gain2, diagonals, onehot, shard
):
    rows, model, length = n1.shape
    tokens = rows * length
    wide = grad_out_w.shape[1] // 2
    groups = model // (2 * shard)
    whole = lambda t, c: (0, 0)
    half = lambda t, c: (0, t)
    once = pl.Buffered(1)
    lines = 2 * model // LANES + diagonals.shape[0]
    piece = pltpu.HBM((2, groups, shard, 4 * wide + pl.cdiv(lines, shard) * LANES), BF)
    piece_spec = pl.BlockSpec(piece.shape, lambda t, c: (0, 0, 0, 0), pipeline_mode=once)
    return pl.pallas_call(
        functools.partial(weight_kernel, shard),
        out_shape=(piece, piece),
        grid_spec=pltpu.PrefetchScalarGridSpec(
            num_scalar_prefetch=1,
            grid=(2,),
            in_specs=[
                pl.BlockSpec(n1.shape, lambda t, c: (0, 0, 0), pipeline_mode=once),
                pl.BlockSpec((tokens, 3 * wide), half),
                pl.BlockSpec((model, wide), half),
                pl.BlockSpec(part_a.shape, whole, pipeline_mode=once),
                pl.BlockSpec(part_b.shape, whole, pipeline_mode=once),
                pl.BlockSpec(gain.shape, whole, pipeline_mode=once),
                pl.BlockSpec(grad_gain2.shape, whole, pipeline_mode=once),
                pl.BlockSpec(diagonals.shape, whole, pipeline_mode=once),
                pl.BlockSpec(onehot.shape, whole, pipeline_mode=once),
            ],
            out_specs=[piece_spec, piece_spec],
            scratch_shapes=[pltpu.VMEM((model, LANES), F32)],
        ),
        compiler_params=pltpu.CompilerParams(
            dimension_semantics=("arbitrary",), vmem_limit_bytes=40 << 20
        ),
        cost_estimate=pl.CostEstimate(
            flops=tokens * model,
            transcendentals=0,
            bytes_accessed=tokens,
        ),
        name="weight_gradients",
    )(
        core,
        n1,
        grad_qkv,
        grad_out_w,
        part_a,
        part_b,
        gain,
        grad_gain2,
        diagonals,
        onehot,
    )


def body(
    hidden_in,
    segment_ids,
    bucket_of,
    attn_gain,
    w_query,
    w_key,
    w_value,
    w_attn_out,
    bias_table,
    ffn_gain,
    w_gate,
    w_up,
    w_down,
    cotangent,
):
    micro, local_rows, half, width = hidden_in.shape
    rows = micro * local_rows
    seq = segment_ids.shape[2]
    shard = attn_gain.shape[0]
    dp_count = lax.axis_size("dp")
    tp_index = lax.axis_index("tp")
    left_side = tp_index == 0
    local_heads = bias_table.shape[1]
    buckets = bias_table.shape[0]
    head_cols = w_query.shape[1]
    hidden_cols = w_gate.shape[1]
    own_blocks = half // BLOCK
    length = half + BLOCK

    def halo_of(own):
        send = jnp.where(left_side, own[:, half - BLOCK :], own[:, :BLOCK])
        return swap(send, "tp", 0)

    gains = jnp.pad(jnp.stack([attn_gain, ffn_gain], axis=1), ((0, 0), (0, LANES - 2)))
    first_shard = jnp.concatenate([w_query, w_key, w_value, gains], axis=1)
    second_shard = jnp.concatenate([w_gate, w_up, w_down.T, w_attn_out.T], axis=1)
    cut = first_shard.shape[1] // (2 * LANES) * LANES
    second = lax.all_gather(second_shard, ("tp", "dp"), axis=0, tiled=True)
    x_own = hidden_in.reshape(rows, half, width)
    x_halo = halo_of(x_own)
    seg = segment_ids.reshape(rows, seq)
    seg_ext = lax.dynamic_slice_in_dim(seg, tp_index * (half - BLOCK), length, 1)
    seg_pad = jnp.pad(seg_ext, ((0, 0), (BLOCK, BLOCK)), constant_values=-1)
    seg_rows = jnp.broadcast_to(seg_pad[:, :, None], seg_pad.shape + (LANES,))
    seg_lanes = seg_pad.reshape(rows, length // BLOCK + 2, BLOCK)
    other_table = swap(bias_table, "tp", 0)
    table = jnp.where(
        left_side,
        jnp.concatenate([bias_table, other_table], axis=1),
        jnp.concatenate([other_table, bias_table], axis=1),
    )
    near = bucket_of[seq - 2 * BLOCK - 1 : seq + 2 * BLOCK - 1][::-1]
    onehot = (near[None, :] == jnp.arange(buckets, dtype=jnp.int32)[:, None]).astype(F32)
    per_offset = lax.dot_general(
        table, onehot, (((0,), (0,)), ((), ())), precision=HIGHEST_PREC, preferred_element_type=F32
    )
    bias = window_bias(per_offset)
    shift = tp_index.astype(jnp.int32)[None]
    core = (lax.axis_index("dp") & 1).astype(jnp.int32)[None]

    near_halves, (bias, x_halo) = gather_halves(first_shard, cut, (bias, x_halo))
    far_halves = [swap(value, *stage_groups()[2]) for value in near_halves]
    gain_at = near_halves[1].shape[-1] // 2 - LANES
    gain_rows = [h[1][..., gain_at : gain_at + 2] for h in (near_halves, far_halves)]
    own_first = core[0] == 0
    gain_rows = jnp.stack(
        [
            jnp.where(own_first, gain_rows[0], gain_rows[1]),
            jnp.where(own_first, gain_rows[1], gain_rows[0]),
        ],
        axis=1,
    )
    both_gains = gain_rows.reshape(width, 2).T.astype(F32)
    gain1, gain2 = both_gains[:1], both_gains[1:]

    heads_out, qkv, n1, part_a, part_b = attend_forward(
        jnp.concatenate([shift, core]),
        x_own,
        x_halo,
        gain1,
        near_halves,
        far_halves,
        seg_rows,
        seg_lanes,
        bias,
    )
    heads_flat = heads_out.reshape(rows * half, 2 * head_cols)

    cot_flat = cotangent.reshape(rows * half, width)
    block_out, grad_middle, grad_attn, grad_gain2, keep, send, out_weight = feed_forward(
        core,
        heads_flat,
        x_own.reshape(rows * half, width),
        gain2,
        cot_flat,
        second,
        hidden_cols,
        shard,
    )
    grad_attn_rows = grad_attn.reshape(rows, half, width)
    grad_halo = halo_of(grad_attn_rows)
    grad_out_w = dot_tn(grad_attn, heads_flat).astype(BF)
    grad_heads = dot_nn(grad_attn, out_weight).astype(BF).reshape(heads_out.shape)

    far, near, cores = stage_groups()
    far_groups = [far[max(i - 2, 0) : i] for i in range(len(far), 0, -2)]
    stages = [("tp", 0)] + dp_stages()[:-1]
    twice = len(near[0]) > 1

    def both_cores(keep, send, cuts):
        terms = [
            value.reshape((2,) * len(stages) + value.shape[2:])
            for value in (keep, swap_with(send, (cores,)))
        ]
        ends = cuts[1:] + [keep.shape[-1]]
        return [Scatter([Term(t, stages, c, e - c) for t in terms]) for c, e in zip(cuts, ends)]

    feed = both_cores(keep, send, [0])
    others, (grad_heads, grad_halo, grad_out_w) = start_sends(
        feed, [near[0]], (grad_heads, grad_halo, grad_out_w)
    )

    grad_qkv, diagonals = attend_backward(
        shift, qkv, grad_heads, grad_halo, out_weight, seg_rows, seg_lanes, bias
    )
    grad_qkv = grad_qkv.reshape(rows * half, grad_qkv.shape[-1])
    grad_qkv = pltpu.with_memory_space_constraint(grad_qkv, pltpu.HBM)
    keep_w, send_w = weight_gradients(
        core,
        n1,
        grad_qkv,
        grad_out_w,
        part_a,
        part_b,
        gain1,
        grad_gain2,
        diagonals[:, 0],
        onehot,
        shard,
    )
    keep_w, send_w = end_sends(feed, others, (keep_w, send_w))
    tail = both_cores(keep_w, send_w, [0, 2 * head_cols])
    waiting = []
    for group in far_groups:
        end_joint(feed, waiting)
        waiting, (tail[0].terms[0].array,) = start_joint(
            feed, group, (tail[0].terms[0].array,)
        )
    others, (grad_qkv,) = start_sends(tail, [order[:1] for order in near], (grad_qkv,))
    grad_in = input_gradient(
        grad_qkv, part_a, part_b, x_own.reshape(rows * half, width), gain1, grad_middle
    )
    (grad_in,) = end_sends(tail, others, (grad_in,))
    if twice:
        others, _ = start_sends(tail, [order[1:] for order in near])
        flat, (last,) = tie(list(waiting) + others[0], others[1])
        waiting, others = flat[: len(waiting)], [flat[len(waiting) :], [last]]
        end_sends(tail, others)
    end_joint(feed, waiting)
    feed_sums = jnp.concatenate([s.total() for s in feed], axis=-1)
    for group in far_groups:
        others, _ = start_joint(tail, group)
        end_joint(tail, others)
    sums_a, sums_b = [s.total() for s in tail]

    small = sums_b[:, 2 * head_cols :]
    small = jnp.concatenate(
        [small[:, at : at + LANES] for at in range(0, small.shape[1], LANES)], axis=0
    )
    lines = width // LANES
    dp_start = lax.axis_index("dp") * shard
    sum_gain1 = lax.dynamic_slice_in_dim(small[:lines].reshape(-1), dp_start, shard)
    sum_gain2 = lax.dynamic_slice_in_dim(small[lines : 2 * lines].reshape(-1), dp_start, shard)
    sum_table = small[2 * lines : 2 * lines + 2 * local_heads, :buckets]
    sum_table = lax.dynamic_slice_in_dim(sum_table, tp_index * local_heads, local_heads, 0).T

    shape = (micro, local_rows, half, width)
    return (
        block_out.reshape(shape),
        grad_in.reshape(shape),
        sum_gain1,
        sums_a[:, :head_cols],
        sums_a[:, head_cols:],
        sums_b[:, :head_cols],
        sums_b[:, head_cols : 2 * head_cols].T,
        sum_table,
        sum_gain2,
        feed_sums[0],
        feed_sums[1],
        feed_sums[2].T,
    )


def solution(mesh):
    in_specs = (
        P(None, "dp", "tp", None),
        P(None, "dp", None),
        P(),
        P("dp"),
        P("dp", "tp"),
        P("dp", "tp"),
        P("dp", "tp"),
        P("tp", "dp"),
        P(None, "tp"),
        P("dp"),
        P("dp", "tp"),
        P("dp", "tp"),
        P("tp", "dp"),
        P(None, "dp", "tp", None),
    )
    out_specs = (
        P(None, "dp", "tp", None),
        P(None, "dp", "tp", None),
        P("dp"),
        P("dp", "tp"),
        P("dp", "tp"),
        P("dp", "tp"),
        P("tp", "dp"),
        P(None, "tp"),
        P("dp"),
        P("dp", "tp"),
        P("dp", "tp"),
        P("tp", "dp"),
    )
    return jax.shard_map(body, mesh=mesh, in_specs=in_specs, out_specs=out_specs, check_vma=False)
```

```python
import functools

import jax
import jax.numpy as jnp
from jax import lax
from jax.experimental import pallas as pl
from jax.experimental.pallas import tpu as pltpu
from jax.sharding import PartitionSpec as P

EPSILON = 1e-06
MASKED = -1000000000.0
HIGHEST_PREC = lax.Precision.HIGHEST
BLOCK = 128
LANES = 128
FEED_CHUNK = 512
EDGE_CHUNK = 256
BF = jnp.bfloat16
F32 = jnp.float32


def log2_of(count):
    return count.bit_length() - 1


def swap(value, axis, bit):
    count = lax.axis_size(axis)
    return lax.ppermute(value, axis, [(i, i ^ (1 << bit)) for i in range(count)])


def swap_flat(value, axis, bit):
    return swap(value.reshape(-1, value.shape[-1]), axis, bit).reshape(value.shape)


def own_bit(axis, bit):
    return (lax.axis_index(axis) >> bit) & 1


def dp_stages():
    return [("dp", b) for b in range(log2_of(lax.axis_size("dp")) - 1, -1, -1)]


def stage_groups():
    stages = dp_stages()
    near = stages[-2:-1]
    return stages[:-2], (near + [("tp", 0)], [("tp", 0)] + near), stages[-1]


def merge(buf, have, stage):
    axis, bit = stage
    other = swap(buf, axis, bit)
    first = own_bit(axis, bit) == 0
    low, high = jnp.where(first, buf, other), jnp.where(first, other, buf)
    if axis == "tp":
        return jnp.concatenate([low, high], axis=-1), have
    where = sum(1 for s in have if s[1] > bit)
    return jnp.stack([low, high], axis=where), have + [stage]


def tie(values, others):
    both = lax.optimization_barrier((tuple(values), tuple(others)))
    return both[0], both[1]


def gather_halves(piece, cut, before_last):
    far, orders, _ = stage_groups()
    have = []
    bias, halo = before_last
    for index, stage in enumerate(far):
        if index == len(far) - 1:
            (piece,), (halo,) = tie([piece], [halo])
        piece, have = merge(piece, have, stage)
    (piece,), (bias,) = tie([piece], [bias])
    before_last = (bias, halo)
    halves = [(piece[..., :cut], have), (piece[..., cut:], have)]
    for step in range(len(orders[0])):
        done = merge(*halves[0], orders[0][step])
        if step == 0:
            (value,), (first,) = tie([halves[1][0]], [done[0]])
            halves[1], done = (value, halves[1][1]), (first, done[1])
        halves = [done, merge(*halves[1], orders[1][step])]
    shape = (-1, piece.shape[-2])
    return [h[0].reshape(shape + h[0].shape[-1:]) for h in halves], before_last


def flips(group):
    chosen = [()]
    for stage in reversed(group):
        chosen += [c + (stage,) for c in chosen]
    return chosen[1:]


def swap_with(value, flip):
    flat = value.reshape(-1, value.shape[-1])
    across = sum(1 << bit for axis, bit in flip if axis == "tp")
    along = sum(1 << bit for axis, bit in flip if axis == "dp")
    if not across:
        axes, pairs = "dp", [(i, i ^ along) for i in range(lax.axis_size("dp"))]
    elif not along:
        axes, pairs = "tp", [(i, i ^ across) for i in range(lax.axis_size("tp"))]
    else:
        count = lax.axis_size("tp")
        axes = ("dp", "tp")
        pairs = [
            (i * count + j, (i ^ along) * count + (j ^ across))
            for i in range(lax.axis_size("dp"))
            for j in range(count)
        ]
    return lax.ppermute(flat, axes, pairs).reshape(value.shape)


class Term:
    def __init__(self, array, stages, first=0, count=None):
        self.array, self.stages, self.first = array, list(stages), first
        self.count = array.shape[-1] if count is None else count

    def part(self, fixed, flip):
        starts, sizes, kept = [], [], []
        for stage in self.stages:
            if stage in fixed:
                starts.append(1 - own_bit(*stage) if stage in flip else own_bit(*stage))
                sizes.append(1)
            else:
                starts.append(0)
                sizes.append(2)
                kept.append(2)
        rest = self.array.shape[len(self.stages) : -1]
        starts += [0] * len(rest) + [self.first]
        sizes += list(rest) + [self.count]
        part = lax.dynamic_slice(self.array, starts, sizes)
        return part.reshape(tuple(kept) + rest + (self.count,))


class Scatter:
    def __init__(self, terms):
        self.terms, self.done = terms, []
        self.stages = list(terms[0].stages)

    def sends(self, group):
        self.done = self.done + list(group)
        self.stages = [s for s in self.stages if s not in group]
        return [
            sum(t.part(self.done, flip).astype(F32) for t in self.terms).astype(BF)
            for flip in flips(group)
        ]

    def add(self, array, first=0, count=None):
        self.terms.append(Term(array, self.stages, first, count))

    def total(self):
        return sum(t.part(self.done, ()).astype(F32) for t in self.terms)


def start_sends(scatters, groups, later=()):
    sends = [s.sends(group) for s, group in zip(scatters, groups)]
    count = len(sends[0])
    if later:
        flat, later = tie([x for part in sends for x in part], later)
        sends = [flat[i * count : (i + 1) * count] for i in range(len(scatters))]
    others = [
        [swap_with(x, flip) for x, flip in zip(part, flips(group))]
        for part, group in zip(sends, groups)
    ]
    return others, later


def end_sends(scatters, others, later=()):
    count = len(others[0])
    flat = [x for part in others for x in part]
    if later:
        flat, later = tie(flat, later)
    for index, scatter in enumerate(scatters):
        for other in flat[index * count : (index + 1) * count]:
            scatter.add(other)
    return later


def start_joint(scatters, group, later=()):
    sends = [jnp.concatenate(parts, axis=-1) for parts in zip(*[s.sends(group) for s in scatters])]
    if later:
        sends, later = tie(sends, later)
    return [swap_with(x, flip) for x, flip in zip(sends, flips(group))], later


def end_joint(scatters, others, later=()):
    if later:
        others, later = tie(others, later)
    for other in others:
        at = 0
        for scatter in scatters:
            count = scatter.terms[0].count
            scatter.add(other, at, count)
            at += count
    return later


def inverse_rms(values):
    return lax.rsqrt(jnp.mean(values * values, axis=-1, keepdims=True) + EPSILON)


def key_blocks(block, last):
    return jnp.maximum(block - 1, 0), block, jnp.minimum(block + 1, last)


def block_mask(seg_rows_ref, seg_lanes_ref, block):
    seg_k = seg_rows_ref[0, pl.ds(pl.multiple_of(block * BLOCK, BLOCK), 3 * BLOCK), :]
    seg_q = seg_lanes_ref[0, pl.ds(block + 1, 1), :]
    mask = jnp.where(seg_k == seg_q, 0.0, MASKED)
    return jnp.concatenate([mask, mask], axis=1)


def place_of(block):
    return pl.ds(pl.multiple_of(block * BLOCK, BLOCK), BLOCK)


def lanes_of(column):
    return pl.ds(pl.multiple_of(column, LANES), LANES)


def window_of(ref, blocks, column):
    return jnp.concatenate([ref[0, place_of(b), lanes_of(column)] for b in blocks], axis=0)


def stack_heads(value):
    first = lax.broadcasted_iota(jnp.int32, value.shape, 1) < LANES // 2
    zero = jnp.zeros_like(value)
    return jnp.concatenate([jnp.where(first, value, zero), jnp.where(first, zero, value)], axis=0)


def unstack_heads(value):
    first = lax.broadcasted_iota(jnp.int32, (LANES, BLOCK), 0) < LANES // 2
    return jnp.where(first, value[:, :BLOCK], value[:, BLOCK:]).T


def dot_nt(left, right):
    return lax.dot_general(left, right, (((1,), (1,)), ((), ())), preferred_element_type=F32)


def dot_nn(left, right):
    return lax.dot_general(left, right, (((1,), (0,)), ((), ())), preferred_element_type=F32)


def dot_tn(left, right):
    return lax.dot_general(left, right, (((0,), (0,)), ((), ())), preferred_element_type=F32)


def pair_columns(pair, half_pairs):
    half, local = divmod(pair, half_pairs)
    width = half_pairs * LANES
    base = half * 3 * width + local * LANES
    return base, base + width, base + 2 * width


def softmax_of(logits):
    top = jnp.max(logits, axis=0, keepdims=True)
    powers = jnp.exp(logits - top)
    return powers * (1.0 / jnp.sum(powers, axis=0, keepdims=True))


def column_pieces(part_a, part_b):
    wide_a, wide_b = part_a.shape[1] // 2, part_b.shape[1] // 2
    at, pieces = 0, []
    for half in range(2):
        for ref, wide, used in ((part_a, wide_a, wide_a), (part_b, wide_b, wide_b - LANES)):
            pieces.append((ref, half * wide, at, used))
            at += used
    return pieces


def attend_kernel(
    pairs,
    last,
    shift_ref,
    x_ref,
    halo_ref,
    gain_ref,
    a_own_ref,
    a_other_ref,
    b_own_ref,
    b_other_ref,
    segr_ref,
    segl_ref,
    bias_ref,
    out_ref,
    qkv_ref,
    n1_ref,
    wa_ref,
    wb_ref,
    n1_s,
):
    own_blocks = pl.num_programs(1)
    shift = shift_ref[0]
    length = n1_s.shape[0]

    @pl.when(jnp.logical_and(pl.program_id(0) == 0, pl.program_id(1) == 0))
    def _():
        groups, shard = a_own_ref.shape[:2]
        for whole, own, other in (
            (wa_ref, a_own_ref, a_other_ref),
            (wb_ref, b_own_ref, b_other_ref),
        ):
            for core in range(2):

                @pl.when(shift_ref[1] == core)
                def _():
                    for group in range(groups):
                        for side, ref in ((core, own), (1 - core, other)):
                            start = (2 * group + side) * shard
                            whole[start : start + shard, :] = ref[group]

    @pl.when(pl.program_id(1) == 0)
    def _():
        def normed(value):
            value = value.astype(F32)
            return (value * inverse_rms(value) * gain_ref[...]).astype(BF)

        def own(index, carry):
            value = normed(x_ref[0, place_of(index), :])
            n1_ref[0, :, place_of(index)] = value.T
            n1_s[place_of(index + shift), :] = value
            return carry

        lax.fori_loop(0, own_blocks, own, 0)
        n1_s[place_of((1 - shift) * own_blocks), :] = normed(halo_ref[0])
        chunk = length // 2

        def project(index, carry):
            place = pl.ds(pl.multiple_of(index * chunk, chunk), chunk)
            for ref, start, at, used in column_pieces(wa_ref, wb_ref):
                part = dot_nn(n1_s[place, :], ref[:, start : start + used])
                qkv_ref[0, place, at : at + used] = part.astype(BF)
            return carry

        lax.fori_loop(0, 2, project, 0)

    block = pl.program_id(1) + shift
    blocks = key_blocks(block, last)
    mask = block_mask(segr_ref, segl_ref, block)
    columns = [pair_columns(pair, pairs // 2) for pair in range(pairs)]
    logits = [
        dot_nt(
            window_of(qkv_ref, blocks, col_k),
            stack_heads(qkv_ref[0, place_of(block), col_q : col_q + LANES]),
        )
        for col_q, col_k, _ in columns
    ]
    weights = [
        softmax_of(value + (bias_ref[pair] + mask)).astype(BF) for pair, value in enumerate(logits)
    ]
    mixed = [
        dot_tn(window_of(qkv_ref, blocks, col_v), value)
        for (_, _, col_v), value in zip(columns, weights)
    ]
    for pair, value in enumerate(mixed):
        out_ref[0, :, pair * LANES : (pair + 1) * LANES] = unstack_heads(value).astype(BF)


def attend_forward(place, x_own, x_halo, gain, halves, others, seg_rows, seg_lanes, bias):
    rows, half, model = x_own.shape
    own_blocks = half // BLOCK
    length = half + BLOCK
    pairs = bias.shape[0]
    last = length // BLOCK - 1
    widths = [h.shape[-1] for h in halves]
    width = sum(widths) - 2 * LANES
    steps = rows * own_blocks * pairs
    once = pl.Buffered(1)
    cost = pl.CostEstimate(
        flops=steps * 8 * BLOCK * 3 * BLOCK * LANES + 2 * rows * length * model * width,
        transcendentals=steps * 6 * BLOCK * BLOCK,
        bytes_accessed=rows * length * (width + 2 * model) * 2 + bias.size * 4 + model * width * 2,
    )
    return pl.pallas_call(
        functools.partial(attend_kernel, pairs, last),
        out_shape=(
            jax.ShapeDtypeStruct((rows, half, pairs * LANES), BF),
            jax.ShapeDtypeStruct((rows, length, width), BF),
            jax.ShapeDtypeStruct((rows, model, half), BF),
            jax.ShapeDtypeStruct((model, widths[0]), BF),
            jax.ShapeDtypeStruct((model, widths[1]), BF),
        ),
        grid_spec=pltpu.PrefetchScalarGridSpec(
            num_scalar_prefetch=1,
            grid=(rows, own_blocks),
            in_specs=[
                pl.BlockSpec((1, half, model), lambda r, i, s: (r, 0, 0)),
                pl.BlockSpec((1, BLOCK, model), lambda r, i, s: (r, 0, 0)),
                pl.BlockSpec((1, model), lambda r, i, s: (0, 0), pipeline_mode=once),
                pl.BlockSpec(halves[0].shape, lambda r, i, s: (0, 0, 0), pipeline_mode=once),
                pl.BlockSpec(others[0].shape, lambda r, i, s: (0, 0, 0), pipeline_mode=once),
                pl.BlockSpec(halves[1].shape, lambda r, i, s: (0, 0, 0), pipeline_mode=once),
                pl.BlockSpec(others[1].shape, lambda r, i, s: (0, 0, 0), pipeline_mode=once),
                pl.BlockSpec((1,) + seg_rows.shape[1:], lambda r, i, s: (r, 0, 0)),
                pl.BlockSpec((1,) + seg_lanes.shape[1:], lambda r, i, s: (r, 0, 0)),
                pl.BlockSpec(bias.shape, lambda r, i, s: (0, 0, 0), pipeline_mode=once),
            ],
            out_specs=[
                pl.BlockSpec((1, BLOCK, pairs * LANES), lambda r, i, s: (r, i, 0)),
                pl.BlockSpec((1, length, width), lambda r, i, s: (r, 0, 0)),
                pl.BlockSpec((1, model, half), lambda r, i, s: (r, 0, 0)),
                pl.BlockSpec((model, widths[0]), lambda r, i, s: (0, 0), pipeline_mode=once),
                pl.BlockSpec((model, widths[1]), lambda r, i, s: (0, 0), pipeline_mode=once),
            ],
            scratch_shapes=[pltpu.VMEM((length, model), BF)],
        ),
        compiler_params=pltpu.CompilerParams(
            dimension_semantics=("arbitrary", "arbitrary"), vmem_limit_bytes=48 << 20
        ),
        cost_estimate=cost,
        name="attend_forward",
    )(
        place,
        x_own,
        x_halo,
        gain,
        halves[0],
        others[0],
        halves[1],
        others[1],
        seg_rows,
        seg_lanes,
        bias,
    )


def fold_diagonals(block_sum):
    third = [block_sum[step * BLOCK : (step + 1) * BLOCK] for step in range(3)]
    cur = jnp.concatenate([third[2], third[1], third[0], jnp.zeros((BLOCK, BLOCK), F32)], axis=1)
    count = BLOCK // 2
    while count >= 1:
        cur = cur[count:] + pltpu.roll(cur[:count], count, 1)
        count //= 2
    return cur


def attend_back_kernel(
    pairs,
    last,
    own_blocks,
    shift_ref,
    qkv_ref,
    grad_ref,
    halo_ref,
    wo_ref,
    segr_ref,
    segl_ref,
    bias_ref,
    out_ref,
    diag_ref,
    heads_s,
    acc_ref,
    sum_ref,
):
    row, block = pl.program_id(0), pl.program_id(1)
    shift = shift_ref[0]
    blocks = key_blocks(block, last)
    mask = block_mask(segr_ref, segl_ref, block)
    owned = jnp.logical_and(block >= shift, block < shift + own_blocks)
    keep = jnp.where(owned, 1.0, 0.0)

    @pl.when(block == 0)
    def _():
        acc_ref[...] = jnp.zeros_like(acc_ref)
        own = pl.ds(pl.multiple_of(shift * BLOCK, BLOCK), own_blocks * BLOCK)
        heads_s[own, :] = grad_ref[0]
        other = place_of((1 - shift) * own_blocks)
        heads_s[other, :] = dot_nn(halo_ref[0], wo_ref[...]).astype(BF)

    @pl.when(jnp.logical_and(block == 0, row == 0))
    def _():
        sum_ref[...] = jnp.zeros_like(sum_ref)

    columns = [pair_columns(pair, pairs // 2) for pair in range(pairs)]
    here = place_of(block)
    queries = [stack_heads(qkv_ref[0, here, c[0] : c[0] + LANES]) for c in columns]
    grads = [stack_heads(heads_s[here, p * LANES : (p + 1) * LANES]) for p in range(pairs)]
    keys = [window_of(qkv_ref, blocks, c[1]) for c in columns]
    logits = [dot_nt(k, q) for k, q in zip(keys, queries)]
    grads_w = [dot_nt(window_of(qkv_ref, blocks, c[2]), g) for c, g in zip(columns, grads)]
    probs = [softmax_of(value + (bias_ref[p] + mask)) for p, value in enumerate(logits)]
    grads_v = [dot_nn(p.astype(BF), g) for p, g in zip(probs, grads)]
    grads_l = [
        (p * (g - jnp.sum(p * g, axis=0, keepdims=True))).astype(BF)
        for p, g in zip(probs, grads_w)
    ]
    grads_k = [dot_nn(g, q) for g, q in zip(grads_l, queries)]
    grads_q = [dot_tn(k, g) for k, g in zip(keys, grads_l)]
    for pair, (col_q, col_k, col_v) in enumerate(columns):
        sum_ref[pair] += grads_l[pair].astype(F32) * keep
        acc_ref[here, col_q : col_q + LANES] = unstack_heads(grads_q[pair])
        for part in range(3):
            piece = slice(part * BLOCK, (part + 1) * BLOCK)
            acc_ref[place_of(blocks[part]), col_k : col_k + LANES] += grads_k[pair][piece]
            acc_ref[place_of(blocks[part]), col_v : col_v + LANES] += grads_v[pair][piece]

    @pl.when(block == last)
    def _():
        start = pl.multiple_of(shift * BLOCK, BLOCK)
        out_ref[0] = acc_ref[pl.ds(start, own_blocks * BLOCK), :].astype(BF)

    @pl.when(jnp.logical_and(block == last, row == pl.num_programs(0) - 1))
    def _():
        def fold(pair, carry):
            diag_ref[2 * pair] = fold_diagonals(sum_ref[pair, :, :BLOCK])
            diag_ref[2 * pair + 1] = fold_diagonals(sum_ref[pair, :, BLOCK:])
            return carry

        lax.fori_loop(0, pairs, fold, 0)


def attend_backward(
    shift, qkv, grad_heads, grad_halo, out_weight, seg_rows, seg_lanes, bias
):
    rows, length, width = qkv.shape
    half, cols = grad_heads.shape[1:]
    model = grad_halo.shape[2]
    own_blocks = half // BLOCK
    pairs = bias.shape[0]
    last = length // BLOCK - 1
    steps = rows * (last + 1) * pairs
    once = pl.Buffered(1)
    cost = pl.CostEstimate(
        flops=steps * 120 * BLOCK * 3 * BLOCK * LANES + 2 * rows * BLOCK * model * cols,
        transcendentals=steps * 6 * BLOCK * BLOCK,
        bytes_accessed=qkv.size * 4 + grad_heads.size * 2 + bias.size * 4 + model * cols * 2,
    )
    return pl.pallas_call(
        functools.partial(attend_back_kernel, pairs, last, own_blocks),
        out_shape=(
            pltpu.HBM((rows, half, width), BF),
            jax.ShapeDtypeStruct((2 * pairs, 1, 4 * BLOCK), F32),
        ),
        grid_spec=pltpu.PrefetchScalarGridSpec(
            num_scalar_prefetch=1,
            grid=(rows, last + 1),
            in_specs=[
                pl.BlockSpec((1, length, width), lambda r, i, s: (r, 0, 0)),
                pl.BlockSpec((1, half, cols), lambda r, i, s: (r, 0, 0)),
                pl.BlockSpec((1, BLOCK, model), lambda r, i, s: (r, 0, 0)),
                pl.BlockSpec((model, cols), lambda r, i, s: (0, 0), pipeline_mode=once),
                pl.BlockSpec((1,) + seg_rows.shape[1:], lambda r, i, s: (r, 0, 0)),
                pl.BlockSpec((1,) + seg_lanes.shape[1:], lambda r, i, s: (r, 0, 0)),
                pl.BlockSpec(bias.shape, lambda r, i, s: (0, 0, 0), pipeline_mode=once),
            ],
            out_specs=[
                pl.BlockSpec((1, half, width), lambda r, i, s: (r, 0, 0)),
                pl.BlockSpec((2 * pairs, 1, 4 * BLOCK), lambda r, i, s: (0, 0, 0)),
            ],
            scratch_shapes=[
                pltpu.VMEM((length, pairs * LANES), BF),
                pltpu.VMEM((length, width), F32),
                pltpu.VMEM(bias.shape, F32),
            ],
        ),
        compiler_params=pltpu.CompilerParams(
            dimension_semantics=("arbitrary", "arbitrary"), vmem_limit_bytes=38 << 20
        ),
        cost_estimate=cost,
        name="attend_backward",
    )(shift, qkv, grad_heads, grad_halo, out_weight, seg_rows, seg_lanes, bias)


def input_kernel(grad_ref, wa_ref, wb_ref, x_ref, gain_ref, gmid_ref, out_ref):
    grad_n1 = None
    for ref, start, at, used in column_pieces(wa_ref, wb_ref):
        part = dot_nt(grad_ref[:, at : at + used], ref[:, start : start + used])
        grad_n1 = part if grad_n1 is None else grad_n1 + part
    x = x_ref[...].astype(F32)
    r1 = inverse_rms(x)
    scaled = grad_n1 * gain_ref[...]
    inner = jnp.mean(scaled * x, axis=-1, keepdims=True)
    out_ref[...] = gmid_ref[...] + r1 * scaled - x * (r1 * r1 * r1 * inner)


def input_gradient(grad_qkv, part_a, part_b, x_own, gain, grad_middle):
    tokens, width = grad_qkv.shape
    model = x_own.shape[1]
    chunk = min(256, tokens)
    once = pl.Buffered(1)
    here = lambda i: (i, 0)
    whole = lambda i: (0, 0)
    return pl.pallas_call(
        input_kernel,
        out_shape=jax.ShapeDtypeStruct((tokens, model), F32),
        grid=(tokens // chunk,),
        in_specs=[
            pl.BlockSpec((chunk, width), here),
            pl.BlockSpec(part_a.shape, whole, pipeline_mode=once),
            pl.BlockSpec(part_b.shape, whole, pipeline_mode=once),
            pl.BlockSpec((chunk, model), here),
            pl.BlockSpec((1, model), whole, pipeline_mode=once),
            pl.BlockSpec((chunk, model), here),
        ],
        out_specs=pl.BlockSpec((chunk, model), here),
        compiler_params=pltpu.CompilerParams(
            dimension_semantics=("arbitrary",), vmem_limit_bytes=60 << 20
        ),
        cost_estimate=pl.CostEstimate(
            flops=tokens * model, transcendentals=tokens, bytes_accessed=tokens
        ),
        name="input_gradient",
    )(grad_qkv, part_a, part_b, x_own, gain, grad_middle)


def bias_kernel(turned_ref, out_ref):
    for side in range(2):
        wide = jnp.broadcast_to(turned_ref[side], (3 * BLOCK, 4 * BLOCK))
        out = pltpu.roll(wide, BLOCK + 1, 1, stride=1, stride_axis=0)
        out_ref[0, :, side * BLOCK : (side + 1) * BLOCK] = out[:, :BLOCK]


def window_bias(turned):
    pairs = turned.shape[0] // 2
    return pl.pallas_call(
        bias_kernel,
        out_shape=jax.ShapeDtypeStruct((pairs, 3 * BLOCK, 2 * BLOCK), F32),
        grid=(pairs,),
        in_specs=[pl.BlockSpec((2, 1, 4 * BLOCK), lambda h: (h, 0, 0))],
        out_specs=pl.BlockSpec((1, 3 * BLOCK, 2 * BLOCK), lambda h: (h, 0, 0)),
        name="window_bias",
    )(turned[:, None, :])


def gelu_parts(gate):
    c, a = 0.7978845608028654, 0.044715
    square = gate * gate
    tanh = jnp.tanh(gate * (c + (c * a) * square))
    t = 0.5 + 0.5 * tanh
    slope = t + (0.5 * gate) * (1.0 - tanh * tanh) * (c + (3.0 * c * a) * square)
    return gate * t, slope


def split_rows(own_core, shard, grad, keep_ref, send_ref, where):
    for core in range(2):
        first, second = (keep_ref, send_ref) if core == 0 else (send_ref, keep_ref)

        @pl.when(own_core == core)
        def _():
            for group in range(grad.shape[0] // (2 * shard)):
                start = group * 2 * shard
                first[(0, group) + where] = grad[start : start + shard]
                second[(0, group) + where] = grad[start + shard : start + 2 * shard]


def feed_kernel(
    chunk,
    shard,
    core_ref,
    heads_ref,
    x_ref,
    gain_ref,
    cot_ref,
    wo0_ref,
    wo1_ref,
    wg_ref,
    wu_ref,
    wd_ref,
    out_ref,
    gmid_ref,
    gattn_ref,
    ggain_ref,
    keep_ref,
    send_ref,
    wo_ref,
    mid_s,
    n2_s,
    n2t_s,
    cott_s,
    hid_s,
    gg_s,
    gu_s,
):
    tokens, width = x_ref.shape
    step = pl.program_id(0) * pl.num_programs(1) + pl.program_id(1)
    final = pl.num_programs(0) * pl.num_programs(1) - 1
    half = heads_ref.shape[1] // 2

    def for_chunks(work, count):
        def one(index, carry):
            work(pl.ds(pl.multiple_of(index * count, count), count))
            return carry

        lax.fori_loop(0, tokens // count, one, 0)

    edge = min(EDGE_CHUNK, tokens)

    @pl.when(step == 0)
    def _():
        wo_ref[:, :half] = wo0_ref[...]
        wo_ref[:, half:] = wo1_ref[...]

        def work(place):
            middle = x_ref[place, :].astype(F32)
            middle = middle + dot_nt(heads_ref[place, :half], wo0_ref[...])
            middle = middle + dot_nt(heads_ref[place, half:], wo1_ref[...])
            mid_s[place, :] = middle
            out_ref[place, :] = middle
            normed = (middle * inverse_rms(middle) * gain_ref[...]).astype(BF)
            n2_s[place, :] = normed
            n2t_s[:, place] = normed.T
            cott_s[:, place] = cot_ref[place, :].T
            gmid_ref[place, :] = jnp.zeros((edge, width), F32)

        for_chunks(work, edge)

    places = [pl.ds(at, chunk) for at in range(0, tokens, chunk)]
    products = [
        (
            dot_nn(n2_s[place, :], wg_ref[...]),
            dot_nn(n2_s[place, :], wu_ref[...]),
            dot_nn(cot_ref[place, :], wd_ref[...]),
        )
        for place in places
    ]
    lows = []
    for place, (gate, up, grad_hidden) in zip(places, products):
        act, slope = gelu_parts(gate)
        low = (act * up, grad_hidden * up * slope, grad_hidden * act)
        lows.append([value.astype(BF) for value in low])
        for ref, value in zip((hid_s, gg_s, gu_s), lows[-1]):
            ref[place, :] = value
    for place, (hidden, grad_gate, grad_up) in zip(places, lows):
        out_ref[place, :] += dot_nt(hidden, wd_ref[...])
        gmid_ref[place, :] += dot_nt(grad_gate, wg_ref[...]) + dot_nt(grad_up, wu_ref[...])

    def store(kind, grad):
        split_rows(core_ref[0], shard, grad.astype(BF), keep_ref, send_ref, (kind,))

    store(0, dot_nn(n2t_s[...], gg_s[...]))
    store(1, dot_nn(n2t_s[...], gu_s[...]))
    store(2, dot_nn(cott_s[...], hid_s[...]))

    @pl.when(step == final)
    def _():
        ggain_ref[...] = jnp.zeros_like(ggain_ref)

        def work(place):
            middle, grad_n2 = mid_s[place, :], gmid_ref[place, :]
            r2 = inverse_rms(middle)
            ggain_ref[...] += jnp.sum(grad_n2 * middle * r2, axis=0, keepdims=True)
            scaled = grad_n2 * gain_ref[...]
            inner = jnp.mean(scaled * middle, axis=-1, keepdims=True)
            grad = cot_ref[place, :].astype(F32) + r2 * scaled - middle * (r2 * r2 * r2 * inner)
            gmid_ref[place, :] = grad
            gattn_ref[place, :] = grad.astype(BF)

        for_chunks(work, edge)


def feed_forward(core, heads_out, x_own, gain, cotangent, weights, hidden_cols, shard):
    tokens, width = x_own.shape
    wide = min(512, hidden_cols)
    steps = hidden_cols // wide
    out_cols = heads_out.shape[1] // 2
    out_at = 3 * hidden_cols // out_cols
    groups = width // (2 * shard)
    whole = lambda t, j, c: (0, 0)
    once = pl.Buffered(1)
    piece = jax.ShapeDtypeStruct((2, groups, 3, shard, hidden_cols), BF)
    piece_spec = pl.BlockSpec((1, groups, 3, shard, wide), lambda t, j, c: (t, 0, 0, 0, j))
    return pl.pallas_call(
        functools.partial(feed_kernel, min(FEED_CHUNK, tokens), shard),
        out_shape=(
            jax.ShapeDtypeStruct((tokens, width), F32),
            jax.ShapeDtypeStruct((tokens, width), F32),
            jax.ShapeDtypeStruct((tokens, width), BF),
            jax.ShapeDtypeStruct((1, width), F32),
            piece,
            piece,
            jax.ShapeDtypeStruct((width, 2 * out_cols), BF),
        ),
        grid_spec=pltpu.PrefetchScalarGridSpec(
            num_scalar_prefetch=1,
            grid=(2, steps),
            in_specs=[
                pl.BlockSpec((tokens, 2 * out_cols), whole, pipeline_mode=once),
                pl.BlockSpec((tokens, width), whole, pipeline_mode=once),
                pl.BlockSpec((1, width), whole, pipeline_mode=once),
                pl.BlockSpec((tokens, width), whole, pipeline_mode=once),
                pl.BlockSpec((width, out_cols), lambda t, j, c: (0, out_at), pipeline_mode=once),
                pl.BlockSpec((width, out_cols), lambda t, j, c: (1, out_at), pipeline_mode=once),
                pl.BlockSpec((width, wide), lambda t, j, c: (t, j)),
                pl.BlockSpec((width, wide), lambda t, j, c: (t, steps + j)),
                pl.BlockSpec((width, wide), lambda t, j, c: (t, 2 * steps + j)),
            ],
            out_specs=[
                pl.BlockSpec((tokens, width), whole, pipeline_mode=once),
                pl.BlockSpec((tokens, width), whole, pipeline_mode=once),
                pl.BlockSpec((tokens, width), whole, pipeline_mode=once),
                pl.BlockSpec((1, width), whole, pipeline_mode=once),
                piece_spec,
                piece_spec,
                pl.BlockSpec((width, 2 * out_cols), whole, pipeline_mode=once),
            ],
            scratch_shapes=[
                pltpu.VMEM((tokens, width), F32),
                pltpu.VMEM((tokens, width), BF),
                pltpu.VMEM((width, tokens), BF),
                pltpu.VMEM((width, tokens), BF),
                pltpu.VMEM((tokens, wide), BF),
                pltpu.VMEM((tokens, wide), BF),
                pltpu.VMEM((tokens, wide), BF),
            ],
        ),
        compiler_params=pltpu.CompilerParams(
            dimension_semantics=("arbitrary", "arbitrary"), vmem_limit_bytes=53 << 20
        ),
        cost_estimate=pl.CostEstimate(
            flops=2 * tokens * width * (18 * hidden_cols + 2 * out_cols),
            transcendentals=2 * tokens * hidden_cols,
            bytes_accessed=weights.size * 2 + tokens * width * 16 + 12 * width * hidden_cols,
        ),
        name="feed_forward",
    )(core, heads_out, x_own, gain, cotangent, weights, weights, weights, weights, weights)


def split_rows_at(own_core, half, shard, grad, keep_ref, send_ref, columns):
    for core in range(2):
        first, second = (keep_ref, send_ref) if core == 0 else (send_ref, keep_ref)

        @pl.when(own_core == core)
        def _():
            for group in range(grad.shape[0] // (2 * shard)):
                start = group * 2 * shard
                first[half, group, :, columns] = grad[start : start + shard]
                second[half, group, :, columns] = grad[start + shard : start + 2 * shard]


def weight_kernel(
    shard,
    core_ref,
    n1_ref,
    gqkv_ref,
    gout_ref,
    wa_ref,
    wb_ref,
    gain_ref,
    ggain_ref,
    diag_ref,
    onehot_ref,
    keep_ref,
    send_ref,
    gain_s,
):
    rows, model, length = n1_ref.shape
    wide = gqkv_ref.shape[1] // 3
    half = pl.program_id(0)

    @pl.when(half == 0)
    def _():
        gain_s[...] = jnp.zeros_like(gain_s)

    wide_a, wide_b = wa_ref.shape[1] // 2, wb_ref.shape[1] // 2
    for index in range(4):
        columns = slice(index * wide, (index + 1) * wide)
        if index < 3:
            grad = sum(
                dot_nn(n1_ref[row], gqkv_ref[row * length : (row + 1) * length, columns])
                for row in range(rows)
            )
            for at in range(index * wide, (index + 1) * wide, LANES):
                if at < wide_a:
                    weight = wa_ref[:, lanes_of(half * wide_a + at)]
                else:
                    weight = wb_ref[:, lanes_of(half * wide_b + at - wide_a)]
                here = at - index * wide
                gain_s[...] += weight.astype(F32) * grad[:, here : here + LANES]
        else:
            grad = gout_ref[...]
        split_rows_at(core_ref[0], half, shard, grad.astype(BF), keep_ref, send_ref, columns)

    @pl.when(half == 1)
    def _():
        ggain1 = jnp.sum(gain_s[...].T, axis=0, keepdims=True) / gain_ref[...]
        table = lax.dot_general(
            diag_ref[...],
            onehot_ref[...],
            (((1,), (1,)), ((), ())),
            precision=HIGHEST_PREC,
            preferred_element_type=F32,
        )
        rows = []
        for value in (ggain1, ggain_ref[...]):
            rows += [value[:, at : at + LANES] for at in range(0, model, LANES)]
        table = jnp.concatenate(
            [table, jnp.zeros((table.shape[0], LANES - table.shape[1]), F32)], axis=1
        )
        small = jnp.concatenate(rows + [table], axis=0).astype(BF)
        for ref in (keep_ref, send_ref):
            ref[:, :, :, 4 * wide :] = jnp.zeros(ref.shape[:3] + (ref.shape[3] - 4 * wide,), BF)
            for at in range(0, small.shape[0], shard):
                lines = small[at : at + shard]
                place = slice(4 * wide + at // shard * LANES, 4 * wide + (at // shard + 1) * LANES)
                for side in range(2):
                    for group in range(ref.shape[1]):
                        ref[side, group, : lines.shape[0], place] = lines


def weight_gradients(
    core, n1, grad_qkv, grad_out_w, part_a, part_b, gain, grad_gain2, diagonals, onehot, shard
):
    rows, model, length = n1.shape
    tokens = rows * length
    wide = grad_out_w.shape[1] // 2
    groups = model // (2 * shard)
    whole = lambda t, c: (0, 0)
    half = lambda t, c: (0, t)
    once = pl.Buffered(1)
    lines = 2 * model // LANES + diagonals.shape[0]
    piece = pltpu.HBM((2, groups, shard, 4 * wide + pl.cdiv(lines, shard) * LANES), BF)
    piece_spec = pl.BlockSpec(piece.shape, lambda t, c: (0, 0, 0, 0), pipeline_mode=once)
    return pl.pallas_call(
        functools.partial(weight_kernel, shard),
        out_shape=(piece, piece),
        grid_spec=pltpu.PrefetchScalarGridSpec(
            num_scalar_prefetch=1,
            grid=(2,),
            in_specs=[
                pl.BlockSpec(n1.shape, lambda t, c: (0, 0, 0), pipeline_mode=once),
                pl.BlockSpec((tokens, 3 * wide), half),
                pl.BlockSpec((model, wide), half),
                pl.BlockSpec(part_a.shape, whole, pipeline_mode=once),
                pl.BlockSpec(part_b.shape, whole, pipeline_mode=once),
                pl.BlockSpec(gain.shape, whole, pipeline_mode=once),
                pl.BlockSpec(grad_gain2.shape, whole, pipeline_mode=once),
                pl.BlockSpec(diagonals.shape, whole, pipeline_mode=once),
                pl.BlockSpec(onehot.shape, whole, pipeline_mode=once),
            ],
            out_specs=[piece_spec, piece_spec],
            scratch_shapes=[pltpu.VMEM((model, LANES), F32)],
        ),
        compiler_params=pltpu.CompilerParams(
            dimension_semantics=("arbitrary",), vmem_limit_bytes=40 << 20
        ),
        cost_estimate=pl.CostEstimate(
            flops=tokens * model,
            transcendentals=0,
            bytes_accessed=tokens,
        ),
        name="weight_gradients",
    )(
        core,
        n1,
        grad_qkv,
        grad_out_w,
        part_a,
        part_b,
        gain,
        grad_gain2,
        diagonals,
        onehot,
    )


def body(
    hidden_in,
    segment_ids,
    bucket_of,
    attn_gain,
    w_query,
    w_key,
    w_value,
    w_attn_out,
    bias_table,
    ffn_gain,
    w_gate,
    w_up,
    w_down,
    cotangent,
):
    micro, local_rows, half, width = hidden_in.shape
    rows = micro * local_rows
    seq = segment_ids.shape[2]
    shard = attn_gain.shape[0]
    dp_count = lax.axis_size("dp")
    tp_index = lax.axis_index("tp")
    left_side = tp_index == 0
    local_heads = bias_table.shape[1]
    buckets = bias_table.shape[0]
    head_cols = w_query.shape[1]
    hidden_cols = w_gate.shape[1]
    own_blocks = half // BLOCK
    length = half + BLOCK

    def halo_of(own):
        send = jnp.where(left_side, own[:, half - BLOCK :], own[:, :BLOCK])
        return swap(send, "tp", 0)

    gains = jnp.pad(jnp.stack([attn_gain, ffn_gain], axis=1), ((0, 0), (0, LANES - 2)))
    first_shard = jnp.concatenate([w_query, w_key, w_value, gains], axis=1)
    second_shard = jnp.concatenate([w_gate, w_up, w_down.T, w_attn_out.T], axis=1)
    cut = first_shard.shape[1] // (2 * LANES) * LANES
    second = lax.all_gather(second_shard, ("tp", "dp"), axis=0, tiled=True)
    x_own = hidden_in.reshape(rows, half, width)
    x_halo = halo_of(x_own)
    seg = segment_ids.reshape(rows, seq)
    seg_ext = lax.dynamic_slice_in_dim(seg, tp_index * (half - BLOCK), length, 1)
    seg_pad = jnp.pad(seg_ext, ((0, 0), (BLOCK, BLOCK)), constant_values=-1)
    seg_rows = jnp.broadcast_to(seg_pad[:, :, None], seg_pad.shape + (LANES,))
    seg_lanes = seg_pad.reshape(rows, length // BLOCK + 2, BLOCK)
    other_table = swap(bias_table, "tp", 0)
    table = jnp.where(
        left_side,
        jnp.concatenate([bias_table, other_table], axis=1),
        jnp.concatenate([other_table, bias_table], axis=1),
    )
    near = bucket_of[seq - 2 * BLOCK - 1 : seq + 2 * BLOCK - 1][::-1]
    onehot = (near[None, :] == jnp.arange(buckets, dtype=jnp.int32)[:, None]).astype(F32)
    per_offset = lax.dot_general(
        table, onehot, (((0,), (0,)), ((), ())), precision=HIGHEST_PREC, preferred_element_type=F32
    )
    bias = window_bias(per_offset)
    shift = tp_index.astype(jnp.int32)[None]
    core = (lax.axis_index("dp") & 1).astype(jnp.int32)[None]

    near_halves, (bias, x_halo) = gather_halves(first_shard, cut, (bias, x_halo))
    far_halves = [swap(value, *stage_groups()[2]) for value in near_halves]
    gain_at = near_halves[1].shape[-1] // 2 - LANES
    gain_rows = [h[1][..., gain_at : gain_at + 2] for h in (near_halves, far_halves)]
    own_first = core[0] == 0
    gain_rows = jnp.stack(
        [
            jnp.where(own_first, gain_rows[0], gain_rows[1]),
            jnp.where(own_first, gain_rows[1], gain_rows[0]),
        ],
        axis=1,
    )
    both_gains = gain_rows.reshape(width, 2).T.astype(F32)
    gain1, gain2 = both_gains[:1], both_gains[1:]

    heads_out, qkv, n1, part_a, part_b = attend_forward(
        jnp.concatenate([shift, core]),
        x_own,
        x_halo,
        gain1,
        near_halves,
        far_halves,
        seg_rows,
        seg_lanes,
        bias,
    )
    heads_flat = heads_out.reshape(rows * half, 2 * head_cols)

    cot_flat = cotangent.reshape(rows * half, width)
    block_out, grad_middle, grad_attn, grad_gain2, keep, send, out_weight = feed_forward(
        core,
        heads_flat,
        x_own.reshape(rows * half, width),
        gain2,
        cot_flat,
        second,
        hidden_cols,
        shard,
    )
    grad_attn_rows = grad_attn.reshape(rows, half, width)
    grad_halo = halo_of(grad_attn_rows)
    grad_out_w = dot_tn(grad_attn, heads_flat).astype(BF)
    grad_heads = dot_nn(grad_attn, out_weight).astype(BF).reshape(heads_out.shape)

    far, near, cores = stage_groups()
    far_groups = [far[max(i - 2, 0) : i] for i in range(len(far), 0, -2)]
    stages = [("tp", 0)] + dp_stages()[:-1]
    twice = len(near[0]) > 1

    def both_cores(keep, send, cuts):
        terms = [
            value.reshape((2,) * len(stages) + value.shape[2:])
            for value in (keep, swap_with(send, (cores,)))
        ]
        ends = cuts[1:] + [keep.shape[-1]]
        return [Scatter([Term(t, stages, c, e - c) for t in terms]) for c, e in zip(cuts, ends)]

    feed = both_cores(keep, send, [0])
    others, (grad_heads, grad_halo, grad_out_w) = start_sends(
        feed, [near[0]], (grad_heads, grad_halo, grad_out_w)
    )

    grad_qkv, diagonals = attend_backward(
        shift, qkv, grad_heads, grad_halo, out_weight, seg_rows, seg_lanes, bias
    )
    grad_qkv = grad_qkv.reshape(rows * half, grad_qkv.shape[-1])
    grad_qkv = pltpu.with_memory_space_constraint(grad_qkv, pltpu.HBM)
    keep_w, send_w = weight_gradients(
        core,
        n1,
        grad_qkv,
        grad_out_w,
        part_a,
        part_b,
        gain1,
        grad_gain2,
        diagonals[:, 0],
        onehot,
        shard,
    )
    keep_w, send_w = end_sends(feed, others, (keep_w, send_w))
    tail = both_cores(keep_w, send_w, [0, 2 * head_cols])
    waiting = []
    for group in far_groups:
        end_joint(feed, waiting)
        waiting, (tail[0].terms[0].array,) = start_joint(
            feed, group, (tail[0].terms[0].array,)
        )
    others, (grad_qkv,) = start_sends(tail, [order[:1] for order in near], (grad_qkv,))
    grad_in = input_gradient(
        grad_qkv, part_a, part_b, x_own.reshape(rows * half, width), gain1, grad_middle
    )
    (grad_in,) = end_sends(tail, others, (grad_in,))
    if twice:
        others, _ = start_sends(tail, [order[1:] for order in near])
        flat, (last,) = tie(list(waiting) + others[0], others[1])
        waiting, others = flat[: len(waiting)], [flat[len(waiting) :], [last]]
        end_sends(tail, others)
    end_joint(feed, waiting)
    feed_sums = jnp.concatenate([s.total() for s in feed], axis=-1)
    for group in far_groups:
        others, _ = start_joint(tail, group)
        end_joint(tail, others)
    sums_a, sums_b = [s.total() for s in tail]

    small = sums_b[:, 2 * head_cols :]
    small = jnp.concatenate(
        [small[:, at : at + LANES] for at in range(0, small.shape[1], LANES)], axis=0
    )
    lines = width // LANES
    dp_start = lax.axis_index("dp") * shard
    sum_gain1 = lax.dynamic_slice_in_dim(small[:lines].reshape(-1), dp_start, shard)
    sum_gain2 = lax.dynamic_slice_in_dim(small[lines : 2 * lines].reshape(-1), dp_start, shard)
    sum_table = small[2 * lines : 2 * lines + 2 * local_heads, :buckets]
    sum_table = lax.dynamic_slice_in_dim(sum_table, tp_index * local_heads, local_heads, 0).T

    shape = (micro, local_rows, half, width)
    return (
        block_out.reshape(shape),
        grad_in.reshape(shape),
        sum_gain1,
        sums_a[:, :head_cols],
        sums_a[:, head_cols:],
        sums_b[:, :head_cols],
        sums_b[:, head_cols : 2 * head_cols].T,
        sum_table,
        sum_gain2,
        feed_sums[0],
        feed_sums[1],
        feed_sums[2].T,
    )


def solution(mesh):
    in_specs = (
        P(None, "dp", "tp", None),
        P(None, "dp", None),
        P(),
        P("dp"),
        P("dp", "tp"),
        P("dp", "tp"),
        P("dp", "tp"),
        P("tp", "dp"),
        P(None, "tp"),
        P("dp"),
        P("dp", "tp"),
        P("dp", "tp"),
        P("tp", "dp"),
        P(None, "dp", "tp", None),
    )
    out_specs = (
        P(None, "dp", "tp", None),
        P(None, "dp", "tp", None),
        P("dp"),
        P("dp", "tp"),
        P("dp", "tp"),
        P("dp", "tp"),
        P("tp", "dp"),
        P(None, "tp"),
        P("dp"),
        P("dp", "tp"),
        P("dp", "tp"),
        P("tp", "dp"),
    )
    return jax.shard_map(body, mesh=mesh, in_specs=in_specs, out_specs=out_specs, check_vma=False)
```
